32 devices in a mesh: gy: 4 (over y, core), gx: 8 (over z, x).
Axes of the slice: x: 2, y: 2, z: 4, core: 2. Of those that a mesh axis runs over, the one named last changes fastest.
Arguments:
- features: bfloat16 [256, 512, 128], P(('gy', 'gx')), may hold values from -6 to 6
- links: int32 [256, 3], P(('gy', 'gx')), may hold values 0 or 1
- block_slot: int32 [256], P(('gy', 'gx')), may hold values from 0 to 15, as said below
- block_level: int32 [256], P(('gy', 'gx')), may hold values from 0 to 3
- slot_column: int32 [32, 16], P(('gy', 'gx')), may hold values from 0 to 31
- conv_first: bfloat16 [7, 128, 128], replicated, may hold values from -0.1875 to 0.1875
- conv_second: bfloat16 [7, 128, 128], replicated, may hold values from -0.1875 to 0.1875
- height_w: bfloat16 [4, 1024, 256], replicated, may hold values from -0.1875 to 0.1875
- plane_first: bfloat16 [3, 3, 256, 256], replicated, may hold values from -0.125 to 0.125
- plane_second: bfloat16 [3, 3, 256, 256], replicated, may hold values from -0.125 to 0.125
Outputs:
- bev_out: bfloat16 [256, 256, 256], P('gy', 'gx')
The draws below stay inside these ranges and needn't reach their ends.
Inputs may be any that keep to these rules, and one draw needn't show every extreme that they name: No two blocks of one device have both the same block_slot and the same block_level. At most 4 blocks of one device have the same block_slot // 2, and every device has exactly 4 such blocks for some value.
All inputs are finite; a program needn't handle non-finite values. No bound on the sum of `links` on one device may be relied on, other than what follows from the above.
Results may differ from the reference program's by a relative error of at most 0.0065.
Values may be sent and summed in bfloat16 or wider, within the bound.
No kernel may reach another device: no remote copies, remote signals or barrier semaphores. Data moves between devices by JAX's collectives and lax.ppermute only.
A program may use at most 64 MiB of HBM per device.

```python
import jax
import jax.numpy as jnp
from jax import lax

C = 128
BEV_C = 256
EDGE = 8
BLOCK_DEV = 8
STRIDE_Y = 8
LEVELS = 4
CAP = 2
TILE_BR = 8
TILE_BC = 4
BLOCKS = 256
SLOTS = 16
COLS = 32
MAP_R = 256
MAP_C = 256
N_GY = 4
N_GX = 8
DEVICES = 32


def choose_cells(key):
    base = jax.random.fold_in(key, 7103)
    cell_total = SLOTS * LEVELS
    tile_total = SLOTS // CAP

    def one_device(device):
        device_key = jax.random.fold_in(base, device)
        key_home, key_score, key_order, key_shift = jax.random.split(device_key, 4)
        cell = jnp.arange(cell_total, dtype=jnp.int32)
        tile = cell // (CAP * LEVELS)
        level = cell % LEVELS
        tile_ids = jnp.arange(tile_total, dtype=jnp.int32)
        start_level = jax.random.randint(key_shift, (tile_total,), 0, LEVELS)
        start_level = jnp.where((device == 0) & (tile_ids == tile_total - 1), 0, start_level).astype(jnp.int32)
        eligible = (level - start_level[tile]) % LEVELS < 2
        home = jax.random.randint(key_home, (), 0, tile_total)
        middle = (tile >= tile_total // 4) & (tile < tile_total - tile_total // 4)
        score = jax.random.randint(key_score, (cell_total,), 0, 1024) + 768 * middle.astype(jnp.int32)
        forced = (tile == home) & eligible | (device == 0) & (cell == cell_total - LEVELS)
        score = score + 100000 * forced.astype(jnp.int32) - 200000 * (1 - eligible.astype(jnp.int32))
        score = score * cell_total + cell
        unused, picked = lax.top_k(score, BLOCK_DEV)
        order = jax.random.permutation(key_order, BLOCK_DEV)
        return picked[order].astype(jnp.int32)
    return jax.vmap(one_device)(jnp.arange(DEVICES, dtype=jnp.int32)).reshape(-1)


def draw_block_slot(key, part):
    return (choose_cells(key) // LEVELS).astype(jnp.int32)


def draw_block_level(key, part):
    return (choose_cells(key) % LEVELS).astype(jnp.int32)


def plant(values, stream_key, low, largest):
    extent = values.shape
    index_at = [jax.random.randint(jax.random.fold_in(stream_key, axis), (), 0, extent[axis]) for axis in range(len(extent))]
    values = values.at[tuple(index_at)].set(low)
    longest = extent.index(max(extent))
    index_at[longest] = (index_at[longest] + 1) % extent[longest]
    return values.at[tuple(index_at)].set(largest)


def levels(rng, extent, pieces, least, high):
    def one(axis_at, shards_of):
        draws = jax.random.uniform(jax.random.fold_in(jax.random.fold_in(rng, 6), axis_at), (shards_of,), jnp.float32, least / len(pieces), high / len(pieces))
        return jnp.repeat(jnp.exp(draws), extent[axis_at] // shards_of).reshape((-1,) + (1,) * (len(extent) - axis_at - 1))

    factor_of = one(*pieces[0])
    for cut in pieces[1:]:
        factor_of = factor_of * one(*cut)
    return factor_of


def gaussian(own_key, dims, deviation, bound, shards=(), kind=jnp.bfloat16):
    array = deviation * jax.random.normal(own_key, dims, jnp.float32)
    if shards:
        array = array * levels(own_key, dims, shards, -0.22, 0.18)
    return jnp.clip(array, -bound, bound).astype(kind)


def setup_inputs(seed: int = 0) -> dict:
    streams_of = jax.random.split(jax.random.key(seed), 11)
    return {
        "features": gaussian(streams_of[0], (BLOCKS, EDGE**3, C), 1.0, 6.0, ((0, 32),)),
        "links": plant((jax.random.randint(streams_of[1], (BLOCKS, 3), 0, 4) < 3).astype(jnp.int32), jax.random.fold_in(streams_of[1], 1), 0, 1),
        "block_slot": draw_block_slot(jax.random.fold_in(streams_of[10], 71), 0),
        "block_level": draw_block_level(jax.random.fold_in(streams_of[10], 71), 0),
        "slot_column": plant(jax.random.randint(streams_of[4], (DEVICES, SLOTS), 0, COLS), jax.random.fold_in(streams_of[4], 1), 0, COLS - 1).astype(jnp.int32),
        "conv_first": gaussian(streams_of[5], (7, C, C), (7 * C) ** -0.5, 0.1875),
        "conv_second": gaussian(streams_of[6], (7, C, C), (7 * C) ** -0.5, 0.1875),
        "height_w": gaussian(streams_of[7], (LEVELS, EDGE * C, BEV_C), (EDGE * C) ** -0.5, 0.1875),
        "plane_first": gaussian(streams_of[8], (3, 3, BEV_C, BEV_C), (9 * BEV_C) ** -0.5, 0.125),
        "plane_second": gaussian(streams_of[9], (3, 3, BEV_C, BEV_C), (9 * BEV_C) ** -0.5, 0.125),
    }


def block_ghosts(blocks, links):
    block_count = blocks.shape[0]
    strides = (1, STRIDE_Y, BLOCK_DEV)
    ghost_plus = []
    ghost_minus = []
    for axis_num in range(3):
        upper = lax.index_in_dim(blocks, EDGE - 1, axis_num + 1, keepdims=False)
        lower = lax.index_in_dim(blocks, 0, axis_num + 1, keepdims=False)
        keeping = links[:, axis_num].astype(blocks.dtype)[:, None, None, None]
        upper = upper * keeping
        stride = strides[axis_num]
        padding = jnp.zeros((stride,) + upper.shape[1:], blocks.dtype)
        ghost_plus.append(jnp.concatenate([lower[stride:], padding], 0) * keeping)
        ghost_minus.append(jnp.concatenate([padding, upper[:block_count - stride]], 0))
    return ghost_plus, ghost_minus


def seven_taps(blocks, ghost_plus, ghost_minus, weights):
    channels = blocks.shape[-1]
    result = jnp.dot(blocks.reshape(-1, channels), weights[0], preferred_element_type=jnp.float32)
    for axis_num in range(3):
        axis = axis_num + 1
        upward = jnp.concatenate([lax.slice_in_dim(blocks, 1, EDGE, axis=axis), jnp.expand_dims(ghost_plus[axis_num], axis)], axis)
        downward = jnp.concatenate([jnp.expand_dims(ghost_minus[axis_num], axis), lax.slice_in_dim(blocks, 0, EDGE - 1, axis=axis)], axis)
        result = result + jnp.dot(upward.reshape(-1, channels), weights[1 + 2 * axis_num], preferred_element_type=jnp.float32)
        result = result + jnp.dot(downward.reshape(-1, channels), weights[2 + 2 * axis_num], preferred_element_type=jnp.float32)
    return result.reshape(blocks.shape)


def plane_conv(padded, kernel, rows_out, cols_out):
    result = jnp.zeros((rows_out * cols_out, kernel.shape[3]), jnp.float32)
    for row_off in range(3):
        for col_off in range(3):
            window = padded[row_off:row_off + rows_out, col_off:col_off + cols_out].reshape(rows_out * cols_out, -1)
            result = result + jnp.dot(window, kernel[row_off, col_off], preferred_element_type=jnp.float32)
    return result.reshape(rows_out, cols_out, -1)


def reference(features, links, block_slot, block_level, slot_column, conv_first, conv_second, height_w, plane_first, plane_second):
    blocks = features.reshape(BLOCKS, EDGE, EDGE, EDGE, C)
    ghost_plus, ghost_minus = block_ghosts(blocks, links)
    hidden = jax.nn.relu(seven_taps(blocks, ghost_plus, ghost_minus, conv_first)).astype(jnp.bfloat16)
    ghost_plus, ghost_minus = block_ghosts(hidden, links)
    voxel = jax.nn.relu(blocks.astype(jnp.float32) + seven_taps(hidden, ghost_plus, ghost_minus, conv_second)).astype(jnp.bfloat16)
    grouped = voxel.reshape(DEVICES, BLOCK_DEV, EDGE * EDGE, EDGE * C)
    level_groups = block_level.reshape(DEVICES, BLOCK_DEV)

    def collapse(pair):
        group_rows, group_levels = pair
        chosen = jnp.take(height_w, group_levels, axis=0).astype(jnp.float32)
        return jnp.einsum("bpk,bkn->bpn", group_rows.astype(jnp.float32), chosen)

    lifted = lax.map(collapse, (grouped, level_groups)).reshape(BLOCKS, EDGE * EDGE, BEV_C)
    device_of = (jnp.arange(BLOCKS, dtype=jnp.int32) // BLOCK_DEV).astype(jnp.int32)
    tile_row = device_of // N_GX
    tile_col = block_slot // CAP
    column = slot_column[device_of, block_slot]
    block_row = tile_row * TILE_BR + column // TILE_BC
    block_col = tile_col * TILE_BC + column % TILE_BC
    target = (block_row * (N_GX * TILE_BC) + block_col).astype(jnp.int32)
    summed = jnp.zeros((N_GY * TILE_BR * N_GX * TILE_BC, EDGE * EDGE, BEV_C), jnp.float32).at[target].add(lifted)
    bev = summed.reshape(N_GY * TILE_BR, N_GX * TILE_BC, EDGE, EDGE, BEV_C).transpose(0, 2, 1, 3, 4)
    bev = bev.reshape(MAP_R, MAP_C, BEV_C).astype(jnp.bfloat16)
    padded = jnp.pad(bev, ((1, 1), (1, 1), (0, 0)))
    first = jax.nn.relu(plane_conv(padded, plane_first, MAP_R, MAP_C)).astype(jnp.bfloat16)
    padded = jnp.pad(first, ((1, 1), (1, 1), (0, 0)))
    return (plane_conv(padded, plane_second, MAP_R, MAP_C) + bev.astype(jnp.float32)).astype(jnp.bfloat16)
```

```python
import functools

import jax
import jax.numpy as jnp
from jax import lax
from jax.experimental import pallas as pl
from jax.experimental.pallas import tpu as pltpu
from jax.sharding import PartitionSpec as P

EDGE = 8
FACE = EDGE * EDGE
CELLS = EDGE * FACE
TILE_BR = 8
TILE_BC = 4
ROWS = TILE_BR * EDGE
COLS = TILE_BC * EDGE
HALO = 2
ID_ROWS = 8
LANES = 128
F32 = jnp.float32
BF16 = jnp.bfloat16

VMEM = pl.BlockSpec(memory_space=pltpu.VMEM)
SMEM = pl.BlockSpec(memory_space=pltpu.SMEM)


def shift(block, axis, distance):
    count = lax.axis_size(axis)
    route = [(i, i + distance) for i in range(count) if 0 <= i + distance < count]
    return lax.ppermute(block, axis, route)


def mm(a, b):
    return jnp.dot(a, b, preferred_element_type=F32)


def link_of(links, block, axis):
    return links[block, axis].astype(F32)


def pack_faces(src, links, up, down):
    count = src.shape[0] // CELLS
    faces = count * FACE
    upper_b, lower_b = [], []
    for j in range(count):
        keep = link_of(links, j, 1)
        for a in range(EDGE):
            base = j * CELLS + a * FACE
            upper_b.append(src[base + FACE - EDGE : base + FACE, :] * keep)
            lower_b.append(src[base : base + EDGE, :])
    up[0:faces, :] = jnp.concatenate(upper_b, 0).astype(BF16)
    down[0:faces, :] = jnp.concatenate(lower_b, 0).astype(BF16)
    upper_c = []
    for j in range(count):
        upper_c.append(
            src[pl.ds(j * CELLS + EDGE - 1, FACE, stride=EDGE), :] * link_of(links, j, 2)
        )
    up[faces : 2 * faces, :] = jnp.concatenate(upper_c, 0).astype(BF16)
    down[faces : 2 * faces, :] = src[pl.ds(0, faces, stride=EDGE), :].astype(BF16)
    last = count * CELLS
    up[2 * faces :, :] = (src[last - FACE : last, :] * link_of(links, count - 1, 0)).astype(BF16)
    down[2 * faces :, :] = src[0:FACE, :].astype(BF16)


def pack_kernel(links, x, up, down, wide):
    wide[...] = x[...].astype(F32)
    pack_faces(wide, links, up, down)


def interior(src, links, weights, out, residual):
    count = src.shape[0] // CELLS
    c_at = lax.broadcasted_iota(jnp.int32, (FACE, EDGE, 128), 1)

    def one(j, carry):
        base = pl.multiple_of(j * CELLS, CELLS)
        rows = src[pl.ds(base, CELLS), :]
        after = jnp.minimum(j + 1, count - 1)
        before = jnp.maximum(j - 1, 0)
        keep_after = jnp.where(j + 1 < count, links[j, 0], 0).astype(F32)
        keep_before = jnp.where(j > 0, links[before, 0], 0).astype(F32)
        over = src[pl.ds(pl.multiple_of(after * CELLS, CELLS), FACE), :]
        under = src[pl.ds(pl.multiple_of(before * CELLS + CELLS - FACE, FACE), FACE), :]
        over = (over.astype(F32) * keep_after).astype(BF16)
        under = (under.astype(F32) * keep_before).astype(BF16)
        wide = rows.astype(F32)
        planes = wide.reshape(EDGE, EDGE, EDGE, 128)
        none = jnp.zeros((EDGE, 1, EDGE, 128), F32)
        lines = wide.reshape(FACE, EDGE, 128)
        taps = [
            rows,
            jnp.concatenate([rows[FACE:], over], 0),
            jnp.concatenate([under, rows[:-FACE]], 0),
            jnp.concatenate([planes[:, 1:], none], 1).reshape(CELLS, 128).astype(BF16),
            jnp.concatenate([none, planes[:, :-1]], 1).reshape(CELLS, 128).astype(BF16),
            jnp.where(c_at == EDGE - 1, 0.0, pltpu.roll(lines, EDGE - 1, 1))
            .reshape(CELLS, 128)
            .astype(BF16),
            jnp.where(c_at == 0, 0.0, pltpu.roll(lines, 1, 1)).reshape(CELLS, 128).astype(BF16),
        ]
        total = mm(jnp.concatenate(taps, 1), weights[...])
        if residual is not None:
            total = total + residual[pl.ds(base, CELLS), :].astype(F32)
        out[pl.ds(base, CELLS), :] = total
        return carry

    lax.fori_loop(0, count, one, 0)


def first_interior_kernel(links, x, weights, out):
    interior(x, links, weights, out, None)


def second_interior_kernel(links, hidden, x, weights, out):
    interior(hidden, links, weights, out, x)


def add_ghosts(total, from_below, from_above, links, weights):
    count = total.shape[0] // CELLS
    faces = count * FACE
    ch = total.shape[1]

    def tap(k):
        return weights[k * ch : (k + 1) * ch, :]

    b_plus = mm(from_above[0:faces, :], tap(3))
    b_minus = mm(from_below[0:faces, :], tap(4))
    for j in range(count):
        keep = link_of(links, j, 1)
        for a in range(EDGE):
            base = j * CELLS + a * FACE
            at = j * FACE + a * EDGE
            total[base + FACE - EDGE : base + FACE, :] += b_plus[at : at + EDGE, :] * keep
            total[base : base + EDGE, :] += b_minus[at : at + EDGE, :]
    c_plus = mm(from_above[faces : 2 * faces, :], tap(5))
    c_minus = mm(from_below[faces : 2 * faces, :], tap(6))
    for j in range(count):
        at = slice(j * FACE, (j + 1) * FACE)
        total[pl.ds(j * CELLS + EDGE - 1, FACE, stride=EDGE), :] += c_plus[at, :] * link_of(
            links, j, 2
        )
        total[pl.ds(j * CELLS, FACE, stride=EDGE), :] += c_minus[at, :]
    last = count * CELLS
    total[last - FACE : last, :] += mm(from_above[2 * faces :, :], tap(1)) * link_of(
        links, count - 1, 0
    )
    total[0:FACE, :] += mm(from_below[2 * faces :, :], tap(2))


def hidden_kernel(links, partial, from_below, from_above, weights, hidden, up, down, total):
    total[...] = partial[...]
    add_ghosts(total, from_below, from_above, links, weights)
    total[...] = jnp.maximum(total[...], 0.0)
    hidden[...] = total[...].astype(BF16)
    pack_faces(total, links, up, down)


def lift_kernel(
    links,
    slots,
    block_levels,
    columns,
    partial,
    from_below,
    from_above,
    weights,
    height,
    out,
    total,
    rows_in,
    sums,
):
    count = partial.shape[0] // CELLS
    faces = count * FACE
    ch = partial.shape[1]
    total[...] = partial[...]
    add_ghosts(total, from_below, from_above, links, weights)
    for c in range(EDGE):
        line = total[pl.ds(c, faces, stride=EDGE), :]
        rows_in[:, c * ch : (c + 1) * ch] = jnp.maximum(line, 0.0).astype(BF16)
    sums[...] = jnp.zeros_like(sums)

    def one(j, carry):
        rows = rows_in[pl.ds(pl.multiple_of(j * FACE, FACE), FACE), :]
        sums[slots[0, j]] += mm(rows, height[block_levels[0, j]])
        return carry

    lax.fori_loop(0, count, one, 0)
    peers = out.shape[0]
    per_peer = sums.shape[0] // peers
    row_at = lax.broadcasted_iota(jnp.int32, (ID_ROWS, out.shape[2]), 0)
    for p in range(peers):
        ids = jnp.zeros(row_at.shape, F32)
        for k in range(per_peer):
            slot = p * per_peer + k
            out[p, k * FACE : (k + 1) * FACE, :] = sums[slot].astype(BF16)
            ids = jnp.where(row_at == k, columns[0, slot].astype(F32), ids)
        out[p, per_peer * FACE :, :] = ids.astype(BF16)


def gather_kernel(arrived, bev, top, bottom, left, right, total):
    peers, rows, ch = arrived.shape
    per_peer = (rows - ID_ROWS) // FACE
    total[...] = jnp.zeros_like(total)
    for p in range(peers):
        ids = arrived[p, per_peer * FACE :, :].astype(F32)
        for k in range(per_peer):
            column = jnp.max(ids[k : k + 1, :]).astype(jnp.int32)
            row_base = (column // TILE_BC) * (EDGE * COLS) + (column % TILE_BC) * EDGE
            block = arrived[p, k * FACE : (k + 1) * FACE, :].astype(F32)
            for a in range(EDGE):
                at = pl.multiple_of(row_base + a * COLS, EDGE)
                for h, lanes in halves(ch):
                    total[h, pl.ds(at, EDGE), :] += block[a * EDGE : (a + 1) * EDGE, lanes]
    for h, lanes in halves(ch):
        bev[:, lanes] = total[h].astype(BF16)
        top[:, lanes] = total[h, 0 : HALO * COLS, :].astype(BF16)
        bottom[:, lanes] = total[h, (ROWS - HALO) * COLS :, :].astype(BF16)
        for x in range(HALO):
            far = COLS - HALO + x
            left[x, :, lanes] = total[h, pl.ds(x, ROWS, stride=COLS), :].astype(BF16)
            right[x, :, lanes] = total[h, pl.ds(far, ROWS, stride=COLS), :].astype(BF16)


def halves(channels):
    return [(h, slice(h * LANES, (h + 1) * LANES)) for h in range(channels // LANES)]


PITCH = COLS + 2 * EDGE
WIDE_ROWS = ROWS + 2 * HALO
MID_ROWS = ROWS + HALO
RIM_ROWS = 72


def side_shifts(padded, before, after, count):
    def one(y, carry):
        at = pl.multiple_of(y * PITCH, EDGE)
        to = pl.multiple_of(y * COLS, COLS)
        for h, lanes in halves(before.shape[1]):
            before[pl.ds(to, COLS), lanes] = padded[h, pl.ds(at + EDGE - 1, COLS), :].astype(BF16)
            after[pl.ds(to, COLS), lanes] = padded[h, pl.ds(at + EDGE + 1, COLS), :].astype(BF16)
        return carry

    lax.fori_loop(0, count, one, 0)


def stacked(sources, first_row, row_count):
    parts = []
    for dy in range(3):
        for source in sources:
            at = pl.multiple_of((first_row + dy) * COLS, COLS)
            parts.append(source[pl.ds(at, row_count * COLS), :])
    return jnp.concatenate(parts, 1)


def plane_kernel(
    flags,
    bev,
    above,
    below,
    left,
    right,
    weights_first,
    weights_second,
    out,
    padded,
    before,
    centre,
    after,
    rim,
):
    ch = bev.shape[1]
    centre[0 : HALO * COLS, :] = above[...]
    centre[HALO * COLS : (HALO + ROWS) * COLS, :] = bev[...]
    centre[(HALO + ROWS) * COLS : WIDE_ROWS * COLS, :] = below[...]

    def widen(y, carry):
        at = pl.multiple_of(y * PITCH + EDGE, EDGE)
        row = centre[pl.ds(pl.multiple_of(y * COLS, COLS), COLS), :].astype(F32)
        for h, lanes in halves(ch):
            padded[h, pl.ds(at, COLS), :] = row[:, lanes]
        return carry

    lax.fori_loop(0, WIDE_ROWS, widen, 0)
    rim[...] = jnp.zeros_like(rim)
    for x in range(HALO):
        lefts = left[x, :, :].astype(F32)
        rights = right[x, :, :].astype(F32)
        rim[x, 0:WIDE_ROWS, :] = lefts
        rim[4 + x, 0:WIDE_ROWS, :] = rights
    for h, lanes in halves(ch):
        own_left = padded[h, pl.ds(EDGE, WIDE_ROWS, stride=PITCH), :]
        own_right = padded[h, pl.ds(EDGE + COLS - 1, WIDE_ROWS, stride=PITCH), :]
        rim[2, 0:WIDE_ROWS, lanes] = own_left
        rim[3, 0:WIDE_ROWS, lanes] = own_right
        padded[h, pl.ds(EDGE - 1, WIDE_ROWS, stride=PITCH), :] = rim[1, 0:WIDE_ROWS, lanes]
        padded[h, pl.ds(EDGE + COLS, WIDE_ROWS, stride=PITCH), :] = rim[4, 0:WIDE_ROWS, lanes]
    side_shifts(padded, before, after, WIDE_ROWS)

    rim_first = []
    for sources in ((0, 1, 2), (3, 4, 5)):
        parts = []
        for dy in range(3):
            for s in sources:
                parts.append(rim[s, dy : dy + RIM_ROWS, :].astype(BF16))
        rim_first.append(jnp.concatenate(parts, 1))
    rim_out = mm(jnp.concatenate(rim_first, 0), weights_first[...])
    rim_out = jnp.maximum(rim_out, 0.0)
    row_at = lax.broadcasted_iota(jnp.int32, (RIM_ROWS, ch), 0)
    inside = jnp.where(
        row_at == 0, flags[0], jnp.where(row_at == MID_ROWS - 1, flags[1], 1)
    ).astype(F32)
    rim_left = rim_out[0:RIM_ROWS, :] * inside * flags[2].astype(F32)
    rim_right = rim_out[RIM_ROWS:, :] * inside * flags[3].astype(F32)

    step = MID_ROWS // 6

    def first_rows(i, carry):
        y = i * step
        block = mm(stacked((before, centre, after), y, step), weights_first[...])
        block = jnp.maximum(block, 0.0)
        for r in range(step):
            keep = jnp.where(
                y + r == 0, flags[0], jnp.where(y + r == MID_ROWS - 1, flags[1], 1)
            ).astype(F32)
            at = pl.multiple_of((y + r) * PITCH + EDGE, EDGE)
            row = block[r * COLS : (r + 1) * COLS, :] * keep
            for h, lanes in halves(ch):
                padded[h, pl.ds(at, COLS), :] = row[:, lanes]
        return carry

    lax.fori_loop(0, MID_ROWS // step, first_rows, 0)
    for h, lanes in halves(ch):
        padded[h, pl.ds(EDGE - 1, MID_ROWS, stride=PITCH), :] = rim_left[0:MID_ROWS, lanes]
        padded[h, pl.ds(EDGE + COLS, MID_ROWS, stride=PITCH), :] = rim_right[0:MID_ROWS, lanes]
    side_shifts(padded, before, after, MID_ROWS)

    def narrow(y, carry):
        at = pl.multiple_of(y * PITCH + EDGE, EDGE)
        to = pl.multiple_of(y * COLS, COLS)
        for h, lanes in halves(ch):
            centre[pl.ds(to, COLS), lanes] = padded[h, pl.ds(at, COLS), :].astype(BF16)
        return carry

    lax.fori_loop(0, MID_ROWS, narrow, 0)
    step2 = 16

    def second_rows(i, carry):
        y = i * step2
        block = mm(stacked((before, centre, after), y, step2), weights_second[...])
        at = pl.multiple_of(y * COLS, COLS)
        own = bev[pl.ds(at, step2 * COLS), :].astype(F32)
        out[pl.ds(at, step2 * COLS), :] = (block + own).astype(BF16)
        return carry

    lax.fori_loop(0, ROWS // step2, second_rows, 0)


def call(kernel, name, out_shape, scalars, arrays, scratch=()):
    multiple = isinstance(out_shape, (list, tuple))
    return pl.pallas_call(
        kernel,
        name=name,
        out_shape=out_shape,
        in_specs=[SMEM] * len(scalars) + [VMEM] * len(arrays),
        out_specs=[VMEM] * len(out_shape) if multiple else VMEM,
        scratch_shapes=list(scratch),
    )(*scalars, *arrays)


def local(
    features,
    links,
    block_slot,
    block_level,
    slot_column,
    conv_first,
    conv_second,
    height_w,
    plane_first,
    plane_second,
):
    count, _, ch = features.shape
    rows = count * CELLS
    faces = (2 * count + 1) * FACE
    mapped = plane_first.shape[3]
    peers = lax.axis_size("gx")
    slot_total = slot_column.shape[1]
    per_peer = slot_total // peers
    x = features.reshape(rows, ch)
    w_first = conv_first.reshape(-1, ch)
    w_second = conv_second.reshape(-1, ch)
    k_first = plane_first.reshape(-1, mapped)
    k_second = plane_second.reshape(-1, mapped)
    slots = block_slot.reshape(1, count)
    block_levels = block_level.reshape(1, count)
    both = ("gy", "gx")

    face_shape = jax.ShapeDtypeStruct((faces, ch), BF16)
    wide = pltpu.VMEM((rows, ch), F32)
    part_shape = jax.ShapeDtypeStruct((rows, ch), F32)

    up, down = call(pack_kernel, "pack", (face_shape, face_shape), (links,), (x,), (wide,))
    from_below = shift(up, both, 1)
    from_above = shift(down, both, -1)
    partial = call(first_interior_kernel, "inside1", part_shape, (links,), (x, w_first))
    hidden, up, down = call(
        hidden_kernel,
        "hidden",
        (jax.ShapeDtypeStruct((rows, ch), BF16), face_shape, face_shape),
        (links,),
        (partial, from_below, from_above, w_first),
        (wide,),
    )
    from_below = shift(up, both, 1)
    from_above = shift(down, both, -1)
    partial = call(second_interior_kernel, "inside2", part_shape, (links,), (hidden, x, w_second))
    outgoing = call(
        lift_kernel,
        "lift",
        jax.ShapeDtypeStruct((peers, per_peer * FACE + ID_ROWS, mapped), BF16),
        (links, slots, block_levels, slot_column),
        (partial, from_below, from_above, w_second, height_w),
        (
            wide,
            pltpu.VMEM((count * FACE, EDGE * ch), BF16),
            pltpu.VMEM((slot_total, FACE, mapped), F32),
        ),
    )
    arrived = lax.all_to_all(outgoing, "gx", split_axis=0, concat_axis=0, tiled=True)

    row_shape = jax.ShapeDtypeStruct((HALO * COLS, mapped), BF16)
    side_shape = jax.ShapeDtypeStruct((HALO, ROWS, mapped), BF16)
    bev, top, bottom, left, right = call(
        gather_kernel,
        "gather",
        (
            jax.ShapeDtypeStruct((ROWS * COLS, mapped), BF16),
            row_shape,
            row_shape,
            side_shape,
            side_shape,
        ),
        (),
        (arrived,),
        (pltpu.VMEM((mapped // LANES, ROWS * COLS, LANES), F32),),
    )
    above = shift(bottom, "gy", 1)
    below = shift(top, "gy", -1)
    corner_above = above.reshape(HALO, COLS, mapped)
    corner_below = below.reshape(HALO, COLS, mapped)

    def side(own, at):
        return jnp.concatenate(
            [
                corner_above[:, at : at + HALO].transpose(1, 0, 2),
                own,
                corner_below[:, at : at + HALO].transpose(1, 0, 2),
            ],
            1,
        )

    from_left = shift(side(right, COLS - HALO), "gx", 1)
    from_right = shift(side(left, 0), "gx", -1)
    gy, gx = lax.axis_index("gy"), lax.axis_index("gx")
    flags = jnp.stack(
        [gy > 0, gy < lax.axis_size("gy") - 1, gx > 0, gx < peers - 1]
    ).astype(jnp.int32)
    out = call(
        plane_kernel,
        "planes",
        jax.ShapeDtypeStruct((ROWS * COLS, mapped), BF16),
        (flags,),
        (bev, above, below, from_left, from_right, k_first, k_second),
        (
            pltpu.VMEM((mapped // LANES, WIDE_ROWS * PITCH, LANES), F32),
            pltpu.VMEM((WIDE_ROWS * COLS, mapped), BF16),
            pltpu.VMEM((WIDE_ROWS * COLS, mapped), BF16),
            pltpu.VMEM((WIDE_ROWS * COLS, mapped), BF16),
            pltpu.VMEM((6, RIM_ROWS + EDGE, mapped), F32),
        ),
    )
    return out.reshape(ROWS, COLS, mapped)


def solution(mesh):
    in_specs = (
        P(("gy", "gx"), None, None),
        P(("gy", "gx"), None),
        P(("gy", "gx")),
        P(("gy", "gx")),
        P(("gy", "gx"), None),
        P(),
        P(),
        P(),
        P(),
        P(),
    )
    out_specs = P("gy", "gx", None)
    return jax.shard_map(local, mesh=mesh, in_specs=in_specs, out_specs=out_specs, check_vma=False)
```

```python
import functools

import jax
import jax.numpy as jnp
from jax import lax
from jax.experimental import pallas as pl
from jax.experimental.pallas import tpu as pltpu
from jax.sharding import PartitionSpec as P

EDGE = 8
FACE = EDGE * EDGE
CELLS = EDGE * FACE
TILE_BR = 8
TILE_BC = 4
ROWS = TILE_BR * EDGE
COLS = TILE_BC * EDGE
HALO = 2
ID_ROWS = 8
LANES = 128
F32 = jnp.float32
BF16 = jnp.bfloat16

VMEM = pl.BlockSpec(memory_space=pltpu.VMEM)
SMEM = pl.BlockSpec(memory_space=pltpu.SMEM)


def shift(block, axis, distance):
    count = lax.axis_size(axis)
    route = [(i, i + distance) for i in range(count) if 0 <= i + distance < count]
    return lax.ppermute(block, axis, route)


def mm(a, b):
    return jnp.dot(a, b, preferred_element_type=F32)


def link_of(links, block, axis):
    return links[axis, block].astype(F32)


def pack_faces(src, links, up, down):
    count = src.shape[0] // CELLS
    faces = count * FACE
    upper_b, lower_b = [], []
    for j in range(count):
        keep = link_of(links, j, 1)
        for a in range(EDGE):
            base = j * CELLS + a * FACE
            upper_b.append(src[base + FACE - EDGE : base + FACE, :] * keep)
            lower_b.append(src[base : base + EDGE, :])
    up[0:faces, :] = jnp.concatenate(upper_b, 0).astype(BF16)
    down[0:faces, :] = jnp.concatenate(lower_b, 0).astype(BF16)
    upper_c = []
    for j in range(count):
        upper_c.append(
            src[pl.ds(j * CELLS + EDGE - 1, FACE, stride=EDGE), :] * link_of(links, j, 2)
        )
    up[faces : 2 * faces, :] = jnp.concatenate(upper_c, 0).astype(BF16)
    down[faces : 2 * faces, :] = src[pl.ds(0, faces, stride=EDGE), :].astype(BF16)
    last = count * CELLS
    up[2 * faces :, :] = (src[last - FACE : last, :] * link_of(links, count - 1, 0)).astype(BF16)
    down[2 * faces :, :] = src[0:FACE, :].astype(BF16)


def pack_kernel(links, x, up, down, wide):
    wide[...] = x[...].astype(F32)
    pack_faces(wide, links, up, down)


def interior(src, links, weights, out, residual):
    count = src.shape[0] // CELLS
    c_at = lax.broadcasted_iota(jnp.int32, (FACE, EDGE, 128), 1)

    def one(j, carry):
        base = pl.multiple_of(j * CELLS, CELLS)
        rows = src[pl.ds(base, CELLS), :]
        after = jnp.minimum(j + 1, count - 1)
        before = jnp.maximum(j - 1, 0)
        keep_after = jnp.where(j + 1 < count, links[0, j], 0).astype(F32)
        keep_before = jnp.where(j > 0, links[0, before], 0).astype(F32)
        over = src[pl.ds(pl.multiple_of(after * CELLS, CELLS), FACE), :]
        under = src[pl.ds(pl.multiple_of(before * CELLS + CELLS - FACE, FACE), FACE), :]
        over = (over.astype(F32) * keep_after).astype(BF16)
        under = (under.astype(F32) * keep_before).astype(BF16)
        wide = rows.astype(F32)
        planes = wide.reshape(EDGE, EDGE, EDGE, 128)
        none = jnp.zeros((EDGE, 1, EDGE, 128), F32)
        lines = wide.reshape(FACE, EDGE, 128)
        taps = [
            rows,
            jnp.concatenate([rows[FACE:], over], 0),
            jnp.concatenate([under, rows[:-FACE]], 0),
            jnp.concatenate([planes[:, 1:], none], 1).reshape(CELLS, 128).astype(BF16),
            jnp.concatenate([none, planes[:, :-1]], 1).reshape(CELLS, 128).astype(BF16),
            jnp.where(c_at == EDGE - 1, 0.0, pltpu.roll(lines, EDGE - 1, 1))
            .reshape(CELLS, 128)
            .astype(BF16),
            jnp.where(c_at == 0, 0.0, pltpu.roll(lines, 1, 1)).reshape(CELLS, 128).astype(BF16),
        ]
        total = mm(jnp.concatenate(taps, 1), weights[...])
        if residual is not None:
            total = total + residual[pl.ds(base, CELLS), :].astype(F32)
        out[pl.ds(base, CELLS), :] = total
        return carry

    lax.fori_loop(0, count, one, 0)


def first_interior_kernel(links, x, weights, out):
    interior(x, links, weights, out, None)


def second_interior_kernel(links, hidden, x, weights, out):
    interior(hidden, links, weights, out, x)


def add_ghosts(total, from_below, from_above, links, weights):
    count = total.shape[0] // CELLS
    faces = count * FACE
    ch = total.shape[1]

    def tap(k):
        return weights[k * ch : (k + 1) * ch, :]

    b_plus = mm(from_above[0:faces, :], tap(3))
    b_minus = mm(from_below[0:faces, :], tap(4))
    for j in range(count):
        keep = link_of(links, j, 1)
        for a in range(EDGE):
            base = j * CELLS + a * FACE
            at = j * FACE + a * EDGE
            total[base + FACE - EDGE : base + FACE, :] += b_plus[at : at + EDGE, :] * keep
            total[base : base + EDGE, :] += b_minus[at : at + EDGE, :]
    c_plus = mm(from_above[faces : 2 * faces, :], tap(5))
    c_minus = mm(from_below[faces : 2 * faces, :], tap(6))
    for j in range(count):
        at = slice(j * FACE, (j + 1) * FACE)
        total[pl.ds(j * CELLS + EDGE - 1, FACE, stride=EDGE), :] += c_plus[at, :] * link_of(
            links, j, 2
        )
        total[pl.ds(j * CELLS, FACE, stride=EDGE), :] += c_minus[at, :]
    last = count * CELLS
    total[last - FACE : last, :] += mm(from_above[2 * faces :, :], tap(1)) * link_of(
        links, count - 1, 0
    )
    total[0:FACE, :] += mm(from_below[2 * faces :, :], tap(2))


def hidden_kernel(links, partial, from_below, from_above, weights, hidden, up, down, total):
    total[...] = partial[...]
    add_ghosts(total, from_below, from_above, links, weights)
    total[...] = jnp.maximum(total[...], 0.0)
    hidden[...] = total[...].astype(BF16)
    pack_faces(total, links, up, down)


def lift_kernel(
    links,
    slots,
    block_levels,
    columns,
    partial,
    from_below,
    from_above,
    weights,
    height,
    out,
    total,
    rows_in,
    sums,
):
    count = partial.shape[0] // CELLS
    faces = count * FACE
    ch = partial.shape[1]
    total[...] = partial[...]
    add_ghosts(total, from_below, from_above, links, weights)
    for c in range(EDGE):
        line = total[pl.ds(c, faces, stride=EDGE), :]
        rows_in[:, c * ch : (c + 1) * ch] = jnp.maximum(line, 0.0).astype(BF16)
    sums[...] = jnp.zeros_like(sums)

    def one(j, carry):
        rows = rows_in[pl.ds(pl.multiple_of(j * FACE, FACE), FACE), :]
        sums[slots[0, j]] += mm(rows, height[block_levels[0, j]])
        return carry

    lax.fori_loop(0, count, one, 0)
    peers = out.shape[0]
    per_peer = sums.shape[0] // peers
    row_at = lax.broadcasted_iota(jnp.int32, (ID_ROWS, out.shape[2]), 0)
    for p in range(peers):
        ids = jnp.zeros(row_at.shape, F32)
        for k in range(per_peer):
            slot = p * per_peer + k
            out[p, k * FACE : (k + 1) * FACE, :] = sums[slot].astype(BF16)
            ids = jnp.where(row_at == k, columns[0, slot].astype(F32), ids)
        out[p, per_peer * FACE :, :] = ids.astype(BF16)


def gather_kernel(arrived, bev, top, bottom, left, right, total):
    peers, rows, ch = arrived.shape
    per_peer = (rows - ID_ROWS) // FACE
    total[...] = jnp.zeros_like(total)
    for p in range(peers):
        ids = arrived[p, per_peer * FACE :, :].astype(F32)
        for k in range(per_peer):
            column = jnp.max(ids[k : k + 1, :]).astype(jnp.int32)
            row_base = (column // TILE_BC) * (EDGE * COLS) + (column % TILE_BC) * EDGE
            block = arrived[p, k * FACE : (k + 1) * FACE, :].astype(F32)
            for a in range(EDGE):
                at = pl.multiple_of(row_base + a * COLS, EDGE)
                for h, lanes in halves(ch):
                    total[h, pl.ds(at, EDGE), :] += block[a * EDGE : (a + 1) * EDGE, lanes]
    for h, lanes in halves(ch):
        bev[:, lanes] = total[h].astype(BF16)
        top[:, lanes] = total[h, 0 : HALO * COLS, :].astype(BF16)
        bottom[:, lanes] = total[h, (ROWS - HALO) * COLS :, :].astype(BF16)
        for x in range(HALO):
            far = COLS - HALO + x
            left[x, :, lanes] = total[h, pl.ds(x, ROWS, stride=COLS), :].astype(BF16)
            right[x, :, lanes] = total[h, pl.ds(far, ROWS, stride=COLS), :].astype(BF16)


def halves(channels):
    return [(h, slice(h * LANES, (h + 1) * LANES)) for h in range(channels // LANES)]


PITCH = COLS + 2 * EDGE
WIDE_ROWS = ROWS + 2 * HALO
MID_ROWS = ROWS + HALO
RIM_ROWS = 72


def side_shifts(padded, before, after, count):
    def one(y, carry):
        at = pl.multiple_of(y * PITCH, EDGE)
        to = pl.multiple_of(y * COLS, COLS)
        for h, lanes in halves(before.shape[1]):
            before[pl.ds(to, COLS), lanes] = padded[h, pl.ds(at + EDGE - 1, COLS), :].astype(BF16)
            after[pl.ds(to, COLS), lanes] = padded[h, pl.ds(at + EDGE + 1, COLS), :].astype(BF16)
        return carry

    lax.fori_loop(0, count, one, 0)


def stacked(sources, first_row, row_count):
    parts = []
    for dy in range(3):
        for source in sources:
            at = pl.multiple_of((first_row + dy) * COLS, COLS)
            parts.append(source[pl.ds(at, row_count * COLS), :])
    return jnp.concatenate(parts, 1)


def plane_kernel(
    flags,
    bev,
    above,
    below,
    left,
    right,
    weights_first,
    weights_second,
    out,
    padded,
    before,
    centre,
    after,
    rim,
):
    ch = bev.shape[1]
    centre[0 : HALO * COLS, :] = above[...]
    centre[HALO * COLS : (HALO + ROWS) * COLS, :] = bev[...]
    centre[(HALO + ROWS) * COLS : WIDE_ROWS * COLS, :] = below[...]

    def widen(y, carry):
        at = pl.multiple_of(y * PITCH + EDGE, EDGE)
        row = centre[pl.ds(pl.multiple_of(y * COLS, COLS), COLS), :].astype(F32)
        for h, lanes in halves(ch):
            padded[h, pl.ds(at, COLS), :] = row[:, lanes]
        return carry

    lax.fori_loop(0, WIDE_ROWS, widen, 0)
    rim[...] = jnp.zeros_like(rim)
    for x in range(HALO):
        lefts = left[x, :, :].astype(F32)
        rights = right[x, :, :].astype(F32)
        rim[x, 0:WIDE_ROWS, :] = lefts
        rim[4 + x, 0:WIDE_ROWS, :] = rights
    for h, lanes in halves(ch):
        own_left = padded[h, pl.ds(EDGE, WIDE_ROWS, stride=PITCH), :]
        own_right = padded[h, pl.ds(EDGE + COLS - 1, WIDE_ROWS, stride=PITCH), :]
        rim[2, 0:WIDE_ROWS, lanes] = own_left
        rim[3, 0:WIDE_ROWS, lanes] = own_right
        padded[h, pl.ds(EDGE - 1, WIDE_ROWS, stride=PITCH), :] = rim[1, 0:WIDE_ROWS, lanes]
        padded[h, pl.ds(EDGE + COLS, WIDE_ROWS, stride=PITCH), :] = rim[4, 0:WIDE_ROWS, lanes]
    side_shifts(padded, before, after, WIDE_ROWS)

    rim_first = []
    for sources in ((0, 1, 2), (3, 4, 5)):
        parts = []
        for dy in range(3):
            for s in sources:
                parts.append(rim[s, dy : dy + RIM_ROWS, :].astype(BF16))
        rim_first.append(jnp.concatenate(parts, 1))
    rim_out = mm(jnp.concatenate(rim_first, 0), weights_first[...])
    rim_out = jnp.maximum(rim_out, 0.0)
    row_at = lax.broadcasted_iota(jnp.int32, (RIM_ROWS, ch), 0)
    inside = jnp.where(
        row_at == 0, flags[0], jnp.where(row_at == MID_ROWS - 1, flags[1], 1)
    ).astype(F32)
    rim_left = rim_out[0:RIM_ROWS, :] * inside * flags[2].astype(F32)
    rim_right = rim_out[RIM_ROWS:, :] * inside * flags[3].astype(F32)

    step = MID_ROWS // 6

    def first_rows(i, carry):
        y = i * step
        block = mm(stacked((before, centre, after), y, step), weights_first[...])
        block = jnp.maximum(block, 0.0)
        for r in range(step):
            keep = jnp.where(
                y + r == 0, flags[0], jnp.where(y + r == MID_ROWS - 1, flags[1], 1)
            ).astype(F32)
            at = pl.multiple_of((y + r) * PITCH + EDGE, EDGE)
            row = block[r * COLS : (r + 1) * COLS, :] * keep
            for h, lanes in halves(ch):
                padded[h, pl.ds(at, COLS), :] = row[:, lanes]
        return carry

    lax.fori_loop(0, MID_ROWS // step, first_rows, 0)
    for h, lanes in halves(ch):
        padded[h, pl.ds(EDGE - 1, MID_ROWS, stride=PITCH), :] = rim_left[0:MID_ROWS, lanes]
        padded[h, pl.ds(EDGE + COLS, MID_ROWS, stride=PITCH), :] = rim_right[0:MID_ROWS, lanes]
    side_shifts(padded, before, after, MID_ROWS)

    def narrow(y, carry):
        at = pl.multiple_of(y * PITCH + EDGE, EDGE)
        to = pl.multiple_of(y * COLS, COLS)
        for h, lanes in halves(ch):
            centre[pl.ds(to, COLS), lanes] = padded[h, pl.ds(at, COLS), :].astype(BF16)
        return carry

    lax.fori_loop(0, MID_ROWS, narrow, 0)
    step2 = 16

    def second_rows(i, carry):
        y = i * step2
        block = mm(stacked((before, centre, after), y, step2), weights_second[...])
        at = pl.multiple_of(y * COLS, COLS)
        own = bev[pl.ds(at, step2 * COLS), :].astype(F32)
        out[pl.ds(at, step2 * COLS), :] = (block + own).astype(BF16)
        return carry

    lax.fori_loop(0, ROWS // step2, second_rows, 0)


def call(kernel, name, out_shape, scalars, arrays, scratch=(), mib=12):
    multiple = isinstance(out_shape, (list, tuple))
    return pl.pallas_call(
        kernel,
        name=name,
        out_shape=out_shape,
        in_specs=[SMEM] * len(scalars) + [VMEM] * len(arrays),
        out_specs=[VMEM] * len(out_shape) if multiple else VMEM,
        scratch_shapes=list(scratch),
        compiler_params=pltpu.CompilerParams(vmem_limit_bytes=mib << 20),
    )(*scalars, *arrays)


def local(
    features,
    links,
    block_slot,
    block_level,
    slot_column,
    conv_first,
    conv_second,
    height_w,
    plane_first,
    plane_second,
):
    count, _, ch = features.shape
    rows = count * CELLS
    faces = (2 * count + 1) * FACE
    mapped = plane_first.shape[3]
    peers = lax.axis_size("gx")
    slot_total = slot_column.shape[1]
    per_peer = slot_total // peers
    x = features.reshape(rows, ch)
    w_first = conv_first.reshape(-1, ch)
    w_second = conv_second.reshape(-1, ch)
    k_first = plane_first.reshape(-1, mapped)
    k_second = plane_second.reshape(-1, mapped)
    slots = block_slot.reshape(1, count)
    block_levels = block_level.reshape(1, count)
    both = ("gy", "gx")
    links = links.T

    face_shape = jax.ShapeDtypeStruct((faces, ch), BF16)
    wide = pltpu.VMEM((rows, ch), F32)
    part_shape = jax.ShapeDtypeStruct((rows, ch), F32)

    up, down = call(pack_kernel, "pack", (face_shape, face_shape), (links,), (x,), (wide,))
    from_below = shift(up, both, 1)
    from_above = shift(down, both, -1)
    partial = call(first_interior_kernel, "inside1", part_shape, (links,), (x, w_first))
    hidden, up, down = call(
        hidden_kernel,
        "hidden",
        (jax.ShapeDtypeStruct((rows, ch), BF16), face_shape, face_shape),
        (links,),
        (partial, from_below, from_above, w_first),
        (wide,),
    )
    from_below = shift(up, both, 1)
    from_above = shift(down, both, -1)
    partial = call(second_interior_kernel, "inside2", part_shape, (links,), (hidden, x, w_second))
    outgoing = call(
        lift_kernel,
        "lift",
        jax.ShapeDtypeStruct((peers, per_peer * FACE + ID_ROWS, mapped), BF16),
        (links, slots, block_levels, slot_column),
        (partial, from_below, from_above, w_second, height_w),
        (
            wide,
            pltpu.VMEM((count * FACE, EDGE * ch), BF16),
            pltpu.VMEM((slot_total, FACE, mapped), F32),
        ),
    )
    arrived = lax.all_to_all(outgoing, "gx", split_axis=0, concat_axis=0, tiled=True)

    row_shape = jax.ShapeDtypeStruct((HALO * COLS, mapped), BF16)
    side_shape = jax.ShapeDtypeStruct((HALO, ROWS, mapped), BF16)
    bev, top, bottom, left, right = call(
        gather_kernel,
        "gather",
        (
            jax.ShapeDtypeStruct((ROWS * COLS, mapped), BF16),
            row_shape,
            row_shape,
            side_shape,
            side_shape,
        ),
        (),
        (arrived,),
        (pltpu.VMEM((mapped // LANES, ROWS * COLS, LANES), F32),),
    )
    above = shift(bottom, "gy", 1)
    below = shift(top, "gy", -1)
    corner_above = above.reshape(HALO, COLS, mapped)
    corner_below = below.reshape(HALO, COLS, mapped)

    def side(own, at):
        return jnp.concatenate(
            [
                corner_above[:, at : at + HALO].transpose(1, 0, 2),
                own,
                corner_below[:, at : at + HALO].transpose(1, 0, 2),
            ],
            1,
        )

    from_left = shift(side(right, COLS - HALO), "gx", 1)
    from_right = shift(side(left, 0), "gx", -1)
    gy, gx = lax.axis_index("gy"), lax.axis_index("gx")
    flags = jnp.stack(
        [gy > 0, gy < lax.axis_size("gy") - 1, gx > 0, gx < peers - 1]
    ).astype(jnp.int32)
    out = call(
        plane_kernel,
        "planes",
        jax.ShapeDtypeStruct((ROWS * COLS, mapped), BF16),
        (flags,),
        (bev, above, below, from_left, from_right, k_first, k_second),
        (
            pltpu.VMEM((mapped // LANES, WIDE_ROWS * PITCH, LANES), F32),
            pltpu.VMEM((WIDE_ROWS * COLS, mapped), BF16),
            pltpu.VMEM((WIDE_ROWS * COLS, mapped), BF16),
            pltpu.VMEM((WIDE_ROWS * COLS, mapped), BF16),
            pltpu.VMEM((6, RIM_ROWS + EDGE, mapped), F32),
        ),
        mib=20,
    )
    return out.reshape(ROWS, COLS, mapped)


def solution(mesh):
    in_specs = (
        P(("gy", "gx"), None, None),
        P(("gy", "gx"), None),
        P(("gy", "gx")),
        P(("gy", "gx")),
        P(("gy", "gx"), None),
        P(),
        P(),
        P(),
        P(),
        P(),
    )
    out_specs = P("gy", "gx", None)
    return jax.shard_map(local, mesh=mesh, in_specs=in_specs, out_specs=out_specs, check_vma=False)
```

```python
import functools

import jax
import jax.numpy as jnp
from jax import lax
from jax.experimental import pallas as pl
from jax.experimental.pallas import tpu as pltpu
from jax.sharding import PartitionSpec as P

EDGE = 8
FACE = EDGE * EDGE
CELLS = EDGE * FACE
TILE_BR = 8
TILE_BC = 4
ROWS = TILE_BR * EDGE
COLS = TILE_BC * EDGE
HALO = 2
ID_ROWS = 8
LANES = 128
F32 = jnp.float32
BF16 = jnp.bfloat16

VMEM = pl.BlockSpec(memory_space=pltpu.VMEM)
SMEM = pl.BlockSpec(memory_space=pltpu.SMEM)


def shift(block, axis, distance):
    count = lax.axis_size(axis)
    route = [(i, i + distance) for i in range(count) if 0 <= i + distance < count]
    return lax.ppermute(block, axis, route)


def mm(a, b):
    return jnp.dot(a, b, preferred_element_type=F32)


def link_of(links, block, axis):
    return links[axis, block].astype(F32)


def pack_faces(src, links, up, down):
    count = src.shape[0] // CELLS
    faces = count * FACE
    upper_b, lower_b = [], []
    for j in range(count):
        keep = link_of(links, j, 1)
        for a in range(EDGE):
            base = j * CELLS + a * FACE
            upper_b.append(src[base + FACE - EDGE : base + FACE, :] * keep)
            lower_b.append(src[base : base + EDGE, :])
    up[0:faces, :] = jnp.concatenate(upper_b, 0).astype(BF16)
    down[0:faces, :] = jnp.concatenate(lower_b, 0).astype(BF16)
    upper_c = []
    for j in range(count):
        upper_c.append(
            src[pl.ds(j * CELLS + EDGE - 1, FACE, stride=EDGE), :] * link_of(links, j, 2)
        )
    up[faces : 2 * faces, :] = jnp.concatenate(upper_c, 0).astype(BF16)
    down[faces : 2 * faces, :] = src[pl.ds(0, faces, stride=EDGE), :].astype(BF16)
    last = count * CELLS
    up[2 * faces :, :] = (src[last - FACE : last, :] * link_of(links, count - 1, 0)).astype(BF16)
    down[2 * faces :, :] = src[0:FACE, :].astype(BF16)


def pack_kernel(links, x, up, down, wide):
    wide[...] = x[...].astype(F32)
    pack_faces(wide, links, up, down)


def interior(src, links, weights, out, residual):
    count = src.shape[0] // CELLS
    c_at = lax.broadcasted_iota(jnp.int32, (FACE, EDGE, 128), 1)

    def one(j, carry):
        base = pl.multiple_of(j * CELLS, CELLS)
        rows = src[pl.ds(base, CELLS), :]
        after = jnp.minimum(j + 1, count - 1)
        before = jnp.maximum(j - 1, 0)
        keep_after = jnp.where(j + 1 < count, links[0, j], 0).astype(F32)
        keep_before = jnp.where(j > 0, links[0, before], 0).astype(F32)
        over = src[pl.ds(pl.multiple_of(after * CELLS, CELLS), FACE), :]
        under = src[pl.ds(pl.multiple_of(before * CELLS + CELLS - FACE, FACE), FACE), :]
        over = (over.astype(F32) * keep_after).astype(BF16)
        under = (under.astype(F32) * keep_before).astype(BF16)
        wide = rows.astype(F32)
        planes = wide.reshape(EDGE, EDGE, EDGE, 128)
        none = jnp.zeros((EDGE, 1, EDGE, 128), F32)
        lines = wide.reshape(FACE, EDGE, 128)
        taps = [
            rows,
            jnp.concatenate([rows[FACE:], over], 0),
            jnp.concatenate([under, rows[:-FACE]], 0),
            jnp.concatenate([planes[:, 1:], none], 1).reshape(CELLS, 128).astype(BF16),
            jnp.concatenate([none, planes[:, :-1]], 1).reshape(CELLS, 128).astype(BF16),
            jnp.where(c_at == EDGE - 1, 0.0, pltpu.roll(lines, EDGE - 1, 1))
            .reshape(CELLS, 128)
            .astype(BF16),
            jnp.where(c_at == 0, 0.0, pltpu.roll(lines, 1, 1)).reshape(CELLS, 128).astype(BF16),
        ]
        total = mm(jnp.concatenate(taps, 1), weights[...])
        if residual is not None:
            total = total + residual[pl.ds(base, CELLS), :].astype(F32)
        out[pl.ds(base, CELLS), :] = total
        return carry

    lax.fori_loop(0, count, one, 0)


def first_interior_kernel(links, x, weights, out):
    interior(x, links, weights, out, None)


def second_interior_kernel(links, hidden, x, weights, out):
    interior(hidden, links, weights, out, x)


def add_ghosts(total, from_below, from_above, links, weights):
    count = total.shape[0] // CELLS
    faces = count * FACE
    ch = total.shape[1]

    def tap(k):
        return weights[k * ch : (k + 1) * ch, :]

    b_plus = mm(from_above[0:faces, :], tap(3))
    b_minus = mm(from_below[0:faces, :], tap(4))
    for j in range(count):
        keep = link_of(links, j, 1)
        for a in range(EDGE):
            base = j * CELLS + a * FACE
            at = j * FACE + a * EDGE
            total[base + FACE - EDGE : base + FACE, :] += b_plus[at : at + EDGE, :] * keep
            total[base : base + EDGE, :] += b_minus[at : at + EDGE, :]
    c_plus = mm(from_above[faces : 2 * faces, :], tap(5))
    c_minus = mm(from_below[faces : 2 * faces, :], tap(6))
    for j in range(count):
        at = slice(j * FACE, (j + 1) * FACE)
        total[pl.ds(j * CELLS + EDGE - 1, FACE, stride=EDGE), :] += c_plus[at, :] * link_of(
            links, j, 2
        )
        total[pl.ds(j * CELLS, FACE, stride=EDGE), :] += c_minus[at, :]
    last = count * CELLS
    total[last - FACE : last, :] += mm(from_above[2 * faces :, :], tap(1)) * link_of(
        links, count - 1, 0
    )
    total[0:FACE, :] += mm(from_below[2 * faces :, :], tap(2))


def hidden_kernel(links, partial, from_below, from_above, weights, hidden, up, down, total):
    total[...] = partial[...]
    add_ghosts(total, from_below, from_above, links, weights)
    total[...] = jnp.maximum(total[...], 0.0)
    hidden[...] = total[...].astype(BF16)
    pack_faces(total, links, up, down)


def lift_kernel(
    links,
    slots,
    block_levels,
    columns,
    partial,
    from_below,
    from_above,
    weights,
    height,
    out,
    total,
    rows_in,
    sums,
):
    count = partial.shape[0] // CELLS
    faces = count * FACE
    ch = partial.shape[1]
    total[...] = partial[...]
    add_ghosts(total, from_below, from_above, links, weights)
    for c in range(EDGE):
        line = total[pl.ds(c, faces, stride=EDGE), :]
        rows_in[:, c * ch : (c + 1) * ch] = jnp.maximum(line, 0.0).astype(BF16)
    sums[...] = jnp.zeros_like(sums)

    def one(j, carry):
        rows = rows_in[pl.ds(pl.multiple_of(j * FACE, FACE), FACE), :]
        sums[slots[0, j]] += mm(rows, height[block_levels[0, j]])
        return carry

    lax.fori_loop(0, count, one, 0)
    peers = out.shape[0]
    per_peer = sums.shape[0] // peers
    row_at = lax.broadcasted_iota(jnp.int32, (ID_ROWS, out.shape[2]), 0)
    for p in range(peers):
        ids = jnp.zeros(row_at.shape, F32)
        for k in range(per_peer):
            slot = p * per_peer + k
            out[p, k * FACE : (k + 1) * FACE, :] = sums[slot].astype(BF16)
            ids = jnp.where(row_at == k, columns[0, slot].astype(F32), ids)
        out[p, per_peer * FACE :, :] = ids.astype(BF16)


def gather_kernel(arrived, bev, top, bottom, left, right, total):
    peers, rows, ch = arrived.shape
    per_peer = (rows - ID_ROWS) // FACE
    total[...] = jnp.zeros_like(total)
    for p in range(peers):
        ids = arrived[p, per_peer * FACE :, :].astype(F32)
        for k in range(per_peer):
            column = jnp.max(ids[k : k + 1, :]).astype(jnp.int32)
            row_base = (column // TILE_BC) * (EDGE * COLS) + (column % TILE_BC) * EDGE
            block = arrived[p, k * FACE : (k + 1) * FACE, :].astype(F32)
            for a in range(EDGE):
                at = pl.multiple_of(row_base + a * COLS, EDGE)
                for h, lanes in halves(ch):
                    total[h, pl.ds(at, EDGE), :] += block[a * EDGE : (a + 1) * EDGE, lanes]
    for h, lanes in halves(ch):
        bev[:, lanes] = total[h].astype(BF16)
        top[:, lanes] = total[h, 0 : HALO * COLS, :].astype(BF16)
        bottom[:, lanes] = total[h, (ROWS - HALO) * COLS :, :].astype(BF16)
        for x in range(HALO):
            far = COLS - HALO + x
            left[x, :, lanes] = total[h, pl.ds(x, ROWS, stride=COLS), :].astype(BF16)
            right[x, :, lanes] = total[h, pl.ds(far, ROWS, stride=COLS), :].astype(BF16)


def halves(channels):
    return [(h, slice(h * LANES, (h + 1) * LANES)) for h in range(channels // LANES)]


WIDE_ROWS = ROWS + 2 * HALO
MID_ROWS = ROWS + HALO
RIM_ROWS = 72
INNER_ROWS = ROWS - 2
CORE_ROWS = ROWS - 4


def tap_columns(weights, dx):
    return jnp.concatenate([weights[dy * 3 + dx] for dy in range(3)], 0)


def three_rows(source, first_row, row_count):
    parts = []
    for dy in range(3):
        at = pl.multiple_of((first_row + dy) * COLS, COLS)
        parts.append(source[pl.ds(at, row_count * COLS), :])
    return jnp.concatenate(parts, 1)


def rows_conv(lhs, weights):
    count = lhs.shape[0]
    x = lax.rem(lax.broadcasted_iota(jnp.int32, (count, weights.shape[2]), 0), COLS)
    from_left = mm(lhs, tap_columns(weights, 0))
    total = jnp.where(x == 0, 0.0, pltpu.roll(from_left, 1, 0))
    total = total + mm(lhs, tap_columns(weights, 1))
    from_right = mm(lhs, tap_columns(weights, 2))
    return total + jnp.where(x == COLS - 1, 0.0, pltpu.roll(from_right, count - 1, 0))


def without_sides(block):
    x = lax.rem(lax.broadcasted_iota(jnp.int32, block.shape, 0), COLS)
    return jnp.where((x == 0) | (x == COLS - 1), 0.0, block)


def first_inner_kernel(bev, weights, inner):
    step = INNER_ROWS // 2

    def one(i, carry):
        block = jnp.maximum(rows_conv(three_rows(bev, i * step, step), weights), 0.0)
        at = pl.multiple_of(i * step * COLS, COLS)
        inner[pl.ds(at, step * COLS), :] = without_sides(block).astype(BF16)
        return carry

    lax.fori_loop(0, INNER_ROWS // step, one, 0)


def second_core_kernel(inner, bev, weights, core):
    step = CORE_ROWS // 4

    def one(i, carry):
        block = rows_conv(three_rows(inner, i * step, step), weights)
        at = pl.multiple_of((i * step + 2) * COLS, COLS)
        block = block + bev[pl.ds(at, step * COLS), :].astype(F32)
        to = pl.multiple_of(i * step * COLS, COLS)
        for h, lanes in halves(block.shape[1]):
            core[h, pl.ds(to, step * COLS), :] = block[:, lanes]
        return carry

    lax.fori_loop(0, CORE_ROWS // step, one, 0)


def edges_kernel(
    flags,
    bev,
    inner,
    core,
    above,
    below,
    own_left,
    own_right,
    left,
    right,
    weights_first,
    weights_second,
    out,
    sides,
    total,
):
    ch = bev.shape[1]
    two = HALO * COLS
    four = 2 * two
    sides[...] = jnp.zeros_like(sides)
    for base, source in ((0, left), (2, own_left), (4, own_right), (6, right)):
        for x in range(HALO):
            sides[base + x, 0:WIDE_ROWS, :] = source[x, :, :].astype(F32)
    lhs = []
    for start in (0, 1, 4, 5):
        parts = []
        for dy in range(3):
            for dx in range(3):
                parts.append(sides[start + dx, dy : dy + RIM_ROWS, :].astype(BF16))
        lhs.append(jnp.concatenate(parts, 1))
    taps = jnp.concatenate([weights_first[t] for t in range(9)], 0)
    columns = jnp.maximum(mm(jnp.concatenate(lhs, 0), taps), 0.0)
    row_at = lax.broadcasted_iota(jnp.int32, (RIM_ROWS, ch), 0)
    keep = jnp.where(row_at == 0, flags[0], jnp.where(row_at == MID_ROWS - 1, flags[1], 1)).astype(
        F32
    )
    for k, side_keep in enumerate((flags[2], 1, 1, flags[3])):
        block = columns[k * RIM_ROWS : (k + 1) * RIM_ROWS, :] * keep
        if k in (0, 3):
            block = block * side_keep.astype(F32)
        sides[k, 0:RIM_ROWS, :] = block

    high = jnp.concatenate([above[...], bev[0:two, :]], 0)
    low = jnp.concatenate([bev[ROWS * COLS - two :, :], below[...]], 0)

    def strips(upper, lower):
        parts = []
        for source in (upper, lower):
            rows = [source[dy * COLS : dy * COLS + two] for dy in range(3)]
            parts.append(jnp.concatenate(rows, 1))
        return jnp.concatenate(parts, 0)

    strip = without_sides(jnp.maximum(rows_conv(strips(high, low), weights_first), 0.0))
    line = lax.broadcasted_iota(jnp.int32, (four, ch), 0) // COLS
    keep = jnp.where(line == 0, flags[0], jnp.where(line == 3, flags[1], 1)).astype(F32)
    strip = (strip * keep).astype(BF16)

    high = jnp.concatenate([strip[0:two], inner[0:two, :]], 0)
    low = jnp.concatenate([inner[INNER_ROWS * COLS - two :, :], strip[two:]], 0)
    strip = rows_conv(strips(high, low), weights_second)
    for h, lanes in halves(ch):
        top_rows = strip[0:two, lanes] + bev[0:two, lanes].astype(F32)
        low_rows = strip[two:, lanes] + bev[ROWS * COLS - two :, lanes].astype(F32)
        total[h, 0:two, :] = top_rows
        total[h, two : ROWS * COLS - two, :] = core[h, :, :]
        total[h, ROWS * COLS - two :, :] = low_rows

    column = []
    for k in range(4):
        rows = [sides[k, dy : dy + ROWS, :].astype(BF16) for dy in range(3)]
        column.append(jnp.concatenate(rows, 1))
    w0, w1, w2 = [tap_columns(weights_second, dx) for dx in range(3)]
    added = (
        (0, mm(column[0], w0) + mm(column[1], w1)),
        (1, mm(column[1], w0)),
        (COLS - 2, mm(column[2], w2)),
        (COLS - 1, mm(column[2], w1) + mm(column[3], w2)),
    )
    for x, block in added:
        for h, lanes in halves(ch):
            total[h, pl.ds(x, ROWS, stride=COLS), :] += block[:, lanes]
    for h, lanes in halves(ch):
        out[:, lanes] = total[h].astype(BF16)


def call(kernel, name, out_shape, scalars, arrays, scratch=(), mib=12):
    multiple = isinstance(out_shape, (list, tuple))
    return pl.pallas_call(
        kernel,
        name=name,
        out_shape=out_shape,
        in_specs=[SMEM] * len(scalars) + [VMEM] * len(arrays),
        out_specs=[VMEM] * len(out_shape) if multiple else VMEM,
        scratch_shapes=list(scratch),
        compiler_params=pltpu.CompilerParams(vmem_limit_bytes=mib << 20),
    )(*scalars, *arrays)


def local(
    features,
    links,
    block_slot,
    block_level,
    slot_column,
    conv_first,
    conv_second,
    height_w,
    plane_first,
    plane_second,
):
    count, _, ch = features.shape
    rows = count * CELLS
    faces = (2 * count + 1) * FACE
    mapped = plane_first.shape[3]
    peers = lax.axis_size("gx")
    slot_total = slot_column.shape[1]
    per_peer = slot_total // peers
    x = features.reshape(rows, ch)
    w_first = conv_first.reshape(-1, ch)
    w_second = conv_second.reshape(-1, ch)
    k_first = plane_first.reshape(9, mapped, mapped)
    k_second = plane_second.reshape(9, mapped, mapped)
    slots = block_slot.reshape(1, count)
    block_levels = block_level.reshape(1, count)
    both = ("gy", "gx")
    links = links.T

    face_shape = jax.ShapeDtypeStruct((faces, ch), BF16)
    wide = pltpu.VMEM((rows, ch), F32)
    part_shape = jax.ShapeDtypeStruct((rows, ch), F32)

    up, down = call(pack_kernel, "pack", (face_shape, face_shape), (links,), (x,), (wide,))
    from_below = shift(up, both, 1)
    from_above = shift(down, both, -1)
    partial = call(first_interior_kernel, "inside1", part_shape, (links,), (x, w_first))
    hidden, up, down = call(
        hidden_kernel,
        "hidden",
        (jax.ShapeDtypeStruct((rows, ch), BF16), face_shape, face_shape),
        (links,),
        (partial, from_below, from_above, w_first),
        (wide,),
    )
    from_below = shift(up, both, 1)
    from_above = shift(down, both, -1)
    partial = call(second_interior_kernel, "inside2", part_shape, (links,), (hidden, x, w_second))
    outgoing = call(
        lift_kernel,
        "lift",
        jax.ShapeDtypeStruct((peers, per_peer * FACE + ID_ROWS, mapped), BF16),
        (links, slots, block_levels, slot_column),
        (partial, from_below, from_above, w_second, height_w),
        (
            wide,
            pltpu.VMEM((count * FACE, EDGE * ch), BF16),
            pltpu.VMEM((slot_total, FACE, mapped), F32),
        ),
    )
    arrived = lax.all_to_all(outgoing, "gx", split_axis=0, concat_axis=0, tiled=True)

    row_shape = jax.ShapeDtypeStruct((HALO * COLS, mapped), BF16)
    side_shape = jax.ShapeDtypeStruct((HALO, ROWS, mapped), BF16)
    bev, top, bottom, left, right = call(
        gather_kernel,
        "gather",
        (
            jax.ShapeDtypeStruct((ROWS * COLS, mapped), BF16),
            row_shape,
            row_shape,
            side_shape,
            side_shape,
        ),
        (),
        (arrived,),
        (pltpu.VMEM((mapped // LANES, ROWS * COLS, LANES), F32),),
    )
    above = shift(bottom, "gy", 1)
    below = shift(top, "gy", -1)
    inner = call(
        first_inner_kernel,
        "first_inner",
        jax.ShapeDtypeStruct((INNER_ROWS * COLS, mapped), BF16),
        (),
        (bev, k_first),
    )
    above, below, inner = lax.optimization_barrier((above, below, inner))
    corner_above = above.reshape(HALO, COLS, mapped)
    corner_below = below.reshape(HALO, COLS, mapped)

    def side(own, at):
        return jnp.concatenate(
            [
                corner_above[:, at : at + HALO].transpose(1, 0, 2),
                own,
                corner_below[:, at : at + HALO].transpose(1, 0, 2),
            ],
            1,
        )

    own_left, own_right = side(left, 0), side(right, COLS - HALO)
    from_left = shift(own_right, "gx", 1)
    from_right = shift(own_left, "gx", -1)
    core = call(
        second_core_kernel,
        "second_core",
        jax.ShapeDtypeStruct((mapped // LANES, CORE_ROWS * COLS, LANES), F32),
        (),
        (inner, bev, k_second),
    )
    gy, gx = lax.axis_index("gy"), lax.axis_index("gx")
    flags = jnp.stack(
        [gy > 0, gy < lax.axis_size("gy") - 1, gx > 0, gx < peers - 1]
    ).astype(jnp.int32)
    out = call(
        edges_kernel,
        "edges",
        jax.ShapeDtypeStruct((ROWS * COLS, mapped), BF16),
        (flags,),
        (
            bev,
            inner,
            core,
            above,
            below,
            own_left,
            own_right,
            from_left,
            from_right,
            k_first,
            k_second,
        ),
        (
            pltpu.VMEM((8, RIM_ROWS + EDGE, mapped), F32),
            pltpu.VMEM((mapped // LANES, ROWS * COLS, LANES), F32),
        ),
    )
    return out.reshape(ROWS, COLS, mapped)


def solution(mesh):
    in_specs = (
        P(("gy", "gx"), None, None),
        P(("gy", "gx"), None),
        P(("gy", "gx")),
        P(("gy", "gx")),
        P(("gy", "gx"), None),
        P(),
        P(),
        P(),
        P(),
        P(),
    )
    out_specs = P("gy", "gx", None)
    return jax.shard_map(local, mesh=mesh, in_specs=in_specs, out_specs=out_specs, check_vma=False)
```

```python
import functools

import jax
import jax.numpy as jnp
from jax import lax
from jax.experimental import pallas as pl
from jax.experimental.pallas import tpu as pltpu
from jax.sharding import PartitionSpec as P

EDGE = 8
FACE = EDGE * EDGE
CELLS = EDGE * FACE
TILE_BR = 8
TILE_BC = 4
ROWS = TILE_BR * EDGE
COLS = TILE_BC * EDGE
HALO = 2
ID_ROWS = 8
LANES = 128
F32 = jnp.float32
BF16 = jnp.bfloat16

VMEM = pl.BlockSpec(memory_space=pltpu.VMEM)
SMEM = pl.BlockSpec(memory_space=pltpu.SMEM)


def shift(block, axis, distance):
    count = lax.axis_size(axis)
    route = [(i, i + distance) for i in range(count) if 0 <= i + distance < count]
    return lax.ppermute(block, axis, route)


def swap(first, second, axis):
    count = lax.axis_size(axis)
    near = [(i, i ^ 1) for i in range(count) if i ^ 1 < count]
    far = [(i, i + 1 if i % 2 else i - 1) for i in range(1, count)]
    far = [(i, k) for i, k in far if k < count]
    return lax.ppermute(first, axis, near), lax.ppermute(second, axis, far)


def route(odd, up, down, first, second):
    @pl.when(odd == 0)
    def _():
        first[...] = up[...]
        second[...] = down[...]

    @pl.when(odd != 0)
    def _():
        first[...] = down[...]
        second[...] = up[...]


def mm(a, b):
    return jnp.dot(a, b, preferred_element_type=F32)


def link_of(links, block, axis):
    return links[axis, block].astype(F32)


def pack_faces(src, links, up, down):
    count = src.shape[0] // CELLS
    faces = count * FACE
    upper_b, lower_b = [], []
    for j in range(count):
        keep = link_of(links, j, 1)
        for a in range(EDGE):
            base = j * CELLS + a * FACE
            upper_b.append(src[base + FACE - EDGE : base + FACE, :] * keep)
            lower_b.append(src[base : base + EDGE, :])
    up[0:faces, :] = jnp.concatenate(upper_b, 0).astype(BF16)
    down[0:faces, :] = jnp.concatenate(lower_b, 0).astype(BF16)
    upper_c = []
    for j in range(count):
        upper_c.append(
            src[pl.ds(j * CELLS + EDGE - 1, FACE, stride=EDGE), :] * link_of(links, j, 2)
        )
    up[faces : 2 * faces, :] = jnp.concatenate(upper_c, 0).astype(BF16)
    down[faces : 2 * faces, :] = src[pl.ds(0, faces, stride=EDGE), :].astype(BF16)
    last = count * CELLS
    up[2 * faces :, :] = (src[last - FACE : last, :] * link_of(links, count - 1, 0)).astype(BF16)
    down[2 * faces :, :] = src[0:FACE, :].astype(BF16)


def pack_kernel(flags, links, x, first, second, wide, up, down):
    wide[...] = x[...].astype(F32)
    pack_faces(wide, links, up, down)
    route(flags[4], up, down, first, second)


def interior(src, links, weights, out, residual):
    count = src.shape[0] // CELLS
    c_at = lax.broadcasted_iota(jnp.int32, (FACE, EDGE, 128), 1)

    def one(j, carry):
        base = pl.multiple_of(j * CELLS, CELLS)
        rows = src[pl.ds(base, CELLS), :]
        after = jnp.minimum(j + 1, count - 1)
        before = jnp.maximum(j - 1, 0)
        keep_after = jnp.where(j + 1 < count, links[0, j], 0).astype(F32)
        keep_before = jnp.where(j > 0, links[0, before], 0).astype(F32)
        over = src[pl.ds(pl.multiple_of(after * CELLS, CELLS), FACE), :]
        under = src[pl.ds(pl.multiple_of(before * CELLS + CELLS - FACE, FACE), FACE), :]
        over = (over.astype(F32) * keep_after).astype(BF16)
        under = (under.astype(F32) * keep_before).astype(BF16)
        wide = rows.astype(F32)
        planes = wide.reshape(EDGE, EDGE, EDGE, 128)
        none = jnp.zeros((EDGE, 1, EDGE, 128), F32)
        lines = wide.reshape(FACE, EDGE, 128)
        taps = [
            rows,
            jnp.concatenate([rows[FACE:], over], 0),
            jnp.concatenate([under, rows[:-FACE]], 0),
            jnp.concatenate([planes[:, 1:], none], 1).reshape(CELLS, 128).astype(BF16),
            jnp.concatenate([none, planes[:, :-1]], 1).reshape(CELLS, 128).astype(BF16),
            jnp.where(c_at == EDGE - 1, 0.0, pltpu.roll(lines, EDGE - 1, 1))
            .reshape(CELLS, 128)
            .astype(BF16),
            jnp.where(c_at == 0, 0.0, pltpu.roll(lines, 1, 1)).reshape(CELLS, 128).astype(BF16),
        ]
        total = mm(jnp.concatenate(taps, 1), weights[...])
        if residual is not None:
            total = total + residual[pl.ds(base, CELLS), :].astype(F32)
        out[pl.ds(base, CELLS), :] = total
        return carry

    lax.fori_loop(0, count, one, 0)


def first_interior_kernel(links, x, weights, out):
    interior(x, links, weights, out, None)


def second_interior_kernel(links, hidden, x, weights, out):
    interior(hidden, links, weights, out, x)


def add_ghosts(total, from_below, from_above, links, weights):
    count = total.shape[0] // CELLS
    faces = count * FACE
    ch = total.shape[1]

    def tap(k):
        return weights[k * ch : (k + 1) * ch, :]

    b_plus = mm(from_above[0:faces, :], tap(3))
    b_minus = mm(from_below[0:faces, :], tap(4))
    for j in range(count):
        keep = link_of(links, j, 1)
        for a in range(EDGE):
            base = j * CELLS + a * FACE
            at = j * FACE + a * EDGE
            total[base + FACE - EDGE : base + FACE, :] += b_plus[at : at + EDGE, :] * keep
            total[base : base + EDGE, :] += b_minus[at : at + EDGE, :]
    c_plus = mm(from_above[faces : 2 * faces, :], tap(5))
    c_minus = mm(from_below[faces : 2 * faces, :], tap(6))
    for j in range(count):
        at = slice(j * FACE, (j + 1) * FACE)
        total[pl.ds(j * CELLS + EDGE - 1, FACE, stride=EDGE), :] += c_plus[at, :] * link_of(
            links, j, 2
        )
        total[pl.ds(j * CELLS, FACE, stride=EDGE), :] += c_minus[at, :]
    last = count * CELLS
    total[last - FACE : last, :] += mm(from_above[2 * faces :, :], tap(1)) * link_of(
        links, count - 1, 0
    )
    total[0:FACE, :] += mm(from_below[2 * faces :, :], tap(2))


def hidden_kernel(
    flags,
    links,
    partial,
    first_in,
    second_in,
    weights,
    hidden,
    first,
    second,
    total,
    up,
    down,
    from_below,
    from_above,
):
    total[...] = partial[...]
    route(flags[4], first_in, second_in, from_above, from_below)
    add_ghosts(total, from_below, from_above, links, weights)
    total[...] = jnp.maximum(total[...], 0.0)
    hidden[...] = total[...].astype(BF16)
    pack_faces(total, links, up, down)
    route(flags[4], up, down, first, second)


def lift_kernel(
    flags,
    links,
    slots,
    block_levels,
    columns,
    partial,
    first_in,
    second_in,
    weights,
    height,
    out,
    total,
    rows_in,
    sums,
    from_below,
    from_above,
):
    count = partial.shape[0] // CELLS
    faces = count * FACE
    ch = partial.shape[1]
    total[...] = partial[...]
    route(flags[4], first_in, second_in, from_above, from_below)
    add_ghosts(total, from_below, from_above, links, weights)
    for c in range(EDGE):
        line = total[pl.ds(c, faces, stride=EDGE), :]
        rows_in[:, c * ch : (c + 1) * ch] = jnp.maximum(line, 0.0).astype(BF16)
    sums[...] = jnp.zeros_like(sums)

    def one(j, carry):
        rows = rows_in[pl.ds(pl.multiple_of(j * FACE, FACE), FACE), :]
        sums[slots[0, j]] += mm(rows, height[block_levels[0, j]])
        return carry

    lax.fori_loop(0, count, one, 0)
    peers = out.shape[0]
    per_peer = sums.shape[0] // peers
    row_at = lax.broadcasted_iota(jnp.int32, (ID_ROWS, out.shape[2]), 0)
    for p in range(peers):
        ids = jnp.zeros(row_at.shape, F32)
        for k in range(per_peer):
            slot = p * per_peer + k
            out[p, k * FACE : (k + 1) * FACE, :] = sums[slot].astype(BF16)
            ids = jnp.where(row_at == k, columns[0, slot].astype(F32), ids)
        out[p, per_peer * FACE :, :] = ids.astype(BF16)


def gather_kernel(arrived, bev, top, bottom, left, right, total):
    peers, rows, ch = arrived.shape
    per_peer = (rows - ID_ROWS) // FACE
    total[...] = jnp.zeros_like(total)
    for p in range(peers):
        ids = arrived[p, per_peer * FACE :, :].astype(F32)
        for k in range(per_peer):
            column = jnp.max(ids[k : k + 1, :]).astype(jnp.int32)
            row_base = (column // TILE_BC) * (EDGE * COLS) + (column % TILE_BC) * EDGE
            block = arrived[p, k * FACE : (k + 1) * FACE, :].astype(F32)
            for a in range(EDGE):
                at = pl.multiple_of(row_base + a * COLS, EDGE)
                for h, lanes in halves(ch):
                    total[h, pl.ds(at, EDGE), :] += block[a * EDGE : (a + 1) * EDGE, lanes]
    for h, lanes in halves(ch):
        bev[:, lanes] = total[h].astype(BF16)
        top[:, lanes] = total[h, 0 : HALO * COLS, :].astype(BF16)
        bottom[:, lanes] = total[h, (ROWS - HALO) * COLS :, :].astype(BF16)
        for x in range(HALO):
            far = COLS - HALO + x
            left[x, :, lanes] = total[h, pl.ds(x, ROWS, stride=COLS), :].astype(BF16)
            right[x, :, lanes] = total[h, pl.ds(far, ROWS, stride=COLS), :].astype(BF16)


def halves(channels):
    return [(h, slice(h * LANES, (h + 1) * LANES)) for h in range(channels // LANES)]


WIDE_ROWS = ROWS + 2 * HALO
MID_ROWS = ROWS + HALO
RIM_ROWS = 72
INNER_ROWS = ROWS - 2
CORE_ROWS = ROWS - 4


def tap_columns(weights, dx):
    return jnp.concatenate([weights[dy * 3 + dx] for dy in range(3)], 0)


def three_rows(source, first_row, row_count):
    parts = []
    for dy in range(3):
        at = pl.multiple_of((first_row + dy) * COLS, COLS)
        parts.append(source[pl.ds(at, row_count * COLS), :])
    return jnp.concatenate(parts, 1)


def rows_conv(lhs, weights):
    count = lhs.shape[0]
    x = lax.rem(lax.broadcasted_iota(jnp.int32, (count, weights.shape[2]), 0), COLS)
    from_left = mm(lhs, tap_columns(weights, 0))
    total = jnp.where(x == 0, 0.0, pltpu.roll(from_left, 1, 0))
    total = total + mm(lhs, tap_columns(weights, 1))
    from_right = mm(lhs, tap_columns(weights, 2))
    return total + jnp.where(x == COLS - 1, 0.0, pltpu.roll(from_right, count - 1, 0))


def without_sides(block):
    x = lax.rem(lax.broadcasted_iota(jnp.int32, block.shape, 0), COLS)
    return jnp.where((x == 0) | (x == COLS - 1), 0.0, block)


def first_inner_kernel(bev, weights, inner):
    step = INNER_ROWS // 2

    def one(i, carry):
        block = jnp.maximum(rows_conv(three_rows(bev, i * step, step), weights), 0.0)
        at = pl.multiple_of(i * step * COLS, COLS)
        inner[pl.ds(at, step * COLS), :] = without_sides(block).astype(BF16)
        return carry

    lax.fori_loop(0, INNER_ROWS // step, one, 0)


def second_core_kernel(inner, bev, weights, core):
    step = CORE_ROWS // 4

    def one(i, carry):
        block = rows_conv(three_rows(inner, i * step, step), weights)
        at = pl.multiple_of((i * step + 2) * COLS, COLS)
        block = block + bev[pl.ds(at, step * COLS), :].astype(F32)
        to = pl.multiple_of(i * step * COLS, COLS)
        for h, lanes in halves(block.shape[1]):
            core[h, pl.ds(to, step * COLS), :] = block[:, lanes]
        return carry

    lax.fori_loop(0, CORE_ROWS // step, one, 0)


def edges_kernel(
    flags,
    bev,
    inner,
    core,
    above,
    below,
    own_left,
    own_right,
    first_in,
    second_in,
    weights_first,
    weights_second,
    out,
    sides,
    total,
):
    ch = bev.shape[1]
    two = HALO * COLS
    four = 2 * two
    sides[...] = jnp.zeros_like(sides)

    def place(base, source):
        for x in range(HALO):
            sides[base + x, 0:WIDE_ROWS, :] = source[x, :, :].astype(F32)

    place(2, own_left)
    place(4, own_right)

    @pl.when(flags[5] == 0)
    def _():
        place(0, second_in)
        place(6, first_in)

    @pl.when(flags[5] != 0)
    def _():
        place(0, first_in)
        place(6, second_in)

    lhs = []
    for start in (0, 1, 4, 5):
        parts = []
        for dy in range(3):
            for dx in range(3):
                parts.append(sides[start + dx, dy : dy + RIM_ROWS, :].astype(BF16))
        lhs.append(jnp.concatenate(parts, 1))
    taps = jnp.concatenate([weights_first[t] for t in range(9)], 0)
    columns = jnp.maximum(mm(jnp.concatenate(lhs, 0), taps), 0.0)
    row_at = lax.broadcasted_iota(jnp.int32, (RIM_ROWS, ch), 0)
    keep = jnp.where(row_at == 0, flags[0], jnp.where(row_at == MID_ROWS - 1, flags[1], 1)).astype(
        F32
    )
    for k, side_keep in enumerate((flags[2], 1, 1, flags[3])):
        block = columns[k * RIM_ROWS : (k + 1) * RIM_ROWS, :] * keep
        if k in (0, 3):
            block = block * side_keep.astype(F32)
        sides[k, 0:RIM_ROWS, :] = block

    high = jnp.concatenate([above[...], bev[0:two, :]], 0)
    low = jnp.concatenate([bev[ROWS * COLS - two :, :], below[...]], 0)

    def strips(upper, lower):
        parts = []
        for source in (upper, lower):
            rows = [source[dy * COLS : dy * COLS + two] for dy in range(3)]
            parts.append(jnp.concatenate(rows, 1))
        return jnp.concatenate(parts, 0)

    strip = without_sides(jnp.maximum(rows_conv(strips(high, low), weights_first), 0.0))
    line = lax.broadcasted_iota(jnp.int32, (four, ch), 0) // COLS
    keep = jnp.where(line == 0, flags[0], jnp.where(line == 3, flags[1], 1)).astype(F32)
    strip = (strip * keep).astype(BF16)

    high = jnp.concatenate([strip[0:two], inner[0:two, :]], 0)
    low = jnp.concatenate([inner[INNER_ROWS * COLS - two :, :], strip[two:]], 0)
    strip = rows_conv(strips(high, low), weights_second)
    for h, lanes in halves(ch):
        top_rows = strip[0:two, lanes] + bev[0:two, lanes].astype(F32)
        low_rows = strip[two:, lanes] + bev[ROWS * COLS - two :, lanes].astype(F32)
        total[h, 0:two, :] = top_rows
        total[h, two : ROWS * COLS - two, :] = core[h, :, :]
        total[h, ROWS * COLS - two :, :] = low_rows

    column = []
    for k in range(4):
        rows = [sides[k, dy : dy + ROWS, :].astype(BF16) for dy in range(3)]
        column.append(jnp.concatenate(rows, 1))
    w0, w1, w2 = [tap_columns(weights_second, dx) for dx in range(3)]
    added = (
        (0, mm(column[0], w0) + mm(column[1], w1)),
        (1, mm(column[1], w0)),
        (COLS - 2, mm(column[2], w2)),
        (COLS - 1, mm(column[2], w1) + mm(column[3], w2)),
    )
    for x, block in added:
        for h, lanes in halves(ch):
            total[h, pl.ds(x, ROWS, stride=COLS), :] += block[:, lanes]
    for h, lanes in halves(ch):
        out[:, lanes] = total[h].astype(BF16)


def call(kernel, name, out_shape, scalars, arrays, scratch=(), mib=12):
    multiple = isinstance(out_shape, (list, tuple))
    return pl.pallas_call(
        kernel,
        name=name,
        out_shape=out_shape,
        in_specs=[SMEM] * len(scalars) + [VMEM] * len(arrays),
        out_specs=[VMEM] * len(out_shape) if multiple else VMEM,
        scratch_shapes=list(scratch),
        compiler_params=pltpu.CompilerParams(vmem_limit_bytes=mib << 20),
    )(*scalars, *arrays)


def local(
    features,
    links,
    block_slot,
    block_level,
    slot_column,
    conv_first,
    conv_second,
    height_w,
    plane_first,
    plane_second,
):
    count, _, ch = features.shape
    rows = count * CELLS
    faces = (2 * count + 1) * FACE
    mapped = plane_first.shape[3]
    peers = lax.axis_size("gx")
    slot_total = slot_column.shape[1]
    per_peer = slot_total // peers
    x = features.reshape(rows, ch)
    w_first = conv_first.reshape(-1, ch)
    w_second = conv_second.reshape(-1, ch)
    k_first = plane_first.reshape(9, mapped, mapped)
    k_second = plane_second.reshape(9, mapped, mapped)
    slots = block_slot.reshape(1, count)
    block_levels = block_level.reshape(1, count)
    both = ("gy", "gx")
    links = links.T

    face_shape = jax.ShapeDtypeStruct((faces, ch), BF16)
    wide = pltpu.VMEM((rows, ch), F32)
    part_shape = jax.ShapeDtypeStruct((rows, ch), F32)

    gy, gx = lax.axis_index("gy"), lax.axis_index("gx")
    flags = jnp.stack(
        [gy > 0, gy < lax.axis_size("gy") - 1, gx > 0, gx < peers - 1, lax.axis_index(both) % 2, gx % 2]
    ).astype(jnp.int32)
    face = pltpu.VMEM((faces, ch), BF16)
    first, second = call(
        pack_kernel, "pack", (face_shape, face_shape), (flags, links), (x,), (wide, face, face)
    )
    first, second = swap(first, second, both)
    partial = call(first_interior_kernel, "inside1", part_shape, (links,), (x, w_first))
    hidden, first, second = call(
        hidden_kernel,
        "hidden",
        (jax.ShapeDtypeStruct((rows, ch), BF16), face_shape, face_shape),
        (flags, links),
        (partial, first, second, w_first),
        (wide, face, face, face, face),
    )
    first, second = swap(first, second, both)
    partial = call(second_interior_kernel, "inside2", part_shape, (links,), (hidden, x, w_second))
    outgoing = call(
        lift_kernel,
        "lift",
        jax.ShapeDtypeStruct((peers, per_peer * FACE + ID_ROWS, mapped), BF16),
        (flags, links, slots, block_levels, slot_column),
        (partial, first, second, w_second, height_w),
        (
            wide,
            pltpu.VMEM((count * FACE, EDGE * ch), BF16),
            pltpu.VMEM((slot_total, FACE, mapped), F32),
            face,
            face,
        ),
    )
    arrived = lax.all_to_all(outgoing, "gx", split_axis=0, concat_axis=0, tiled=True)

    row_shape = jax.ShapeDtypeStruct((HALO * COLS, mapped), BF16)
    side_shape = jax.ShapeDtypeStruct((HALO, ROWS, mapped), BF16)
    bev, top, bottom, left, right = call(
        gather_kernel,
        "gather",
        (
            jax.ShapeDtypeStruct((ROWS * COLS, mapped), BF16),
            row_shape,
            row_shape,
            side_shape,
            side_shape,
        ),
        (),
        (arrived,),
        (pltpu.VMEM((mapped // LANES, ROWS * COLS, LANES), F32),),
    )
    above = shift(bottom, "gy", 1)
    below = shift(top, "gy", -1)
    inner = call(
        first_inner_kernel,
        "first_inner",
        jax.ShapeDtypeStruct((INNER_ROWS * COLS, mapped), BF16),
        (),
        (bev, k_first),
    )
    above, below, inner = lax.optimization_barrier((above, below, inner))
    corner_above = above.reshape(HALO, COLS, mapped)
    corner_below = below.reshape(HALO, COLS, mapped)

    def side(own, at):
        return jnp.concatenate(
            [
                corner_above[:, at : at + HALO].transpose(1, 0, 2),
                own,
                corner_below[:, at : at + HALO].transpose(1, 0, 2),
            ],
            1,
        )

    own_left, own_right = side(left, 0), side(right, COLS - HALO)
    odd = gx % 2 == 1
    first, second = swap(
        jnp.where(odd, own_left, own_right), jnp.where(odd, own_right, own_left), "gx"
    )
    core = call(
        second_core_kernel,
        "second_core",
        jax.ShapeDtypeStruct((mapped // LANES, CORE_ROWS * COLS, LANES), F32),
        (),
        (inner, bev, k_second),
    )
    out = call(
        edges_kernel,
        "edges",
        jax.ShapeDtypeStruct((ROWS * COLS, mapped), BF16),
        (flags,),
        (
            bev,
            inner,
            core,
            above,
            below,
            own_left,
            own_right,
            first,
            second,
            k_first,
            k_second,
        ),
        (
            pltpu.VMEM((8, RIM_ROWS + EDGE, mapped), F32),
            pltpu.VMEM((mapped // LANES, ROWS * COLS, LANES), F32),
        ),
    )
    return out.reshape(ROWS, COLS, mapped)


def solution(mesh):
    in_specs = (
        P(("gy", "gx"), None, None),
        P(("gy", "gx"), None),
        P(("gy", "gx")),
        P(("gy", "gx")),
        P(("gy", "gx"), None),
        P(),
        P(),
        P(),
        P(),
        P(),
    )
    out_specs = P("gy", "gx", None)
    return jax.shard_map(local, mesh=mesh, in_specs=in_specs, out_specs=out_specs, check_vma=False)
```

```python
import jax
import jax.numpy as jnp
from jax import lax
from jax.experimental import pallas as pl
from jax.experimental.pallas import tpu as pltpu
from jax.sharding import PartitionSpec as P


EDGE = 8
FACE = EDGE * EDGE
CELLS = EDGE * FACE
TILE_BR = 8
TILE_BC = 4
ROWS = TILE_BR * EDGE
COLS = TILE_BC * EDGE
HALO = 2
ID_ROWS = 8
LANES = 128
F32 = jnp.float32
BF16 = jnp.bfloat16

VMEM = pl.BlockSpec(memory_space=pltpu.VMEM)
SMEM = pl.BlockSpec(memory_space=pltpu.SMEM)


def swap(first, second, axis):
    count = lax.axis_size(axis)
    near = [(i, i ^ 1) for i in range(count) if i ^ 1 < count]
    far = [(i, i + 1 if i % 2 else i - 1) for i in range(1, count)]
    far = [(i, k) for i, k in far if k < count]
    first = lax.ppermute(first, axis, near)
    second = lax.ppermute(second, axis, far)
    return first, second


def route(odd, up, down, first, second):
    @pl.when(odd == 0)
    def _():
        first[...] = up[...]
        second[...] = down[...]

    @pl.when(odd != 0)
    def _():
        first[...] = down[...]
        second[...] = up[...]


def mm(a, b):
    return jnp.dot(a, b, preferred_element_type=F32)


def link_of(links, block, axis):
    return links[axis, block].astype(F32)


def pack_faces(src, links, up, down):
    count = src.shape[0] // CELLS
    faces = count * FACE
    upper_b, lower_b = [], []
    for j in range(count):
        keep = link_of(links, j, 1)
        for a in range(EDGE):
            base = j * CELLS + a * FACE
            upper_b.append(src[base + FACE - EDGE : base + FACE, :] * keep)
            lower_b.append(src[base : base + EDGE, :])
    up[0:faces, :] = jnp.concatenate(upper_b, 0).astype(BF16)
    down[0:faces, :] = jnp.concatenate(lower_b, 0).astype(BF16)
    upper_c = []
    for j in range(count):
        upper_c.append(
            src[pl.ds(j * CELLS + EDGE - 1, FACE, stride=EDGE), :] * link_of(links, j, 2)
        )
    up[faces : 2 * faces, :] = jnp.concatenate(upper_c, 0).astype(BF16)
    down[faces : 2 * faces, :] = src[pl.ds(0, faces, stride=EDGE), :].astype(BF16)
    last = count * CELLS
    up[2 * faces :, :] = (src[last - FACE : last, :] * link_of(links, count - 1, 0)).astype(BF16)
    down[2 * faces :, :] = src[0:FACE, :].astype(BF16)


def pack_kernel(links, x, first, second, wide, up, down):
    wide[...] = x[...].astype(F32)
    pack_faces(wide, links, up, down)
    route(links[3, 4], up, down, first, second)


def interior(src, links, weights, out, residual):
    count = src.shape[0] // CELLS
    c_at = lax.broadcasted_iota(jnp.int32, (FACE, EDGE, 128), 1)

    def one(j, carry):
        base = pl.multiple_of(j * CELLS, CELLS)
        rows = src[pl.ds(base, CELLS), :]
        after = jnp.minimum(j + 1, count - 1)
        before = jnp.maximum(j - 1, 0)
        keep_after = jnp.where(j + 1 < count, links[0, j], 0).astype(F32)
        keep_before = jnp.where(j > 0, links[0, before], 0).astype(F32)
        over = src[pl.ds(pl.multiple_of(after * CELLS, CELLS), FACE), :]
        under = src[pl.ds(pl.multiple_of(before * CELLS + CELLS - FACE, FACE), FACE), :]
        over = (over.astype(F32) * keep_after).astype(BF16)
        under = (under.astype(F32) * keep_before).astype(BF16)
        wide = rows.astype(F32)
        planes = wide.reshape(EDGE, EDGE, EDGE, 128)
        none = jnp.zeros((EDGE, 1, EDGE, 128), F32)
        lines = wide.reshape(FACE, EDGE, 128)
        taps = [
            rows,
            jnp.concatenate([rows[FACE:], over], 0),
            jnp.concatenate([under, rows[:-FACE]], 0),
            jnp.concatenate([planes[:, 1:], none], 1).reshape(CELLS, 128).astype(BF16),
            jnp.concatenate([none, planes[:, :-1]], 1).reshape(CELLS, 128).astype(BF16),
            jnp.where(c_at == EDGE - 1, 0.0, pltpu.roll(lines, EDGE - 1, 1))
            .reshape(CELLS, 128)
            .astype(BF16),
            jnp.where(c_at == 0, 0.0, pltpu.roll(lines, 1, 1)).reshape(CELLS, 128).astype(BF16),
        ]
        total = mm(jnp.concatenate(taps, 1), weights[...])
        if residual is not None:
            total = total + residual[pl.ds(base, CELLS), :].astype(F32)
        out[pl.ds(base, CELLS), :] = total
        return carry

    lax.fori_loop(0, count, one, 0)


def first_interior_kernel(links, x, weights, out):
    interior(x, links, weights, out, None)


def second_interior_kernel(links, hidden, x, weights, out):
    interior(hidden, links, weights, out, x)


def add_ghosts(total, from_below, from_above, links, weights):
    count = total.shape[0] // CELLS
    faces = count * FACE
    ch = total.shape[1]

    def tap(k):
        return weights[k * ch : (k + 1) * ch, :]

    b_plus = mm(from_above[0:faces, :], tap(3))
    b_minus = mm(from_below[0:faces, :], tap(4))
    for j in range(count):
        keep = link_of(links, j, 1)
        for a in range(EDGE):
            base = j * CELLS + a * FACE
            at = j * FACE + a * EDGE
            total[base + FACE - EDGE : base + FACE, :] += b_plus[at : at + EDGE, :] * keep
            total[base : base + EDGE, :] += b_minus[at : at + EDGE, :]
    c_plus = mm(from_above[faces : 2 * faces, :], tap(5))
    c_minus = mm(from_below[faces : 2 * faces, :], tap(6))
    for j in range(count):
        at = slice(j * FACE, (j + 1) * FACE)
        total[pl.ds(j * CELLS + EDGE - 1, FACE, stride=EDGE), :] += c_plus[at, :] * link_of(
            links, j, 2
        )
        total[pl.ds(j * CELLS, FACE, stride=EDGE), :] += c_minus[at, :]
    last = count * CELLS
    total[last - FACE : last, :] += mm(from_above[2 * faces :, :], tap(1)) * link_of(
        links, count - 1, 0
    )
    total[0:FACE, :] += mm(from_below[2 * faces :, :], tap(2))


def hidden_kernel(
    links,
    partial,
    first_in,
    second_in,
    weights,
    hidden,
    first,
    second,
    total,
    up,
    down,
    from_below,
    from_above,
):
    total[...] = partial[...]
    route(links[3, 4], first_in, second_in, from_above, from_below)
    add_ghosts(total, from_below, from_above, links, weights)
    total[...] = jnp.maximum(total[...], 0.0)
    hidden[...] = total[...].astype(BF16)
    pack_faces(total, links, up, down)
    route(links[3, 4], up, down, first, second)


def lift_kernel(
    links,
    slots,
    block_levels,
    columns,
    partial,
    first_in,
    second_in,
    weights,
    height,
    out,
    total,
    rows_in,
    sums,
    from_below,
    from_above,
):
    count = partial.shape[0] // CELLS
    faces = count * FACE
    ch = partial.shape[1]
    total[...] = partial[...]
    route(links[3, 4], first_in, second_in, from_above, from_below)
    add_ghosts(total, from_below, from_above, links, weights)
    for c in range(EDGE):
        line = total[pl.ds(c, faces, stride=EDGE), :]
        rows_in[:, c * ch : (c + 1) * ch] = jnp.maximum(line, 0.0).astype(BF16)
    sums[...] = jnp.zeros_like(sums)

    def one(j, carry):
        rows = rows_in[pl.ds(pl.multiple_of(j * FACE, FACE), FACE), :]
        sums[slots[0, j]] += mm(rows, height[block_levels[0, j]])
        return carry

    lax.fori_loop(0, count, one, 0)
    peers = out.shape[0]
    per_peer = sums.shape[0] // peers
    row_at = lax.broadcasted_iota(jnp.int32, (ID_ROWS, out.shape[2]), 0)
    for p in range(peers):
        ids = jnp.zeros(row_at.shape, F32)
        for k in range(per_peer):
            slot = p * per_peer + k
            out[p, k * FACE : (k + 1) * FACE, :] = sums[slot].astype(BF16)
            ids = jnp.where(row_at == k, columns[0, slot].astype(F32), ids)
        out[p, per_peer * FACE :, :] = ids.astype(BF16)


def gather_kernel(links, arrived, bev, first, second, own, total, top, bottom):
    peers, rows, ch = arrived.shape
    per_peer = (rows - ID_ROWS) // FACE
    total[...] = jnp.zeros_like(total)
    for p in range(peers):
        ids = arrived[p, per_peer * FACE :, :].astype(F32)
        for k in range(per_peer):
            column = jnp.max(ids[k : k + 1, :]).astype(jnp.int32)
            row_base = (column // TILE_BC) * (EDGE * COLS) + (column % TILE_BC) * EDGE
            block = arrived[p, k * FACE : (k + 1) * FACE, :].astype(F32)
            for a in range(EDGE):
                at = pl.multiple_of(row_base + a * COLS, EDGE)
                for h, lanes in halves(ch):
                    total[h, pl.ds(at, EDGE), :] += block[a * EDGE : (a + 1) * EDGE, lanes]
    for h, lanes in halves(ch):
        bev[:, lanes] = total[h].astype(BF16)
        top[:, lanes] = total[h, 0 : HALO * COLS, :].astype(BF16)
        bottom[:, lanes] = total[h, (ROWS - HALO) * COLS :, :].astype(BF16)
        for x in range(HALO):
            far = COLS - HALO + x
            own[x, :, lanes] = total[h, pl.ds(x, ROWS, stride=COLS), :].astype(BF16)
            own[HALO + x, :, lanes] = total[h, pl.ds(far, ROWS, stride=COLS), :].astype(BF16)
    route(links[3, 6], bottom, top, first, second)


def halves(channels):
    return [(h, slice(h * LANES, (h + 1) * LANES)) for h in range(channels // LANES)]


WIDE_ROWS = ROWS + 2 * HALO
MID_ROWS = ROWS + HALO
RIM_ROWS = 72
INNER_ROWS = ROWS - 2
CORE_ROWS = ROWS - 4


def tap_columns(weights, dx):
    return jnp.concatenate([weights[dy * 3 + dx] for dy in range(3)], 0)


def three_rows(source, first_row, row_count):
    parts = []
    for dy in range(3):
        at = pl.multiple_of((first_row + dy) * COLS, COLS)
        parts.append(source[pl.ds(at, row_count * COLS), :])
    return jnp.concatenate(parts, 1)


def rows_conv(lhs, weights):
    count = lhs.shape[0]
    x = lax.rem(lax.broadcasted_iota(jnp.int32, (count, weights.shape[2]), 0), COLS)
    from_left = mm(lhs, tap_columns(weights, 0))
    total = jnp.where(x == 0, 0.0, pltpu.roll(from_left, 1, 0))
    total = total + mm(lhs, tap_columns(weights, 1))
    from_right = mm(lhs, tap_columns(weights, 2))
    return total + jnp.where(x == COLS - 1, 0.0, pltpu.roll(from_right, count - 1, 0))


def without_sides(block):
    x = lax.rem(lax.broadcasted_iota(jnp.int32, block.shape, 0), COLS)
    return jnp.where((x == 0) | (x == COLS - 1), 0.0, block)


def first_inner_kernel(bev, weights, inner):
    step = INNER_ROWS // 2

    def one(i, carry):
        block = jnp.maximum(rows_conv(three_rows(bev, i * step, step), weights), 0.0)
        at = pl.multiple_of(i * step * COLS, COLS)
        inner[pl.ds(at, step * COLS), :] = without_sides(block).astype(BF16)
        return carry

    lax.fori_loop(0, INNER_ROWS // step, one, 0)


def strips(upper, lower):
    parts = []
    for source in (upper, lower):
        rows = [source[dy * COLS : (dy + HALO) * COLS] for dy in range(3)]
        parts.append(jnp.concatenate(rows, 1))
    return jnp.concatenate(parts, 0)


def second_core_kernel(
    links,
    inner,
    bev,
    first_row,
    second_row,
    weights_first,
    weights_second,
    middle,
    flanks,
    above,
    below,
):
    ch = bev.shape[1]
    two = HALO * COLS
    step = CORE_ROWS // 4

    def store(block, row):
        count = block.shape[0] // COLS
        at = row * COLS if isinstance(row, int) else pl.multiple_of(row * COLS, COLS)
        middle[pl.ds(at, count * COLS), :] = block.astype(BF16)
        lines = block.reshape(count, COLS, ch)
        for side, x in enumerate((0, COLS - EDGE)):
            flank = lines[:, x : x + EDGE, :].reshape(count * EDGE, ch)
            to = side * ROWS * EDGE + row * EDGE
            to = to if isinstance(row, int) else pl.multiple_of(to, EDGE)
            for h, lanes in halves(ch):
                flanks[h, pl.ds(to, count * EDGE), :] = flank[:, lanes]

    def one(i, carry):
        block = rows_conv(three_rows(inner, i * step, step), weights_second)
        at = pl.multiple_of((i * step + 2) * COLS, COLS)
        store(block + bev[pl.ds(at, step * COLS), :].astype(F32), i * step + 2)
        return carry

    lax.fori_loop(0, CORE_ROWS // step, one, 0)

    route(links[3, 6], first_row, second_row, below, above)
    top, bottom = bev[0:two, :], bev[ROWS * COLS - two :, :]
    high = jnp.concatenate([above[...], top], 0)
    low = jnp.concatenate([bottom, below[...]], 0)
    strip = without_sides(jnp.maximum(rows_conv(strips(high, low), weights_first), 0.0))
    line = lax.broadcasted_iota(jnp.int32, strip.shape, 0) // COLS
    keep = jnp.where(line == 0, links[3, 0], jnp.where(line == 3, links[3, 1], 1)).astype(F32)
    strip = (strip * keep).astype(BF16)

    high = jnp.concatenate([strip[0:two], inner[0:two, :]], 0)
    low = jnp.concatenate([inner[INNER_ROWS * COLS - two :, :], strip[two:]], 0)
    strip = rows_conv(strips(high, low), weights_second)
    store(strip[0:two] + top.astype(F32), 0)
    store(strip[two:] + bottom.astype(F32), ROWS - HALO)


def edges_kernel(
    links,
    middle,
    flanks,
    own_left,
    own_right,
    first_in,
    second_in,
    weights_first,
    weights_second,
    out,
    sides,
    total,
):
    ch = middle.shape[1]
    sides[...] = jnp.zeros_like(sides)

    def place(base, source):
        for x in range(HALO):
            sides[base + x, 0:WIDE_ROWS, :] = source[x, :, :].astype(F32)

    place(2, own_left)
    place(4, own_right)

    @pl.when(links[3, 5] == 0)
    def _():
        place(0, second_in)
        place(6, first_in)

    @pl.when(links[3, 5] != 0)
    def _():
        place(0, first_in)
        place(6, second_in)

    lhs = []
    for start in (0, 1, 4, 5):
        parts = []
        for dy in range(3):
            for dx in range(3):
                parts.append(sides[start + dx, dy : dy + RIM_ROWS, :].astype(BF16))
        lhs.append(jnp.concatenate(parts, 1))
    taps = jnp.concatenate([weights_first[t] for t in range(9)], 0)
    columns = jnp.maximum(mm(jnp.concatenate(lhs, 0), taps), 0.0)
    row_at = lax.broadcasted_iota(jnp.int32, (RIM_ROWS, ch), 0)
    keep = jnp.where(row_at == MID_ROWS - 1, links[3, 1], 1)
    keep = jnp.where(row_at == 0, links[3, 0], keep).astype(F32)
    for k, side_keep in enumerate((links[3, 2], None, None, links[3, 3])):
        block = columns[k * RIM_ROWS : (k + 1) * RIM_ROWS, :] * keep
        if side_keep is not None:
            block = block * side_keep.astype(F32)
        sides[k, 0:RIM_ROWS, :] = block

    column = []
    for k in range(4):
        rows = [sides[k, dy : dy + ROWS, :].astype(BF16) for dy in range(3)]
        column.append(jnp.concatenate(rows, 1))
    w0, w1, w2 = [tap_columns(weights_second, dx) for dx in range(3)]
    added = (
        (0, mm(column[0], w0) + mm(column[1], w1)),
        (1, mm(column[1], w0)),
        (ROWS * EDGE + EDGE - 2, mm(column[2], w2)),
        (ROWS * EDGE + EDGE - 1, mm(column[2], w1) + mm(column[3], w2)),
    )
    total[...] = flanks[...]
    for at, block in added:
        for h, lanes in halves(ch):
            total[h, pl.ds(at, ROWS, stride=EDGE), :] += block[:, lanes]
    for y in range(ROWS):
        at = y * COLS
        out[at + EDGE : at + COLS - EDGE, :] = middle[at + EDGE : at + COLS - EDGE, :]
        for side, x in enumerate((0, COLS - EDGE)):
            group = side * ROWS * EDGE + y * EDGE
            for h, lanes in halves(ch):
                out[at + x : at + x + EDGE, lanes] = total[h, group : group + EDGE, :].astype(BF16)


def call(kernel, out_shape, scalars, arrays, scratch=(), mib=12):
    multiple = isinstance(out_shape, (list, tuple))
    return pl.pallas_call(
        kernel,
        out_shape=out_shape,
        in_specs=[SMEM] * len(scalars) + [VMEM] * len(arrays),
        out_specs=[VMEM] * len(out_shape) if multiple else VMEM,
        scratch_shapes=list(scratch),
        compiler_params=pltpu.CompilerParams(vmem_limit_bytes=mib << 20),
    )(*scalars, *arrays)


def local(
    features,
    links,
    block_slot,
    block_level,
    slot_column,
    conv_first,
    conv_second,
    height_w,
    plane_first,
    plane_second,
):
    count, _, ch = features.shape
    rows = count * CELLS
    faces = (2 * count + 1) * FACE
    mapped = plane_first.shape[3]
    peers = lax.axis_size("gx")
    slot_total = slot_column.shape[1]
    per_peer = slot_total // peers
    x = features.reshape(rows, ch)
    w_first = conv_first.reshape(-1, ch)
    w_second = conv_second.reshape(-1, ch)
    k_first = plane_first.reshape(9, mapped, mapped)
    k_second = plane_second.reshape(9, mapped, mapped)
    slots = block_slot.reshape(1, count)
    block_levels = block_level.reshape(1, count)
    both = ("gy", "gx")

    face_shape = jax.ShapeDtypeStruct((faces, ch), BF16)
    wide = pltpu.VMEM((rows, ch), F32)
    part_shape = jax.ShapeDtypeStruct((rows, ch), F32)

    gy, gx = lax.axis_index("gy"), lax.axis_index("gx")
    last_y = lax.axis_size("gy") - 1
    places = [gy > 0, gy < last_y, gx > 0, gx < peers - 1, lax.axis_index(both) % 2, gx % 2, gy % 2]
    lane = lax.broadcasted_iota(jnp.int32, (1, count), 1)
    flags = sum(jnp.where(lane == k, jnp.int32(v), 0) for k, v in enumerate(places))
    links = jnp.concatenate([links.T, flags], 0)
    face = pltpu.VMEM((faces, ch), BF16)
    first, second = call(pack_kernel, (face_shape, face_shape), (links,), (x,), (wide, face, face))
    first, second = swap(first, second, both)
    partial = call(first_interior_kernel, part_shape, (links,), (x, w_first))
    hidden, first, second = call(
        hidden_kernel,
        (jax.ShapeDtypeStruct((rows, ch), BF16), face_shape, face_shape),
        (links,),
        (partial, first, second, w_first),
        (wide, face, face, face, face),
    )
    first, second = swap(first, second, both)
    partial = call(second_interior_kernel, part_shape, (links,), (hidden, x, w_second))
    outgoing = call(
        lift_kernel,
        jax.ShapeDtypeStruct((peers, per_peer * FACE + ID_ROWS, mapped), BF16),
        (links, slots, block_levels, slot_column),
        (partial, first, second, w_second, height_w),
        (
            wide,
            pltpu.VMEM((count * FACE, EDGE * ch), BF16),
            pltpu.VMEM((slot_total, FACE, mapped), F32),
            face,
            face,
        ),
    )
    arrived = lax.all_to_all(outgoing, "gx", split_axis=0, concat_axis=0, tiled=True)

    row_shape = jax.ShapeDtypeStruct((HALO * COLS, mapped), BF16)
    row = pltpu.VMEM((HALO * COLS, mapped), BF16)
    bev, first, second, own = call(
        gather_kernel,
        (
            jax.ShapeDtypeStruct((ROWS * COLS, mapped), BF16),
            row_shape,
            row_shape,
            jax.ShapeDtypeStruct((2 * HALO, ROWS, mapped), BF16),
        ),
        (links,),
        (arrived,),
        (pltpu.VMEM((mapped // LANES, ROWS * COLS, LANES), F32), row, row),
    )
    first_row, second_row = swap(first, second, "gy")
    inner = call(
        first_inner_kernel,
        jax.ShapeDtypeStruct((INNER_ROWS * COLS, mapped), BF16),
        (),
        (bev, k_first),
    )
    first_row, second_row, inner = lax.optimization_barrier((first_row, second_row, inner))
    odd_y, odd_x = gy % 2 == 1, gx % 2 == 1
    corner_above = jnp.where(odd_y, first_row, second_row).reshape(HALO, COLS, mapped)
    corner_below = jnp.where(odd_y, second_row, first_row).reshape(HALO, COLS, mapped)

    def side(own, at):
        return jnp.concatenate(
            [
                corner_above[:, at : at + HALO].transpose(1, 0, 2),
                own,
                corner_below[:, at : at + HALO].transpose(1, 0, 2),
            ],
            1,
        )

    own_left, own_right = side(own[:HALO], 0), side(own[HALO:], COLS - HALO)
    first, second = swap(
        jnp.where(odd_x, own_left, own_right), jnp.where(odd_x, own_right, own_left), "gx"
    )
    middle, flanks = call(
        second_core_kernel,
        (
            jax.ShapeDtypeStruct((ROWS * COLS, mapped), BF16),
            jax.ShapeDtypeStruct((mapped // LANES, 2 * ROWS * EDGE, LANES), F32),
        ),
        (links,),
        (inner, bev, first_row, second_row, k_first, k_second),
        (row, row),
    )
    out = call(
        edges_kernel,
        jax.ShapeDtypeStruct((ROWS * COLS, mapped), BF16),
        (links,),
        (middle, flanks, own_left, own_right, first, second, k_first, k_second),
        (
            pltpu.VMEM((8, RIM_ROWS + EDGE, mapped), F32),
            pltpu.VMEM((mapped // LANES, 2 * ROWS * EDGE, LANES), F32),
        ),
    )
    return out.reshape(ROWS, COLS, mapped)


def solution(mesh):
    in_specs = (
        P(("gy", "gx"), None, None),
        P(("gy", "gx"), None),
        P(("gy", "gx")),
        P(("gy", "gx")),
        P(("gy", "gx"), None),
        P(),
        P(),
        P(),
        P(),
        P(),
    )
    out_specs = P("gy", "gx", None)

    return jax.shard_map(local, mesh=mesh, in_specs=in_specs, out_specs=out_specs, check_vma=False)
```

```python
import jax
import jax.numpy as jnp
from jax import lax
from jax.experimental import pallas as pl
from jax.experimental.pallas import tpu as pltpu
from jax.sharding import PartitionSpec as P


EDGE = 8
FACE = EDGE * EDGE
CELLS = EDGE * FACE
TILE_BR = 8
TILE_BC = 4
ROWS = TILE_BR * EDGE
COLS = TILE_BC * EDGE
HALO = 2
ID_ROWS = 8
LANES = 128
F32 = jnp.float32
BF16 = jnp.bfloat16

VMEM = pl.BlockSpec(memory_space=pltpu.VMEM)
SMEM = pl.BlockSpec(memory_space=pltpu.SMEM)


def swap(first, second, axis):
    count = lax.axis_size(axis)
    near = [(i, i ^ 1) for i in range(count) if i ^ 1 < count]
    far = [(i, i + 1 if i % 2 else i - 1) for i in range(1, count)]
    far = [(i, k) for i, k in far if k < count]
    first = lax.ppermute(first, axis, near)
    second = lax.ppermute(second, axis, far)
    return first, second


def trade_order(count):
    assert count & (count - 1) == 0
    return [*range(count // 2, count), *range(1, count // 2)]


def route(odd, up, down, first, second):
    @pl.when(odd == 0)
    def _():
        first[...] = up[...]
        second[...] = down[...]

    @pl.when(odd != 0)
    def _():
        first[...] = down[...]
        second[...] = up[...]


def mm(a, b):
    return jnp.dot(a, b, preferred_element_type=F32)


def link_of(links, block, axis):
    return links[axis, block].astype(F32)


def pack_faces(src, links, up, down):
    count = src.shape[0] // CELLS
    faces = count * FACE
    upper_b, lower_b = [], []
    for j in range(count):
        keep = link_of(links, j, 1)
        for a in range(EDGE):
            base = j * CELLS + a * FACE
            upper_b.append(src[base + FACE - EDGE : base + FACE, :] * keep)
            lower_b.append(src[base : base + EDGE, :])
    up[0:faces, :] = jnp.concatenate(upper_b, 0).astype(BF16)
    down[0:faces, :] = jnp.concatenate(lower_b, 0).astype(BF16)
    upper_c = []
    for j in range(count):
        upper_c.append(
            src[pl.ds(j * CELLS + EDGE - 1, FACE, stride=EDGE), :] * link_of(links, j, 2)
        )
    up[faces : 2 * faces, :] = jnp.concatenate(upper_c, 0).astype(BF16)
    down[faces : 2 * faces, :] = src[pl.ds(0, faces, stride=EDGE), :].astype(BF16)
    last = count * CELLS
    up[2 * faces :, :] = (src[last - FACE : last, :] * link_of(links, count - 1, 0)).astype(BF16)
    down[2 * faces :, :] = src[0:FACE, :].astype(BF16)


def pack_kernel(links, x, first, second, wide, up, down):
    wide[...] = x[...].astype(F32)
    pack_faces(wide, links, up, down)
    route(links[3, 4], up, down, first, second)


def interior(src, links, weights, out, residual):
    count = src.shape[0] // CELLS
    c_at = lax.broadcasted_iota(jnp.int32, (FACE, EDGE, 128), 1)

    def one(j, carry):
        base = pl.multiple_of(j * CELLS, CELLS)
        rows = src[pl.ds(base, CELLS), :]
        after = jnp.minimum(j + 1, count - 1)
        before = jnp.maximum(j - 1, 0)
        keep_after = jnp.where(j + 1 < count, links[0, j], 0).astype(F32)
        keep_before = jnp.where(j > 0, links[0, before], 0).astype(F32)
        over = src[pl.ds(pl.multiple_of(after * CELLS, CELLS), FACE), :]
        under = src[pl.ds(pl.multiple_of(before * CELLS + CELLS - FACE, FACE), FACE), :]
        over = (over.astype(F32) * keep_after).astype(BF16)
        under = (under.astype(F32) * keep_before).astype(BF16)
        wide = rows.astype(F32)
        planes = wide.reshape(EDGE, EDGE, EDGE, 128)
        none = jnp.zeros((EDGE, 1, EDGE, 128), F32)
        lines = wide.reshape(FACE, EDGE, 128)
        taps = [
            rows,
            jnp.concatenate([rows[FACE:], over], 0),
            jnp.concatenate([under, rows[:-FACE]], 0),
            jnp.concatenate([planes[:, 1:], none], 1).reshape(CELLS, 128).astype(BF16),
            jnp.concatenate([none, planes[:, :-1]], 1).reshape(CELLS, 128).astype(BF16),
            jnp.where(c_at == EDGE - 1, 0.0, pltpu.roll(lines, EDGE - 1, 1))
            .reshape(CELLS, 128)
            .astype(BF16),
            jnp.where(c_at == 0, 0.0, pltpu.roll(lines, 1, 1)).reshape(CELLS, 128).astype(BF16),
        ]
        total = mm(jnp.concatenate(taps, 1), weights[...])
        if residual is not None:
            total = total + residual[pl.ds(base, CELLS), :].astype(F32)
        out[pl.ds(base, CELLS), :] = total
        return carry

    lax.fori_loop(0, count, one, 0)


def first_interior_kernel(links, x, weights, out):
    interior(x, links, weights, out, None)


def second_interior_kernel(links, hidden, x, weights, out):
    interior(hidden, links, weights, out, x)


def add_ghosts(total, from_below, from_above, links, weights):
    count = total.shape[0] // CELLS
    faces = count * FACE
    ch = total.shape[1]

    def tap(k):
        return weights[k * ch : (k + 1) * ch, :]

    b_plus = mm(from_above[0:faces, :], tap(3))
    b_minus = mm(from_below[0:faces, :], tap(4))
    for j in range(count):
        keep = link_of(links, j, 1)
        for a in range(EDGE):
            base = j * CELLS + a * FACE
            at = j * FACE + a * EDGE
            total[base + FACE - EDGE : base + FACE, :] += b_plus[at : at + EDGE, :] * keep
            total[base : base + EDGE, :] += b_minus[at : at + EDGE, :]
    c_plus = mm(from_above[faces : 2 * faces, :], tap(5))
    c_minus = mm(from_below[faces : 2 * faces, :], tap(6))
    for j in range(count):
        at = slice(j * FACE, (j + 1) * FACE)
        total[pl.ds(j * CELLS + EDGE - 1, FACE, stride=EDGE), :] += c_plus[at, :] * link_of(
            links, j, 2
        )
        total[pl.ds(j * CELLS, FACE, stride=EDGE), :] += c_minus[at, :]
    last = count * CELLS
    total[last - FACE : last, :] += mm(from_above[2 * faces :, :], tap(1)) * link_of(
        links, count - 1, 0
    )
    total[0:FACE, :] += mm(from_below[2 * faces :, :], tap(2))


def hidden_kernel(
    links,
    partial,
    first_in,
    second_in,
    weights,
    hidden,
    first,
    second,
    total,
    up,
    down,
    from_below,
    from_above,
):
    total[...] = partial[...]
    route(links[3, 4], first_in, second_in, from_above, from_below)
    add_ghosts(total, from_below, from_above, links, weights)
    total[...] = jnp.maximum(total[...], 0.0)
    hidden[...] = total[...].astype(BF16)
    pack_faces(total, links, up, down)
    route(links[3, 4], up, down, first, second)


def lift_kernel(
    links,
    slots,
    block_levels,
    columns,
    partial,
    first_in,
    second_in,
    weights,
    height,
    *refs,
):
    *outs, total, rows_in, sums, from_below, from_above = refs
    count = partial.shape[0] // CELLS
    faces = count * FACE
    ch = partial.shape[1]
    total[...] = partial[...]
    route(links[3, 4], first_in, second_in, from_above, from_below)
    add_ghosts(total, from_below, from_above, links, weights)
    for c in range(EDGE):
        line = total[pl.ds(c, faces, stride=EDGE), :]
        rows_in[:, c * ch : (c + 1) * ch] = jnp.maximum(line, 0.0).astype(BF16)
    sums[...] = jnp.zeros_like(sums)

    def one(j, carry):
        rows = rows_in[pl.ds(pl.multiple_of(j * FACE, FACE), FACE), :]
        sums[slots[0, j]] += mm(rows, height[block_levels[0, j]])
        return carry

    lax.fori_loop(0, count, one, 0)
    peers = len(outs)
    per_peer = sums.shape[0] // peers
    row_at = lax.broadcasted_iota(jnp.int32, (ID_ROWS, LANES), 0)
    for k, out in enumerate(outs):
        ids = jnp.zeros(row_at.shape, F32)
        for i in range(per_peer):
            slot = (links[3, 7] ^ k) * per_peer + i
            block = sums[slot].astype(BF16)
            for h, lanes in halves(block.shape[1]):
                at = (h * per_peer + i) * FACE
                out[at : at + FACE, :] = block[:, lanes]
            ids = jnp.where(row_at == i, columns[0, slot].astype(F32), ids)
        out[out.shape[0] - ID_ROWS :, :] = ids.astype(BF16)


def gather_kernel(links, *refs):
    *arrived, bev, first, second, own, total, top, bottom = refs
    ch = bev.shape[1]
    parts = ch // LANES
    per_peer = (arrived[0].shape[0] - ID_ROWS) // (parts * FACE)
    total[...] = jnp.zeros_like(total)
    for source in arrived:
        ids = source[source.shape[0] - ID_ROWS :, :].astype(F32)
        for k in range(per_peer):
            column = jnp.max(ids[k : k + 1, :]).astype(jnp.int32)
            row_base = (column // TILE_BC) * (EDGE * COLS) + (column % TILE_BC) * EDGE
            for h in range(parts):
                start = (h * per_peer + k) * FACE
                block = source[start : start + FACE, :].astype(F32)
                for a in range(EDGE):
                    at = pl.multiple_of(row_base + a * COLS, EDGE)
                    total[h, pl.ds(at, EDGE), :] += block[a * EDGE : (a + 1) * EDGE, :]
    for h, lanes in halves(ch):
        bev[:, lanes] = total[h].astype(BF16)
        top[:, lanes] = total[h, 0 : HALO * COLS, :].astype(BF16)
        bottom[:, lanes] = total[h, (ROWS - HALO) * COLS :, :].astype(BF16)
        for x in range(HALO):
            far = COLS - HALO + x
            own[x, :, lanes] = total[h, pl.ds(x, ROWS, stride=COLS), :].astype(BF16)
            own[HALO + x, :, lanes] = total[h, pl.ds(far, ROWS, stride=COLS), :].astype(BF16)
    route(links[3, 6], bottom, top, first, second)


def halves(channels):
    return [(h, slice(h * LANES, (h + 1) * LANES)) for h in range(channels // LANES)]


WIDE_ROWS = ROWS + 2 * HALO
MID_ROWS = ROWS + HALO
RIM_ROWS = 72
INNER_ROWS = ROWS - 2
CORE_ROWS = ROWS - 4


def tap_columns(weights, dx):
    return jnp.concatenate([weights[dy * 3 + dx] for dy in range(3)], 0)


def three_rows(source, first_row, row_count):
    parts = []
    for dy in range(3):
        at = pl.multiple_of((first_row + dy) * COLS, COLS)
        parts.append(source[pl.ds(at, row_count * COLS), :])
    return jnp.concatenate(parts, 1)


def rows_conv(lhs, weights):
    count = lhs.shape[0]
    x = lax.rem(lax.broadcasted_iota(jnp.int32, (count, weights.shape[2]), 0), COLS)
    from_left = mm(lhs, tap_columns(weights, 0))
    total = jnp.where(x == 0, 0.0, pltpu.roll(from_left, 1, 0))
    total = total + mm(lhs, tap_columns(weights, 1))
    from_right = mm(lhs, tap_columns(weights, 2))
    return total + jnp.where(x == COLS - 1, 0.0, pltpu.roll(from_right, count - 1, 0))


def without_sides(block):
    x = lax.rem(lax.broadcasted_iota(jnp.int32, block.shape, 0), COLS)
    return jnp.where((x == 0) | (x == COLS - 1), 0.0, block)


def first_inner_kernel(bev, weights, inner):
    step = INNER_ROWS // 2

    def one(i, carry):
        block = jnp.maximum(rows_conv(three_rows(bev, i * step, step), weights), 0.0)
        at = pl.multiple_of(i * step * COLS, COLS)
        inner[pl.ds(at, step * COLS), :] = without_sides(block).astype(BF16)
        return carry

    lax.fori_loop(0, INNER_ROWS // step, one, 0)


def strips(upper, lower):
    parts = []
    for source in (upper, lower):
        rows = [source[dy * COLS : (dy + HALO) * COLS] for dy in range(3)]
        parts.append(jnp.concatenate(rows, 1))
    return jnp.concatenate(parts, 0)


def second_core_kernel(
    links,
    inner,
    bev,
    first_row,
    second_row,
    weights_first,
    weights_second,
    middle,
    flanks,
    above,
    below,
):
    ch = bev.shape[1]
    two = HALO * COLS
    step = CORE_ROWS // 4

    def store(block, row):
        count = block.shape[0] // COLS
        at = row * COLS if isinstance(row, int) else pl.multiple_of(row * COLS, COLS)
        middle[pl.ds(at, count * COLS), :] = block.astype(BF16)
        lines = block.reshape(count, COLS, ch)
        for side, x in enumerate((0, COLS - EDGE)):
            flank = lines[:, x : x + EDGE, :].reshape(count * EDGE, ch)
            to = side * ROWS * EDGE + row * EDGE
            to = to if isinstance(row, int) else pl.multiple_of(to, EDGE)
            for h, lanes in halves(ch):
                flanks[h, pl.ds(to, count * EDGE), :] = flank[:, lanes]

    def one(i, carry):
        block = rows_conv(three_rows(inner, i * step, step), weights_second)
        at = pl.multiple_of((i * step + 2) * COLS, COLS)
        store(block + bev[pl.ds(at, step * COLS), :].astype(F32), i * step + 2)
        return carry

    lax.fori_loop(0, CORE_ROWS // step, one, 0)

    route(links[3, 6], first_row, second_row, below, above)
    top, bottom = bev[0:two, :], bev[ROWS * COLS - two :, :]
    high = jnp.concatenate([above[...], top], 0)
    low = jnp.concatenate([bottom, below[...]], 0)
    strip = without_sides(jnp.maximum(rows_conv(strips(high, low), weights_first), 0.0))
    line = lax.broadcasted_iota(jnp.int32, strip.shape, 0) // COLS
    keep = jnp.where(line == 0, links[3, 0], jnp.where(line == 3, links[3, 1], 1)).astype(F32)
    strip = (strip * keep).astype(BF16)

    high = jnp.concatenate([strip[0:two], inner[0:two, :]], 0)
    low = jnp.concatenate([inner[INNER_ROWS * COLS - two :, :], strip[two:]], 0)
    strip = rows_conv(strips(high, low), weights_second)
    store(strip[0:two] + top.astype(F32), 0)
    store(strip[two:] + bottom.astype(F32), ROWS - HALO)


def edges_kernel(
    links,
    middle,
    flanks,
    own_left,
    own_right,
    first_in,
    second_in,
    weights_first,
    weights_second,
    out,
    sides,
    total,
):
    ch = middle.shape[1]
    sides[...] = jnp.zeros_like(sides)

    def place(base, source):
        for x in range(HALO):
            sides[base + x, 0:WIDE_ROWS, :] = source[x, :, :].astype(F32)

    place(2, own_left)
    place(4, own_right)

    @pl.when(links[3, 5] == 0)
    def _():
        place(0, second_in)
        place(6, first_in)

    @pl.when(links[3, 5] != 0)
    def _():
        place(0, first_in)
        place(6, second_in)

    lhs = []
    for start in (0, 1, 4, 5):
        parts = []
        for dy in range(3):
            for dx in range(3):
                parts.append(sides[start + dx, dy : dy + RIM_ROWS, :].astype(BF16))
        lhs.append(jnp.concatenate(parts, 1))
    taps = jnp.concatenate([weights_first[t] for t in range(9)], 0)
    columns = jnp.maximum(mm(jnp.concatenate(lhs, 0), taps), 0.0)
    row_at = lax.broadcasted_iota(jnp.int32, (RIM_ROWS, ch), 0)
    keep = jnp.where(row_at == MID_ROWS - 1, links[3, 1], 1)
    keep = jnp.where(row_at == 0, links[3, 0], keep).astype(F32)
    for k, side_keep in enumerate((links[3, 2], None, None, links[3, 3])):
        block = columns[k * RIM_ROWS : (k + 1) * RIM_ROWS, :] * keep
        if side_keep is not None:
            block = block * side_keep.astype(F32)
        sides[k, 0:RIM_ROWS, :] = block

    column = []
    for k in range(4):
        rows = [sides[k, dy : dy + ROWS, :].astype(BF16) for dy in range(3)]
        column.append(jnp.concatenate(rows, 1))
    w0, w1, w2 = [tap_columns(weights_second, dx) for dx in range(3)]
    added = (
        (0, mm(column[0], w0) + mm(column[1], w1)),
        (1, mm(column[1], w0)),
        (ROWS * EDGE + EDGE - 2, mm(column[2], w2)),
        (ROWS * EDGE + EDGE - 1, mm(column[2], w1) + mm(column[3], w2)),
    )
    total[...] = flanks[...]
    for at, block in added:
        for h, lanes in halves(ch):
            total[h, pl.ds(at, ROWS, stride=EDGE), :] += block[:, lanes]
    for y in range(ROWS):
        at = y * COLS
        out[at + EDGE : at + COLS - EDGE, :] = middle[at + EDGE : at + COLS - EDGE, :]
        for side, x in enumerate((0, COLS - EDGE)):
            group = side * ROWS * EDGE + y * EDGE
            for h, lanes in halves(ch):
                out[at + x : at + x + EDGE, lanes] = total[h, group : group + EDGE, :].astype(BF16)


def call(kernel, out_shape, scalars, arrays, scratch=(), mib=12):
    multiple = isinstance(out_shape, (list, tuple))
    return pl.pallas_call(
        kernel,
        out_shape=out_shape,
        in_specs=[SMEM] * len(scalars) + [VMEM] * len(arrays),
        out_specs=[VMEM] * len(out_shape) if multiple else VMEM,
        scratch_shapes=list(scratch),
        compiler_params=pltpu.CompilerParams(vmem_limit_bytes=mib << 20),
    )(*scalars, *arrays)


def local(
    features,
    links,
    block_slot,
    block_level,
    slot_column,
    conv_first,
    conv_second,
    height_w,
    plane_first,
    plane_second,
):
    count, _, ch = features.shape
    rows = count * CELLS
    faces = (2 * count + 1) * FACE
    mapped = plane_first.shape[3]
    peers = lax.axis_size("gx")
    slot_total = slot_column.shape[1]
    per_peer = slot_total // peers
    x = features.reshape(rows, ch)
    w_first = conv_first.reshape(-1, ch)
    w_second = conv_second.reshape(-1, ch)
    k_first = plane_first.reshape(9, mapped, mapped)
    k_second = plane_second.reshape(9, mapped, mapped)
    slots = block_slot.reshape(1, count)
    block_levels = block_level.reshape(1, count)
    both = ("gy", "gx")

    face_shape = jax.ShapeDtypeStruct((faces, ch), BF16)
    wide = pltpu.VMEM((rows, ch), F32)
    part_shape = jax.ShapeDtypeStruct((rows, ch), F32)

    gy, gx = lax.axis_index("gy"), lax.axis_index("gx")
    last_y = lax.axis_size("gy") - 1
    places = [gy > 0, gy < last_y, gx > 0, gx < peers - 1, lax.axis_index(both) % 2, gx % 2, gy % 2, gx]
    lane = lax.broadcasted_iota(jnp.int32, (1, count), 1)
    flags = sum(jnp.where(lane == k, jnp.int32(v), 0) for k, v in enumerate(places))
    links = jnp.concatenate([links.T, flags], 0)
    face = pltpu.VMEM((faces, ch), BF16)
    first, second = call(pack_kernel, (face_shape, face_shape), (links,), (x,), (wide, face, face))
    first, second = swap(first, second, both)
    partial = call(first_interior_kernel, part_shape, (links,), (x, w_first))
    hidden, first, second = call(
        hidden_kernel,
        (jax.ShapeDtypeStruct((rows, ch), BF16), face_shape, face_shape),
        (links,),
        (partial, first, second, w_first),
        (wide, face, face, face, face),
    )
    first, second = swap(first, second, both)
    partial = call(second_interior_kernel, part_shape, (links,), (hidden, x, w_second))
    payload = (mapped // LANES * per_peer * FACE + ID_ROWS, LANES)
    outgoing = call(
        lift_kernel,
        [jax.ShapeDtypeStruct(payload, BF16)] * peers,
        (links, slots, block_levels, slot_column),
        (partial, first, second, w_second, height_w),
        (
            wide,
            pltpu.VMEM((count * FACE, EDGE * ch), BF16),
            pltpu.VMEM((slot_total, FACE, mapped), F32),
            face,
            face,
        ),
    )
    arrived = list(outgoing)
    for k in trade_order(peers):
        arrived[k] = lax.ppermute(outgoing[k], "gx", [(i, i ^ k) for i in range(peers)])

    row_shape = jax.ShapeDtypeStruct((HALO * COLS, mapped), BF16)
    row = pltpu.VMEM((HALO * COLS, mapped), BF16)
    bev, first, second, own = call(
        gather_kernel,
        (
            jax.ShapeDtypeStruct((ROWS * COLS, mapped), BF16),
            row_shape,
            row_shape,
            jax.ShapeDtypeStruct((2 * HALO, ROWS, mapped), BF16),
        ),
        (links,),
        arrived,
        (pltpu.VMEM((mapped // LANES, ROWS * COLS, LANES), F32), row, row),
    )
    first_row, second_row = swap(first, second, "gy")
    inner = call(
        first_inner_kernel,
        jax.ShapeDtypeStruct((INNER_ROWS * COLS, mapped), BF16),
        (),
        (bev, k_first),
    )
    first_row, second_row, inner = lax.optimization_barrier((first_row, second_row, inner))
    odd_y, odd_x = gy % 2 == 1, gx % 2 == 1
    corner_above = jnp.where(odd_y, first_row, second_row).reshape(HALO, COLS, mapped)
    corner_below = jnp.where(odd_y, second_row, first_row).reshape(HALO, COLS, mapped)

    def side(own, at):
        return jnp.concatenate(
            [
                corner_above[:, at : at + HALO].transpose(1, 0, 2),
                own,
                corner_below[:, at : at + HALO].transpose(1, 0, 2),
            ],
            1,
        )

    own_left, own_right = side(own[:HALO], 0), side(own[HALO:], COLS - HALO)
    first, second = swap(
        jnp.where(odd_x, own_left, own_right), jnp.where(odd_x, own_right, own_left), "gx"
    )
    middle, flanks = call(
        second_core_kernel,
        (
            jax.ShapeDtypeStruct((ROWS * COLS, mapped), BF16),
            jax.ShapeDtypeStruct((mapped // LANES, 2 * ROWS * EDGE, LANES), F32),
        ),
        (links,),
        (inner, bev, first_row, second_row, k_first, k_second),
        (row, row),
    )
    out = call(
        edges_kernel,
        jax.ShapeDtypeStruct((ROWS * COLS, mapped), BF16),
        (links,),
        (middle, flanks, own_left, own_right, first, second, k_first, k_second),
        (
            pltpu.VMEM((8, RIM_ROWS + EDGE, mapped), F32),
            pltpu.VMEM((mapped // LANES, 2 * ROWS * EDGE, LANES), F32),
        ),
    )
    return out.reshape(ROWS, COLS, mapped)


def solution(mesh):
    in_specs = (
        P(("gy", "gx"), None, None),
        P(("gy", "gx"), None),
        P(("gy", "gx")),
        P(("gy", "gx")),
        P(("gy", "gx"), None),
        P(),
        P(),
        P(),
        P(),
        P(),
    )
    out_specs = P("gy", "gx", None)

    return jax.shard_map(local, mesh=mesh, in_specs=in_specs, out_specs=out_specs, check_vma=False)
```

```python
import jax
import jax.numpy as jnp
from jax import lax
from jax.experimental import pallas as pl
from jax.experimental.pallas import tpu as pltpu
from jax.sharding import PartitionSpec as P


EDGE = 8
FACE = EDGE * EDGE
CELLS = EDGE * FACE
TILE_BR = 8
TILE_BC = 4
ROWS = TILE_BR * EDGE
COLS = TILE_BC * EDGE
HALO = 2
ID_ROWS = 8
LANES = 128
F32 = jnp.float32
BF16 = jnp.bfloat16

VMEM = pl.BlockSpec(memory_space=pltpu.VMEM)
SMEM = pl.BlockSpec(memory_space=pltpu.SMEM)
ANY = pl.BlockSpec(memory_space=pl.ANY)


def swap(first, second, axis):
    count = lax.axis_size(axis)
    near = [(i, i ^ 1) for i in range(count) if i ^ 1 < count]
    far = [(i, i + 1 if i % 2 else i - 1) for i in range(1, count)]
    far = [(i, k) for i, k in far if k < count]
    first = lax.ppermute(first, axis, near)
    second = lax.ppermute(second, axis, far)
    return first, second


def trade_order(count):
    assert count & (count - 1) == 0
    return [*range(count // 2, count), *range(1, count // 2)]


def route(odd, up, down, first, second):
    @pl.when(odd == 0)
    def _():
        first[...] = up[...]
        second[...] = down[...]

    @pl.when(odd != 0)
    def _():
        first[...] = down[...]
        second[...] = up[...]


def mm(a, b):
    return jnp.dot(a, b, preferred_element_type=F32)


def link_of(links, block, axis):
    return links[axis, block].astype(F32)


def pack_faces(src, links, up, down):
    count = src.shape[0] // CELLS
    faces = count * FACE
    upper_b, lower_b = [], []
    for j in range(count):
        keep = link_of(links, j, 1)
        for a in range(EDGE):
            base = j * CELLS + a * FACE
            upper_b.append(src[base + FACE - EDGE : base + FACE, :] * keep)
            lower_b.append(src[base : base + EDGE, :])
    up[0:faces, :] = jnp.concatenate(upper_b, 0).astype(BF16)
    down[0:faces, :] = jnp.concatenate(lower_b, 0).astype(BF16)
    upper_c = []
    for j in range(count):
        upper_c.append(
            src[pl.ds(j * CELLS + EDGE - 1, FACE, stride=EDGE), :] * link_of(links, j, 2)
        )
    up[faces : 2 * faces, :] = jnp.concatenate(upper_c, 0).astype(BF16)
    down[faces : 2 * faces, :] = src[pl.ds(0, faces, stride=EDGE), :].astype(BF16)
    last = count * CELLS
    up[2 * faces :, :] = (src[last - FACE : last, :] * link_of(links, count - 1, 0)).astype(BF16)
    down[2 * faces :, :] = src[0:FACE, :].astype(BF16)


def pack_kernel(links, x, first, second, wide, up, down):
    wide[...] = x[...].astype(F32)
    pack_faces(wide, links, up, down)
    route(links[3, 4], up, down, first, second)


def interior(src, links, weights, out, residual):
    count = src.shape[0] // CELLS
    c_at = lax.broadcasted_iota(jnp.int32, (FACE, EDGE, 128), 1)

    def one(j, carry):
        base = pl.multiple_of(j * CELLS, CELLS)
        rows = src[pl.ds(base, CELLS), :]
        after = jnp.minimum(j + 1, count - 1)
        before = jnp.maximum(j - 1, 0)
        keep_after = jnp.where(j + 1 < count, links[0, j], 0).astype(F32)
        keep_before = jnp.where(j > 0, links[0, before], 0).astype(F32)
        over = src[pl.ds(pl.multiple_of(after * CELLS, CELLS), FACE), :]
        under = src[pl.ds(pl.multiple_of(before * CELLS + CELLS - FACE, FACE), FACE), :]
        over = (over.astype(F32) * keep_after).astype(BF16)
        under = (under.astype(F32) * keep_before).astype(BF16)
        wide = rows.astype(F32)
        planes = wide.reshape(EDGE, EDGE, EDGE, 128)
        none = jnp.zeros((EDGE, 1, EDGE, 128), F32)
        lines = wide.reshape(FACE, EDGE, 128)
        taps = [
            rows,
            jnp.concatenate([rows[FACE:], over], 0),
            jnp.concatenate([under, rows[:-FACE]], 0),
            jnp.concatenate([planes[:, 1:], none], 1).reshape(CELLS, 128).astype(BF16),
            jnp.concatenate([none, planes[:, :-1]], 1).reshape(CELLS, 128).astype(BF16),
            jnp.where(c_at == EDGE - 1, 0.0, pltpu.roll(lines, EDGE - 1, 1))
            .reshape(CELLS, 128)
            .astype(BF16),
            jnp.where(c_at == 0, 0.0, pltpu.roll(lines, 1, 1)).reshape(CELLS, 128).astype(BF16),
        ]
        total = mm(jnp.concatenate(taps, 1), weights[...])
        if residual is not None:
            total = total + residual[pl.ds(base, CELLS), :].astype(F32)
        out[pl.ds(base, CELLS), :] = total
        return carry

    lax.fori_loop(0, count, one, 0)


def first_interior_kernel(links, x, weights, out):
    interior(x, links, weights, out, None)


def second_interior_kernel(links, hidden, x, weights, out):
    interior(hidden, links, weights, out, x)


def add_ghosts(total, from_below, from_above, links, weights):
    count = total.shape[0] // CELLS
    faces = count * FACE
    ch = total.shape[1]

    def tap(k):
        return weights[k * ch : (k + 1) * ch, :]

    b_plus = mm(from_above[0:faces, :], tap(3))
    b_minus = mm(from_below[0:faces, :], tap(4))
    for j in range(count):
        keep = link_of(links, j, 1)
        for a in range(EDGE):
            base = j * CELLS + a * FACE
            at = j * FACE + a * EDGE
            total[base + FACE - EDGE : base + FACE, :] += b_plus[at : at + EDGE, :] * keep
            total[base : base + EDGE, :] += b_minus[at : at + EDGE, :]
    c_plus = mm(from_above[faces : 2 * faces, :], tap(5))
    c_minus = mm(from_below[faces : 2 * faces, :], tap(6))
    for j in range(count):
        at = slice(j * FACE, (j + 1) * FACE)
        total[pl.ds(j * CELLS + EDGE - 1, FACE, stride=EDGE), :] += c_plus[at, :] * link_of(
            links, j, 2
        )
        total[pl.ds(j * CELLS, FACE, stride=EDGE), :] += c_minus[at, :]
    last = count * CELLS
    total[last - FACE : last, :] += mm(from_above[2 * faces :, :], tap(1)) * link_of(
        links, count - 1, 0
    )
    total[0:FACE, :] += mm(from_below[2 * faces :, :], tap(2))


def hidden_kernel(
    links,
    partial,
    first_in,
    second_in,
    weights,
    hidden,
    first,
    second,
    total,
    up,
    down,
    from_below,
    from_above,
):
    total[...] = partial[...]
    route(links[3, 4], first_in, second_in, from_above, from_below)
    add_ghosts(total, from_below, from_above, links, weights)
    total[...] = jnp.maximum(total[...], 0.0)
    hidden[...] = total[...].astype(BF16)
    pack_faces(total, links, up, down)
    route(links[3, 4], up, down, first, second)


def lift_kernel(
    links,
    slots,
    block_levels,
    columns,
    partial,
    first_in,
    second_in,
    weights,
    height,
    *refs,
):
    *outs, total, rows_in, sums, from_below, from_above = refs
    count = partial.shape[0] // CELLS
    faces = count * FACE
    ch = partial.shape[1]
    total[...] = partial[...]
    route(links[3, 4], first_in, second_in, from_above, from_below)
    add_ghosts(total, from_below, from_above, links, weights)
    for c in range(EDGE):
        line = total[pl.ds(c, faces, stride=EDGE), :]
        rows_in[:, c * ch : (c + 1) * ch] = jnp.maximum(line, 0.0).astype(BF16)
    sums[...] = jnp.zeros_like(sums)

    def one(j, carry):
        rows = rows_in[pl.ds(pl.multiple_of(j * FACE, FACE), FACE), :]
        sums[slots[0, j]] += mm(rows, height[block_levels[0, j]])
        return carry

    lax.fori_loop(0, count, one, 0)
    peers = len(outs)
    per_peer = sums.shape[0] // peers
    row_at = lax.broadcasted_iota(jnp.int32, (ID_ROWS, LANES), 0)
    for k, out in enumerate(outs):
        ids = jnp.zeros(row_at.shape, F32)
        for i in range(per_peer):
            slot = (links[3, 7] ^ k) * per_peer + i
            block = sums[slot].astype(BF16)
            for h, lanes in halves(block.shape[1]):
                at = (h * per_peer + i) * FACE
                out[at : at + FACE, :] = block[:, lanes]
            ids = jnp.where(row_at == i, columns[0, slot].astype(F32), ids)
        out[out.shape[0] - ID_ROWS :, :] = ids.astype(BF16)


def gather_kernel(links, *refs):
    *arrived, bev, first, second, own, total, top, bottom = refs
    ch = bev.shape[1]
    parts = ch // LANES
    per_peer = (arrived[0].shape[0] - ID_ROWS) // (parts * FACE)
    total[...] = jnp.zeros_like(total)
    for source in arrived:
        ids = source[source.shape[0] - ID_ROWS :, :].astype(F32)
        for k in range(per_peer):
            column = jnp.max(ids[k : k + 1, :]).astype(jnp.int32)
            row_base = (column // TILE_BC) * (EDGE * COLS) + (column % TILE_BC) * EDGE
            for h in range(parts):
                start = (h * per_peer + k) * FACE
                block = source[start : start + FACE, :].astype(F32)
                for a in range(EDGE):
                    at = pl.multiple_of(row_base + a * COLS, EDGE)
                    total[h, pl.ds(at, EDGE), :] += block[a * EDGE : (a + 1) * EDGE, :]
    for h, lanes in halves(ch):
        bev[:, lanes] = total[h].astype(BF16)
        top[:, lanes] = total[h, 0 : HALO * COLS, :].astype(BF16)
        bottom[:, lanes] = total[h, (ROWS - HALO) * COLS :, :].astype(BF16)
        for x in range(HALO):
            far = COLS - HALO + x
            own[x, :, lanes] = total[h, pl.ds(x, ROWS, stride=COLS), :].astype(BF16)
            own[HALO + x, :, lanes] = total[h, pl.ds(far, ROWS, stride=COLS), :].astype(BF16)
    route(links[3, 6], bottom, top, first, second)


def halves(channels):
    return [(h, slice(h * LANES, (h + 1) * LANES)) for h in range(channels // LANES)]


WIDE_ROWS = ROWS + 2 * HALO
MID_ROWS = ROWS + HALO
RIM_ROWS = 72
INNER_ROWS = ROWS - 2
CORE_ROWS = ROWS - 4


def tap_columns(weights, dx):
    return jnp.concatenate([weights[dy * 3 + dx] for dy in range(3)], 0)


def three_rows(source, first_row, row_count):
    parts = []
    for dy in range(3):
        at = pl.multiple_of((first_row + dy) * COLS, COLS)
        parts.append(source[pl.ds(at, row_count * COLS), :])
    return jnp.concatenate(parts, 1)


def rows_conv(lhs, weights):
    count = lhs.shape[0]
    x = lax.rem(lax.broadcasted_iota(jnp.int32, (count, weights.shape[2]), 0), COLS)
    from_left = mm(lhs, tap_columns(weights, 0))
    total = jnp.where(x == 0, 0.0, pltpu.roll(from_left, 1, 0))
    total = total + mm(lhs, tap_columns(weights, 1))
    from_right = mm(lhs, tap_columns(weights, 2))
    return total + jnp.where(x == COLS - 1, 0.0, pltpu.roll(from_right, count - 1, 0))


def without_sides(block):
    x = lax.rem(lax.broadcasted_iota(jnp.int32, block.shape, 0), COLS)
    return jnp.where((x == 0) | (x == COLS - 1), 0.0, block)


def first_inner_kernel(bev, weights, inner):
    step = INNER_ROWS // 2

    def one(i, carry):
        block = jnp.maximum(rows_conv(three_rows(bev, i * step, step), weights), 0.0)
        at = pl.multiple_of(i * step * COLS, COLS)
        inner[pl.ds(at, step * COLS), :] = without_sides(block).astype(BF16)
        return carry

    lax.fori_loop(0, INNER_ROWS // step, one, 0)


def strips(upper, lower):
    parts = []
    for source in (upper, lower):
        rows = [source[dy * COLS : (dy + HALO) * COLS] for dy in range(3)]
        parts.append(jnp.concatenate(rows, 1))
    return jnp.concatenate(parts, 0)


def second_core_kernel(
    links,
    inner,
    bev,
    first_row,
    second_row,
    weights_first,
    weights_second,
    out,
    flanks,
    middle,
    above,
    below,
    sems,
):
    ch = bev.shape[1]
    two = HALO * COLS
    steps = 4
    step = CORE_ROWS // steps

    def send(row, count, k):
        rows = pl.ds(row, count)
        return pltpu.make_async_copy(middle.at[rows], out.at[rows], sems.at[k])

    def store(block, row):
        count = block.shape[0] // COLS
        lines = block.reshape(count, COLS, ch)
        middle[pl.ds(row, count), :, :] = lines.astype(BF16)
        for side, x in enumerate((0, COLS - EDGE)):
            flank = lines[:, x : x + EDGE, :].reshape(count * EDGE, ch)
            to = side * ROWS * EDGE + row * EDGE
            to = to if isinstance(row, int) else pl.multiple_of(to, EDGE)
            for h, lanes in halves(ch):
                flanks[h, pl.ds(to, count * EDGE), :] = flank[:, lanes]

    def one(i, carry):
        block = rows_conv(three_rows(inner, i * step, step), weights_second)
        at = pl.multiple_of((i * step + 2) * COLS, COLS)
        store(block + bev[pl.ds(at, step * COLS), :].astype(F32), i * step + 2)
        send(i * step + 2, step, i).start()
        return carry

    lax.fori_loop(0, steps, one, 0)

    route(links[3, 6], first_row, second_row, below, above)
    top, bottom = bev[0:two, :], bev[ROWS * COLS - two :, :]
    high = jnp.concatenate([above[...], top], 0)
    low = jnp.concatenate([bottom, below[...]], 0)
    strip = without_sides(jnp.maximum(rows_conv(strips(high, low), weights_first), 0.0))
    line = lax.broadcasted_iota(jnp.int32, strip.shape, 0) // COLS
    keep = jnp.where(line == 0, links[3, 0], jnp.where(line == 3, links[3, 1], 1)).astype(F32)
    strip = (strip * keep).astype(BF16)

    high = jnp.concatenate([strip[0:two], inner[0:two, :]], 0)
    low = jnp.concatenate([inner[INNER_ROWS * COLS - two :, :], strip[two:]], 0)
    strip = rows_conv(strips(high, low), weights_second)
    store(strip[0:two] + top.astype(F32), 0)
    store(strip[two:] + bottom.astype(F32), ROWS - HALO)
    send(0, HALO, steps).start()
    send(ROWS - HALO, HALO, steps + 1).start()
    for k in range(steps):
        send(k * step + 2, step, k).wait()
    send(0, HALO, steps).wait()
    send(ROWS - HALO, HALO, steps + 1).wait()


def edges_kernel(
    links,
    unused,
    flanks,
    own_left,
    own_right,
    first_in,
    second_in,
    weights_first,
    weights_second,
    out,
    sides,
    total,
    edge,
    sems,
):
    ch = out.shape[2]
    sides[:, WIDE_ROWS:, :] = jnp.zeros_like(sides[:, WIDE_ROWS:, :])

    def place(base, source):
        for x in range(HALO):
            sides[base + x, 0:WIDE_ROWS, :] = source[x, :, :].astype(F32)

    place(2, own_left)
    place(4, own_right)

    @pl.when(links[3, 5] == 0)
    def _():
        place(0, second_in)
        place(6, first_in)

    @pl.when(links[3, 5] != 0)
    def _():
        place(0, first_in)
        place(6, second_in)

    tall = sides.shape[1]
    total[...] = flanks[...]
    narrow = [sides[k, :, :].astype(BF16) for k in range(8)]
    lhs = [jnp.concatenate(narrow[start : start + 3], 1) for start in (0, 1, 4, 5)]
    lhs = jnp.concatenate(lhs, 0)
    taps = []
    for dy in range(3):
        rows = [weights_first[dy * 3 + dx] for dx in range(3)]
        taps.append(mm(lhs, jnp.concatenate(rows, 0)))
    row_at = lax.broadcasted_iota(jnp.int32, (RIM_ROWS, ch), 0)
    keep = jnp.where(row_at == MID_ROWS - 1, links[3, 1], 1)
    keep = jnp.where(row_at == 0, links[3, 0], keep).astype(F32)
    column = []
    for k, side_keep in enumerate((links[3, 2], None, None, links[3, 3])):
        at = k * tall
        block = sum(taps[dy][at + dy : at + dy + RIM_ROWS, :] for dy in range(3))
        block = jnp.maximum(block, 0.0) * keep
        if side_keep is not None:
            block = block * side_keep.astype(F32)
        zeros = jnp.zeros((tall - RIM_ROWS, ch), F32)
        column.append(jnp.concatenate([block, zeros], 0).astype(BF16))

    parts = []
    for dx, pair in enumerate(((0, 1), (1, 2), (2, 3))):
        lhs = jnp.concatenate([column[k] for k in pair], 0)
        taps = [mm(lhs, weights_second[dy * 3 + dx]) for dy in range(3)]
        for at in (0, tall):
            parts.append(sum(taps[dy][at + dy : at + dy + ROWS, :] for dy in range(3)))
    added = (
        (0, parts[0] + parts[2]),
        (1, parts[1]),
        (ROWS * EDGE + EDGE - 2, parts[4]),
        (ROWS * EDGE + EDGE - 1, parts[3] + parts[5]),
    )
    for at, block in added:
        for h, lanes in halves(ch):
            total[h, pl.ds(at, ROWS, stride=EDGE), :] += block[:, lanes]
    copies = []
    for side, x in enumerate((0, COLS - EDGE)):
        group = slice(side * ROWS * EDGE, (side + 1) * ROWS * EDGE)
        for h, lanes in halves(ch):
            edge[side, :, :, lanes] = total[h, group, :].reshape(ROWS, EDGE, LANES).astype(BF16)
        copies.append(
            pltpu.make_async_copy(edge.at[side], out.at[:, x : x + EDGE, :], sems.at[side])
        )
        copies[-1].start()
    for copy in copies:
        copy.wait()


def call(kernel, out_shape, scalars, arrays, scratch=(), mib=12):
    multiple = isinstance(out_shape, (list, tuple))
    return pl.pallas_call(
        kernel,
        out_shape=out_shape,
        in_specs=[SMEM] * len(scalars) + [VMEM] * len(arrays),
        out_specs=[VMEM] * len(out_shape) if multiple else VMEM,
        scratch_shapes=list(scratch),
        compiler_params=pltpu.CompilerParams(vmem_limit_bytes=mib << 20),
    )(*scalars, *arrays)


def local(
    features,
    links,
    block_slot,
    block_level,
    slot_column,
    conv_first,
    conv_second,
    height_w,
    plane_first,
    plane_second,
):
    count, _, ch = features.shape
    rows = count * CELLS
    faces = (2 * count + 1) * FACE
    mapped = plane_first.shape[3]
    peers = lax.axis_size("gx")
    slot_total = slot_column.shape[1]
    per_peer = slot_total // peers
    x = features.reshape(rows, ch)
    w_first = conv_first.reshape(-1, ch)
    w_second = conv_second.reshape(-1, ch)
    k_first = plane_first.reshape(9, mapped, mapped)
    k_second = plane_second.reshape(9, mapped, mapped)
    slots = block_slot.reshape(1, count)
    block_levels = block_level.reshape(1, count)
    both = ("gy", "gx")

    face_shape = jax.ShapeDtypeStruct((faces, ch), BF16)
    wide = pltpu.VMEM((rows, ch), F32)
    part_shape = jax.ShapeDtypeStruct((rows, ch), F32)

    gy, gx = lax.axis_index("gy"), lax.axis_index("gx")
    last_y = lax.axis_size("gy") - 1
    places = [gy > 0, gy < last_y, gx > 0, gx < peers - 1, lax.axis_index(both) % 2, gx % 2, gy % 2, gx]
    lane = lax.broadcasted_iota(jnp.int32, (1, count), 1)
    flags = sum(jnp.where(lane == k, jnp.int32(v), 0) for k, v in enumerate(places))
    links = jnp.concatenate([links.T, flags], 0)
    face = pltpu.VMEM((faces, ch), BF16)
    first, second = call(pack_kernel, (face_shape, face_shape), (links,), (x,), (wide, face, face))
    first, second = swap(first, second, both)
    partial = call(first_interior_kernel, part_shape, (links,), (x, w_first))
    hidden, first, second = call(
        hidden_kernel,
        (jax.ShapeDtypeStruct((rows, ch), BF16), face_shape, face_shape),
        (links,),
        (partial, first, second, w_first),
        (wide, face, face, face, face),
    )
    first, second = swap(first, second, both)
    partial = call(second_interior_kernel, part_shape, (links,), (hidden, x, w_second))
    payload = (mapped // LANES * per_peer * FACE + ID_ROWS, LANES)
    outgoing = call(
        lift_kernel,
        [jax.ShapeDtypeStruct(payload, BF16)] * peers,
        (links, slots, block_levels, slot_column),
        (partial, first, second, w_second, height_w),
        (
            wide,
            pltpu.VMEM((count * FACE, EDGE * ch), BF16),
            pltpu.VMEM((slot_total, FACE, mapped), F32),
            face,
            face,
        ),
    )
    arrived = list(outgoing)
    for k in trade_order(peers):
        arrived[k] = lax.ppermute(outgoing[k], "gx", [(i, i ^ k) for i in range(peers)])

    row_shape = jax.ShapeDtypeStruct((HALO * COLS, mapped), BF16)
    row = pltpu.VMEM((HALO * COLS, mapped), BF16)
    bev, first, second, own = call(
        gather_kernel,
        (
            jax.ShapeDtypeStruct((ROWS * COLS, mapped), BF16),
            row_shape,
            row_shape,
            jax.ShapeDtypeStruct((2 * HALO, ROWS, mapped), BF16),
        ),
        (links,),
        arrived,
        (pltpu.VMEM((mapped // LANES, ROWS * COLS, LANES), F32), row, row),
    )
    first_row, second_row = swap(first, second, "gy")
    inner = call(
        first_inner_kernel,
        jax.ShapeDtypeStruct((INNER_ROWS * COLS, mapped), BF16),
        (),
        (bev, k_first),
    )
    first_row, second_row, inner = lax.optimization_barrier((first_row, second_row, inner))
    odd_y, odd_x = gy % 2 == 1, gx % 2 == 1
    corner_above = jnp.where(odd_y, first_row, second_row).reshape(HALO, COLS, mapped)
    corner_below = jnp.where(odd_y, second_row, first_row).reshape(HALO, COLS, mapped)

    def side(own, at):
        return jnp.concatenate(
            [
                corner_above[:, at : at + HALO].transpose(1, 0, 2),
                own,
                corner_below[:, at : at + HALO].transpose(1, 0, 2),
            ],
            1,
        )

    own_left, own_right = side(own[:HALO], 0), side(own[HALO:], COLS - HALO)
    first, second = swap(
        jnp.where(odd_x, own_left, own_right), jnp.where(odd_x, own_right, own_left), "gx"
    )
    flank = (mapped // LANES, 2 * ROWS * EDGE, LANES)
    out_shape = jax.ShapeDtypeStruct((ROWS, COLS, mapped), BF16)
    limit = pltpu.CompilerParams(vmem_limit_bytes=12 << 20)
    out, flanks = pl.pallas_call(
        second_core_kernel,
        name="second_core",
        out_shape=(out_shape, jax.ShapeDtypeStruct(flank, F32)),
        in_specs=[SMEM] + [VMEM] * 6,
        out_specs=[ANY, VMEM],
        scratch_shapes=[
            pltpu.VMEM((ROWS, COLS, mapped), BF16),
            row,
            row,
            pltpu.SemaphoreType.DMA((6,)),
        ],
        compiler_params=limit,
    )(links, inner, bev, first_row, second_row, k_first, k_second)
    return pl.pallas_call(
        edges_kernel,
        name="edges",
        out_shape=out_shape,
        in_specs=[SMEM, ANY] + [VMEM] * 7,
        out_specs=ANY,
        scratch_shapes=[
            pltpu.VMEM((8, RIM_ROWS + EDGE, mapped), F32),
            pltpu.VMEM(flank, F32),
            pltpu.VMEM((2, ROWS, EDGE, mapped), BF16),
            pltpu.SemaphoreType.DMA((2,)),
        ],
        input_output_aliases={1: 0},
        compiler_params=limit,
    )(links, out, flanks, own_left, own_right, first, second, k_first, k_second)


def solution(mesh):
    in_specs = (
        P(("gy", "gx"), None, None),
        P(("gy", "gx"), None),
        P(("gy", "gx")),
        P(("gy", "gx")),
        P(("gy", "gx"), None),
        P(),
        P(),
        P(),
        P(),
        P(),
    )
    out_specs = P("gy", "gx", None)

    return jax.shard_map(local, mesh=mesh, in_specs=in_specs, out_specs=out_specs, check_vma=False)
```

```python
import jax
import jax.numpy as jnp
from jax import lax
from jax.experimental import pallas as pl
from jax.experimental.pallas import tpu as pltpu
from jax.sharding import PartitionSpec as P


EDGE = 8
FACE = EDGE * EDGE
CELLS = EDGE * FACE
TILE_BR = 8
TILE_BC = 4
ROWS = TILE_BR * EDGE
COLS = TILE_BC * EDGE
HALO = 2
ID_ROWS = 8
LANES = 128
F32 = jnp.float32
BF16 = jnp.bfloat16

VMEM = pl.BlockSpec(memory_space=pltpu.VMEM)
SMEM = pl.BlockSpec(memory_space=pltpu.SMEM)
ANY = pl.BlockSpec(memory_space=pl.ANY)


def swap(first, second, axis):
    count = lax.axis_size(axis)
    near = [(i, i ^ 1) for i in range(count) if i ^ 1 < count]
    far = [(i, i + 1 if i % 2 else i - 1) for i in range(1, count)]
    far = [(i, k) for i, k in far if k < count]
    first = lax.ppermute(first, axis, near)
    second = lax.ppermute(second, axis, far)
    return first, second


def trade_order(count):
    assert count & (count - 1) == 0
    far, near = range(count // 2, count), range(1, count // 2)
    return [k for half in (far, near) for odd in (1, 0) for k in half if k % 2 == odd]


def route(odd, up, down, first, second):
    @pl.when(odd == 0)
    def _():
        first[...] = up[...]
        second[...] = down[...]

    @pl.when(odd != 0)
    def _():
        first[...] = down[...]
        second[...] = up[...]


def mm(a, b):
    return jnp.dot(a, b, preferred_element_type=F32)


def link_of(links, block, axis):
    return links[axis, block].astype(F32)


def pack_faces(src, links, up, down):
    count = src.shape[0] // CELLS
    faces = count * FACE
    upper_b, lower_b = [], []
    for j in range(count):
        keep = link_of(links, j, 1)
        for a in range(EDGE):
            base = j * CELLS + a * FACE
            upper_b.append(src[base + FACE - EDGE : base + FACE, :] * keep)
            lower_b.append(src[base : base + EDGE, :])
    up[0:faces, :] = jnp.concatenate(upper_b, 0).astype(BF16)
    down[0:faces, :] = jnp.concatenate(lower_b, 0).astype(BF16)
    upper_c = []
    for j in range(count):
        upper_c.append(
            src[pl.ds(j * CELLS + EDGE - 1, FACE, stride=EDGE), :] * link_of(links, j, 2)
        )
    up[faces : 2 * faces, :] = jnp.concatenate(upper_c, 0).astype(BF16)
    down[faces : 2 * faces, :] = src[pl.ds(0, faces, stride=EDGE), :].astype(BF16)
    last = count * CELLS
    up[2 * faces :, :] = (src[last - FACE : last, :] * link_of(links, count - 1, 0)).astype(BF16)
    down[2 * faces :, :] = src[0:FACE, :].astype(BF16)


def pack_kernel(links, x, first, second, wide, up, down):
    wide[...] = x[...].astype(F32)
    pack_faces(wide, links, up, down)
    route(links[3, 4], up, down, first, second)


def interior(src, links, weights, out, residual):
    count = src.shape[0] // CELLS
    c_at = lax.broadcasted_iota(jnp.int32, (FACE, EDGE, 128), 1)

    def one(j, carry):
        base = pl.multiple_of(j * CELLS, CELLS)
        rows = src[pl.ds(base, CELLS), :]
        after = jnp.minimum(j + 1, count - 1)
        before = jnp.maximum(j - 1, 0)
        keep_after = jnp.where(j + 1 < count, links[0, j], 0).astype(F32)
        keep_before = jnp.where(j > 0, links[0, before], 0).astype(F32)
        over = src[pl.ds(pl.multiple_of(after * CELLS, CELLS), FACE), :]
        under = src[pl.ds(pl.multiple_of(before * CELLS + CELLS - FACE, FACE), FACE), :]
        over = (over.astype(F32) * keep_after).astype(BF16)
        under = (under.astype(F32) * keep_before).astype(BF16)
        wide = rows.astype(F32)
        planes = wide.reshape(EDGE, EDGE, EDGE, 128)
        none = jnp.zeros((EDGE, 1, EDGE, 128), F32)
        lines = wide.reshape(FACE, EDGE, 128)
        taps = [
            rows,
            jnp.concatenate([rows[FACE:], over], 0),
            jnp.concatenate([under, rows[:-FACE]], 0),
            jnp.concatenate([planes[:, 1:], none], 1).reshape(CELLS, 128).astype(BF16),
            jnp.concatenate([none, planes[:, :-1]], 1).reshape(CELLS, 128).astype(BF16),
            jnp.where(c_at == EDGE - 1, 0.0, pltpu.roll(lines, EDGE - 1, 1))
            .reshape(CELLS, 128)
            .astype(BF16),
            jnp.where(c_at == 0, 0.0, pltpu.roll(lines, 1, 1)).reshape(CELLS, 128).astype(BF16),
        ]
        total = mm(jnp.concatenate(taps, 1), weights[...])
        if residual is not None:
            total = total + residual[pl.ds(base, CELLS), :].astype(F32)
        out[pl.ds(base, CELLS), :] = total
        return carry

    lax.fori_loop(0, count, one, 0)


def first_interior_kernel(links, x, weights, out):
    interior(x, links, weights, out, None)


def second_interior_kernel(links, hidden, x, weights, out):
    interior(hidden, links, weights, out, x)


def ghost_places(count):
    faces = count * FACE
    return (0, faces, 2 * faces, 3 * faces, 4 * faces, 4 * faces + FACE)


def ghost_terms(ghosts, from_below, from_above, links, weights):
    ch = ghosts.shape[1]
    count = (from_below.shape[0] // FACE - 1) // 2
    faces = count * FACE
    b_plus, b_minus, c_plus, c_minus, a_plus, a_minus = ghost_places(count)

    def tap(k):
        return weights[k * ch : (k + 1) * ch, :]

    for start, to, axis, k in ((0, b_plus, 1, 3), (faces, c_plus, 2, 5)):
        product = mm(from_above[start : start + faces, :], tap(k))
        for j in range(count):
            rows = slice(j * FACE, (j + 1) * FACE)
            ghosts[to + j * FACE : to + (j + 1) * FACE, :] = product[rows, :] * link_of(
                links, j, axis
            )
    ghosts[b_minus : b_minus + faces, :] = mm(from_below[0:faces, :], tap(4))
    ghosts[c_minus : c_minus + faces, :] = mm(from_below[faces : 2 * faces, :], tap(6))
    product = mm(from_above[2 * faces :, :], tap(1))
    ghosts[a_plus : a_plus + FACE, :] = product * link_of(links, count - 1, 0)
    ghosts[a_minus : a_minus + FACE, :] = mm(from_below[2 * faces :, :], tap(2))


def hidden_kernel(
    links,
    partial,
    first_in,
    second_in,
    weights,
    hidden,
    first,
    second,
    total,
    up,
    down,
    from_below,
    from_above,
    ghosts,
):
    count = partial.shape[0] // CELLS
    ch = partial.shape[1]
    route(links[3, 4], first_in, second_in, from_above, from_below)
    ghost_terms(ghosts, from_below, from_above, links, weights)
    b_plus, b_minus, c_plus, c_minus, a_plus, a_minus = ghost_places(count)
    c_at = lax.broadcasted_iota(jnp.int32, (EDGE, ch), 0)
    for j in range(count):
        lines = []
        for a in range(EDGE):
            for b in range(EDGE):
                at = j * CELLS + a * FACE + b * EDGE
                line = partial[at : at + EDGE, :]
                face = j * FACE + a * EDGE
                if b == EDGE - 1:
                    line = line + ghosts[b_plus + face : b_plus + face + EDGE, :]
                if b == 0:
                    line = line + ghosts[b_minus + face : b_minus + face + EDGE, :]
                face = j * FACE + a * EDGE + b
                plus = ghosts[pl.ds(c_plus + face, EDGE, stride=0), :]
                minus = ghosts[pl.ds(c_minus + face, EDGE, stride=0), :]
                line = line + jnp.where(
                    c_at == EDGE - 1, plus, jnp.where(c_at == 0, minus, 0.0)
                )
                if j == count - 1 and a == EDGE - 1:
                    line = line + ghosts[a_plus + b * EDGE : a_plus + (b + 1) * EDGE, :]
                if j == 0 and a == 0:
                    line = line + ghosts[a_minus + b * EDGE : a_minus + (b + 1) * EDGE, :]
                lines.append(jnp.maximum(line, 0.0))
        block = jnp.concatenate(lines, 0)
        total[j * CELLS : (j + 1) * CELLS, :] = block
        hidden[j * CELLS : (j + 1) * CELLS, :] = block.astype(BF16)
    pack_faces(total, links, up, down)
    route(links[3, 4], up, down, first, second)


def lift_kernel(
    links,
    slots,
    block_levels,
    columns,
    partial,
    first_in,
    second_in,
    weights,
    height,
    *refs,
):
    *outs, ghosts, rows_in, sums, from_below, from_above = refs
    count = partial.shape[0] // CELLS
    ch = partial.shape[1]
    route(links[3, 4], first_in, second_in, from_above, from_below)
    ghost_terms(ghosts, from_below, from_above, links, weights)
    b_plus, b_minus, c_plus, c_minus, a_plus, a_minus = ghost_places(count)
    b_at = lax.rem(lax.broadcasted_iota(jnp.int32, (FACE, ch), 0), EDGE)

    def spread(to, j, c):
        rows = [to + (j * EDGE + a) * EDGE + c for a in range(EDGE)]
        return jnp.concatenate([ghosts[pl.ds(r, EDGE, stride=0), :] for r in rows], 0)

    for j in range(count):
        own = slice(j * FACE, (j + 1) * FACE)
        for c in range(EDGE):
            line = partial[pl.ds(j * CELLS + c, FACE, stride=EDGE), :]
            sides = jnp.where(b_at == 0, spread(b_minus, j, c), 0.0)
            line = line + jnp.where(b_at == EDGE - 1, spread(b_plus, j, c), sides)
            if c == EDGE - 1:
                line = line + ghosts[c_plus + j * FACE : c_plus + (j + 1) * FACE, :]
            if c == 0:
                line = line + ghosts[c_minus + j * FACE : c_minus + (j + 1) * FACE, :]
            if j == 0:
                low = line[0:EDGE] + ghosts[pl.ds(a_minus + c, EDGE, stride=EDGE), :]
                line = jnp.concatenate([low, line[EDGE:]], 0)
            if j == count - 1:
                high = line[FACE - EDGE :] + ghosts[pl.ds(a_plus + c, EDGE, stride=EDGE), :]
                line = jnp.concatenate([line[: FACE - EDGE], high], 0)
            rows_in[own, c * ch : (c + 1) * ch] = jnp.maximum(line, 0.0).astype(BF16)
    sums[...] = jnp.zeros_like(sums)

    def one(j, carry):
        rows = rows_in[pl.ds(pl.multiple_of(j * FACE, FACE), FACE), :]
        sums[slots[0, j]] += mm(rows, height[block_levels[0, j]])
        return carry

    lax.fori_loop(0, count, one, 0)
    peers = len(outs)
    per_peer = sums.shape[0] // peers
    row_at = lax.broadcasted_iota(jnp.int32, (ID_ROWS, LANES), 0)
    for k, out in enumerate(outs):
        ids = jnp.zeros(row_at.shape, F32)
        for i in range(per_peer):
            slot = (links[3, 7] ^ k) * per_peer + i
            block = sums[slot].astype(BF16)
            for h, lanes in halves(block.shape[1]):
                at = (h * per_peer + i) * FACE
                out[at : at + FACE, :] = block[:, lanes]
            ids = jnp.where(row_at == i, columns[0, slot].astype(F32), ids)
        out[out.shape[0] - ID_ROWS :, :] = ids.astype(BF16)


def gather_kernel(links, *refs):
    *arrived, bev, first, second, own, total, top, bottom = refs
    ch = bev.shape[1]
    parts = ch // LANES
    per_peer = (arrived[0].shape[0] - ID_ROWS) // (parts * FACE)
    total[...] = jnp.zeros_like(total)
    for source in arrived:
        ids = source[source.shape[0] - ID_ROWS :, :].astype(F32)
        for k in range(per_peer):
            column = jnp.max(ids[k : k + 1, :]).astype(jnp.int32)
            row_base = (column // TILE_BC) * (EDGE * COLS) + (column % TILE_BC) * EDGE
            for h in range(parts):
                start = (h * per_peer + k) * FACE
                block = source[start : start + FACE, :].astype(F32)
                for a in range(EDGE):
                    at = pl.multiple_of(row_base + a * COLS, EDGE)
                    total[h, pl.ds(at, EDGE), :] += block[a * EDGE : (a + 1) * EDGE, :]
    for h, lanes in halves(ch):
        bev[:, lanes] = total[h].astype(BF16)
        top[:, lanes] = total[h, 0 : HALO * COLS, :].astype(BF16)
        bottom[:, lanes] = total[h, (ROWS - HALO) * COLS :, :].astype(BF16)
        for x in range(HALO):
            far = COLS - HALO + x
            own[x, :, lanes] = total[h, pl.ds(x, ROWS, stride=COLS), :].astype(BF16)
            own[HALO + x, :, lanes] = total[h, pl.ds(far, ROWS, stride=COLS), :].astype(BF16)
    route(links[3, 6], bottom, top, first, second)


def halves(channels):
    return [(h, slice(h * LANES, (h + 1) * LANES)) for h in range(channels // LANES)]


WIDE_ROWS = ROWS + 2 * HALO
MID_ROWS = ROWS + HALO
RIM_ROWS = 72
INNER_ROWS = ROWS - 2
CORE_ROWS = ROWS - 4


def tap_columns(weights, dx):
    return jnp.concatenate([weights[dy * 3 + dx] for dy in range(3)], 0)


def three_rows(source, first_row, row_count):
    parts = []
    for dy in range(3):
        at = (first_row + dy) * COLS
        parts.append(source[at : at + row_count * COLS, :])
    return jnp.concatenate(parts, 1)


def clear(lines, side):
    at = lax.broadcasted_iota(jnp.int32, (1, EDGE, lines.shape[2]), 1)
    if side == 0:
        return jnp.concatenate([jnp.where(at == 0, 0.0, lines[:, :EDGE]), lines[:, EDGE:]], 1)
    inner = COLS - EDGE
    last = jnp.where(at == EDGE - 1, 0.0, lines[:, inner:])
    return jnp.concatenate([lines[:, :inner], last], 1)


def rows_conv(lhs, weights):
    count = lhs.shape[0]
    shape = (count // COLS, COLS, weights.shape[2])
    from_left = pltpu.roll(mm(lhs, tap_columns(weights, 0)), 1, 0)
    total = clear(from_left.reshape(shape), 0)
    total = total + mm(lhs, tap_columns(weights, 1)).reshape(shape)
    from_right = pltpu.roll(mm(lhs, tap_columns(weights, 2)), count - 1, 0)
    return total + clear(from_right.reshape(shape), 1)


def without_sides(lines):
    return clear(clear(lines, 0), 1)


def first_inner_kernel(bev, weights, inner):
    step = INNER_ROWS // 2
    for row in range(0, INNER_ROWS, step):
        block = jnp.maximum(rows_conv(three_rows(bev, row, step), weights), 0.0)
        block = without_sides(block).reshape(step * COLS, -1).astype(BF16)
        inner[row * COLS : (row + step) * COLS, :] = block


def strips(upper, lower):
    parts = []
    for source in (upper, lower):
        rows = [source[dy * COLS : (dy + HALO) * COLS] for dy in range(3)]
        parts.append(jnp.concatenate(rows, 1))
    return jnp.concatenate(parts, 0)


def second_core_kernel(
    links,
    inner,
    bev,
    first_row,
    second_row,
    weights_first,
    weights_second,
    out,
    flanks,
    ends,
    middle,
    above,
    below,
    sems,
):
    ch = bev.shape[1]
    two = HALO * COLS
    steps = 2
    step = CORE_ROWS // steps

    def store(lines, row, keep):
        count = lines.shape[0]
        keep[...] = lines.astype(BF16)
        for side, x in enumerate((0, COLS - EDGE)):
            flank = lines[:, x : x + EDGE, :].reshape(count * EDGE, ch)
            to = (side * ROWS + row) * EDGE
            for h, lanes in halves(ch):
                flanks[h, to : to + count * EDGE, :] = flank[:, lanes]

    copies = []
    for k in range(steps):
        row = k * step + HALO
        lines = rows_conv(three_rows(inner, k * step, step), weights_second)
        own = bev[row * COLS : (row + step) * COLS, :].astype(F32)
        kept = middle.at[k * step : (k + 1) * step]
        store(lines + own.reshape(lines.shape), row, kept)
        copies.append(pltpu.make_async_copy(kept, out.at[row : row + step], sems.at[k]))
        copies[-1].start()

    route(links[3, 6], first_row, second_row, below, above)
    top, bottom = bev[0:two, :], bev[ROWS * COLS - two :, :]
    high = jnp.concatenate([above[...], top], 0)
    low = jnp.concatenate([bottom, below[...]], 0)
    strip = without_sides(jnp.maximum(rows_conv(strips(high, low), weights_first), 0.0))
    line = lax.broadcasted_iota(jnp.int32, strip.shape, 0)
    keep = jnp.where(line == 0, links[3, 0], jnp.where(line == 3, links[3, 1], 1)).astype(F32)
    strip = (strip * keep).reshape(2 * two, ch).astype(BF16)

    high = jnp.concatenate([strip[0:two], inner[0:two, :]], 0)
    low = jnp.concatenate([inner[INNER_ROWS * COLS - two :, :], strip[two:]], 0)
    lines = rows_conv(strips(high, low), weights_second)
    own = jnp.concatenate([top, bottom], 0).astype(F32)
    lines = lines + own.reshape(lines.shape)
    store(lines[0:HALO], 0, ends.at[0:HALO])
    store(lines[HALO:], ROWS - HALO, ends.at[HALO:])
    for copy in copies:
        copy.wait()


def edges_kernel(
    links,
    unused,
    flanks,
    ends,
    own_left,
    own_right,
    first_in,
    second_in,
    weights_first,
    weights_second,
    out,
    sides,
    total,
    edge,
    sems,
):
    ch = out.shape[2]
    sides[:, WIDE_ROWS:, :] = jnp.zeros_like(sides[:, WIDE_ROWS:, :])

    def place(base, source):
        for x in range(HALO):
            sides[base + x, 0:WIDE_ROWS, :] = source[x, :, :].astype(F32)

    place(2, own_left)
    place(4, own_right)

    @pl.when(links[3, 5] == 0)
    def _():
        place(0, second_in)
        place(6, first_in)

    @pl.when(links[3, 5] != 0)
    def _():
        place(0, first_in)
        place(6, second_in)

    inner_columns = slice(EDGE, COLS - EDGE)
    copies = []
    for k, (row, source) in enumerate(((0, 0), (ROWS - HALO, HALO))):
        kept = ends.at[source : source + HALO, inner_columns, :]
        to = out.at[row : row + HALO, inner_columns, :]
        copies.append(pltpu.make_async_copy(kept, to, sems.at[k]))
        copies[-1].start()
    tall = sides.shape[1]
    total[...] = flanks[...]
    narrow = [sides[k, :, :].astype(BF16) for k in range(8)]
    lhs = [jnp.concatenate(narrow[start : start + 3], 1) for start in (0, 1, 4, 5)]
    lhs = jnp.concatenate(lhs, 0)
    taps = []
    for dy in range(3):
        rows = [weights_first[dy * 3 + dx] for dx in range(3)]
        taps.append(mm(lhs, jnp.concatenate(rows, 0)))
    row_at = lax.broadcasted_iota(jnp.int32, (RIM_ROWS, ch), 0)
    keep = jnp.where(row_at == MID_ROWS - 1, links[3, 1], 1)
    keep = jnp.where(row_at == 0, links[3, 0], keep).astype(F32)
    column = []
    for k, side_keep in enumerate((links[3, 2], None, None, links[3, 3])):
        at = k * tall
        block = sum(taps[dy][at + dy : at + dy + RIM_ROWS, :] for dy in range(3))
        block = jnp.maximum(block, 0.0) * keep
        if side_keep is not None:
            block = block * side_keep.astype(F32)
        zeros = jnp.zeros((tall - RIM_ROWS, ch), F32)
        column.append(jnp.concatenate([block, zeros], 0).astype(BF16))

    parts = []
    for dx, pair in enumerate(((0, 1), (1, 2), (2, 3))):
        lhs = jnp.concatenate([column[k] for k in pair], 0)
        taps = [mm(lhs, weights_second[dy * 3 + dx]) for dy in range(3)]
        for at in (0, tall):
            parts.append(sum(taps[dy][at + dy : at + dy + ROWS, :] for dy in range(3)))
    added = (
        (0, parts[0] + parts[2]),
        (1, parts[1]),
        (ROWS * EDGE + EDGE - 2, parts[4]),
        (ROWS * EDGE + EDGE - 1, parts[3] + parts[5]),
    )
    for at, block in added:
        for h, lanes in halves(ch):
            total[h, pl.ds(at, ROWS, stride=EDGE), :] += block[:, lanes]
    for side, x in enumerate((0, COLS - EDGE)):
        group = slice(side * ROWS * EDGE, (side + 1) * ROWS * EDGE)
        for h, lanes in halves(ch):
            edge[side, :, :, lanes] = total[h, group, :].reshape(ROWS, EDGE, LANES).astype(BF16)
        copies.append(
            pltpu.make_async_copy(edge.at[side], out.at[:, x : x + EDGE, :], sems.at[2 + side])
        )
        copies[-1].start()
    for copy in copies:
        copy.wait()


def call(kernel, out_shape, scalars, arrays, scratch=(), mib=12):
    multiple = isinstance(out_shape, (list, tuple))
    return pl.pallas_call(
        kernel,
        out_shape=out_shape,
        in_specs=[SMEM] * len(scalars) + [VMEM] * len(arrays),
        out_specs=[VMEM] * len(out_shape) if multiple else VMEM,
        scratch_shapes=list(scratch),
        compiler_params=pltpu.CompilerParams(vmem_limit_bytes=mib << 20),
    )(*scalars, *arrays)


def local(
    features,
    links,
    block_slot,
    block_level,
    slot_column,
    conv_first,
    conv_second,
    height_w,
    plane_first,
    plane_second,
):
    count, _, ch = features.shape
    rows = count * CELLS
    faces = (2 * count + 1) * FACE
    mapped = plane_first.shape[3]
    peers = lax.axis_size("gx")
    slot_total = slot_column.shape[1]
    per_peer = slot_total // peers
    x = features.reshape(rows, ch)
    w_first = conv_first.reshape(-1, ch)
    w_second = conv_second.reshape(-1, ch)
    k_first = plane_first.reshape(9, mapped, mapped)
    k_second = plane_second.reshape(9, mapped, mapped)
    slots = block_slot.reshape(1, count)
    block_levels = block_level.reshape(1, count)
    both = ("gy", "gx")

    face_shape = jax.ShapeDtypeStruct((faces, ch), BF16)
    wide = pltpu.VMEM((rows, ch), F32)
    part_shape = jax.ShapeDtypeStruct((rows, ch), F32)

    gy, gx = lax.axis_index("gy"), lax.axis_index("gx")
    last_y = lax.axis_size("gy") - 1
    places = [gy > 0, gy < last_y, gx > 0, gx < peers - 1, lax.axis_index(both) % 2, gx % 2, gy % 2, gx]
    lane = lax.broadcasted_iota(jnp.int32, (1, count), 1)
    flags = sum(jnp.where(lane == k, jnp.int32(v), 0) for k, v in enumerate(places))
    links = jnp.concatenate([links.T, flags], 0)
    face = pltpu.VMEM((faces, ch), BF16)
    ghosts = pltpu.VMEM((2 * faces, ch), F32)
    first, second = call(pack_kernel, (face_shape, face_shape), (links,), (x,), (wide, face, face))
    first, second = swap(first, second, both)
    partial = call(first_interior_kernel, part_shape, (links,), (x, w_first))
    hidden, first, second = call(
        hidden_kernel,
        (jax.ShapeDtypeStruct((rows, ch), BF16), face_shape, face_shape),
        (links,),
        (partial, first, second, w_first),
        (wide, face, face, face, face, ghosts),
    )
    first, second = swap(first, second, both)
    partial = call(second_interior_kernel, part_shape, (links,), (hidden, x, w_second))
    payload = (mapped // LANES * per_peer * FACE + ID_ROWS, LANES)
    outgoing = call(
        lift_kernel,
        [jax.ShapeDtypeStruct(payload, BF16)] * peers,
        (links, slots, block_levels, slot_column),
        (partial, first, second, w_second, height_w),
        (
            ghosts,
            pltpu.VMEM((count * FACE, EDGE * ch), BF16),
            pltpu.VMEM((slot_total, FACE, mapped), F32),
            face,
            face,
        ),
    )
    arrived = list(outgoing)
    for k in trade_order(peers):
        arrived[k] = lax.ppermute(outgoing[k], "gx", [(i, i ^ k) for i in range(peers)])

    row_shape = jax.ShapeDtypeStruct((HALO * COLS, mapped), BF16)
    row = pltpu.VMEM((HALO * COLS, mapped), BF16)
    bev, first, second, own = call(
        gather_kernel,
        (
            jax.ShapeDtypeStruct((ROWS * COLS, mapped), BF16),
            row_shape,
            row_shape,
            jax.ShapeDtypeStruct((2 * HALO, ROWS, mapped), BF16),
        ),
        (links,),
        arrived,
        (pltpu.VMEM((mapped // LANES, ROWS * COLS, LANES), F32), row, row),
    )
    first_row, second_row = swap(first, second, "gy")
    inner = call(
        first_inner_kernel,
        jax.ShapeDtypeStruct((INNER_ROWS * COLS, mapped), BF16),
        (),
        (bev, k_first),
    )
    first_row, second_row, inner = lax.optimization_barrier((first_row, second_row, inner))
    odd_y, odd_x = gy % 2 == 1, gx % 2 == 1
    corner_above = jnp.where(odd_y, first_row, second_row).reshape(HALO, COLS, mapped)
    corner_below = jnp.where(odd_y, second_row, first_row).reshape(HALO, COLS, mapped)

    def side(own, at):
        return jnp.concatenate(
            [
                corner_above[:, at : at + HALO].transpose(1, 0, 2),
                own,
                corner_below[:, at : at + HALO].transpose(1, 0, 2),
            ],
            1,
        )

    own_left, own_right = side(own[:HALO], 0), side(own[HALO:], COLS - HALO)
    first, second = swap(
        jnp.where(odd_x, own_left, own_right), jnp.where(odd_x, own_right, own_left), "gx"
    )
    flank = (mapped // LANES, 2 * ROWS * EDGE, LANES)
    out_shape = jax.ShapeDtypeStruct((ROWS, COLS, mapped), BF16)
    limit = pltpu.CompilerParams(vmem_limit_bytes=12 << 20)
    out, flanks, ends = pl.pallas_call(
        second_core_kernel,
        name="second_core",
        out_shape=(
            out_shape,
            jax.ShapeDtypeStruct(flank, F32),
            jax.ShapeDtypeStruct((2 * HALO, COLS, mapped), BF16),
        ),
        in_specs=[SMEM] + [VMEM] * 6,
        out_specs=[ANY, VMEM, VMEM],
        scratch_shapes=[
            pltpu.VMEM((CORE_ROWS, COLS, mapped), BF16),
            row,
            row,
            pltpu.SemaphoreType.DMA((2,)),
        ],
        compiler_params=limit,
    )(links, inner, bev, first_row, second_row, k_first, k_second)
    return pl.pallas_call(
        edges_kernel,
        name="edges",
        out_shape=out_shape,
        in_specs=[SMEM, ANY] + [VMEM] * 8,
        out_specs=ANY,
        scratch_shapes=[
            pltpu.VMEM((8, RIM_ROWS + EDGE, mapped), F32),
            pltpu.VMEM(flank, F32),
            pltpu.VMEM((2, ROWS, EDGE, mapped), BF16),
            pltpu.SemaphoreType.DMA((4,)),
        ],
        input_output_aliases={1: 0},
        compiler_params=limit,
    )(links, out, flanks, ends, own_left, own_right, first, second, k_first, k_second)


def solution(mesh):
    in_specs = (
        P(("gy", "gx"), None, None),
        P(("gy", "gx"), None),
        P(("gy", "gx")),
        P(("gy", "gx")),
        P(("gy", "gx"), None),
        P(),
        P(),
        P(),
        P(),
        P(),
    )
    out_specs = P("gy", "gx", None)

    return jax.shard_map(local, mesh=mesh, in_specs=in_specs, out_specs=out_specs, check_vma=False)
```

```python
import jax
import jax.numpy as jnp
from jax import lax
from jax.experimental import pallas as pl
from jax.experimental.pallas import tpu as pltpu
from jax.sharding import PartitionSpec as P


EDGE = 8
FACE = EDGE * EDGE
CELLS = EDGE * FACE
TILE_BR = 8
TILE_BC = 4
ROWS = TILE_BR * EDGE
COLS = TILE_BC * EDGE
HALO = 2
ID_ROWS = 8
LANES = 128
F32 = jnp.float32
BF16 = jnp.bfloat16

VMEM = pl.BlockSpec(memory_space=pltpu.VMEM)
SMEM = pl.BlockSpec(memory_space=pltpu.SMEM)
ANY = pl.BlockSpec(memory_space=pl.ANY)


def swap(first, second, axis):
    count = lax.axis_size(axis)
    near = [(i, i ^ 1) for i in range(count) if i ^ 1 < count]
    far = [(i, i + 1 if i % 2 else i - 1) for i in range(1, count)]
    far = [(i, k) for i, k in far if k < count]
    first = lax.ppermute(first, axis, near)
    second = lax.ppermute(second, axis, far)
    return first, second


def trade_order(count):
    assert count & (count - 1) == 0
    far, near = range(count // 2, count), range(1, count // 2)
    return [k for half in (far, near) for odd in (1, 0) for k in half if k % 2 == odd]


def route(odd, up, down, first, second):
    @pl.when(odd == 0)
    def _():
        first[...] = up[...]
        second[...] = down[...]

    @pl.when(odd != 0)
    def _():
        first[...] = down[...]
        second[...] = up[...]


def mm(a, b):
    return jnp.dot(a, b, preferred_element_type=F32)


def link_of(links, block, axis):
    return links[axis, block].astype(F32)


def pack_faces(src, links, up, down):
    count = src.shape[0] // CELLS
    faces = count * FACE
    upper_b, lower_b = [], []
    for j in range(count):
        keep = link_of(links, j, 1)
        for a in range(EDGE):
            base = j * CELLS + a * FACE
            upper_b.append(src[base + FACE - EDGE : base + FACE, :] * keep)
            lower_b.append(src[base : base + EDGE, :])
    up[0:faces, :] = jnp.concatenate(upper_b, 0).astype(BF16)
    down[0:faces, :] = jnp.concatenate(lower_b, 0).astype(BF16)
    upper_c = []
    for j in range(count):
        upper_c.append(
            src[pl.ds(j * CELLS + EDGE - 1, FACE, stride=EDGE), :] * link_of(links, j, 2)
        )
    up[faces : 2 * faces, :] = jnp.concatenate(upper_c, 0).astype(BF16)
    down[faces : 2 * faces, :] = src[pl.ds(0, faces, stride=EDGE), :].astype(BF16)
    last = count * CELLS
    up[2 * faces :, :] = (src[last - FACE : last, :] * link_of(links, count - 1, 0)).astype(BF16)
    down[2 * faces :, :] = src[0:FACE, :].astype(BF16)


def pack_kernel(links, x, first, second, wide, up, down):
    wide[...] = x[...].astype(F32)
    pack_faces(wide, links, up, down)
    route(links[3, 4], up, down, first, second)


def interior(src, links, weights, out, residual):
    count = src.shape[0] // CELLS
    c_at = lax.broadcasted_iota(jnp.int32, (FACE, EDGE, 128), 1)

    def one(j, carry):
        base = pl.multiple_of(j * CELLS, CELLS)
        rows = src[pl.ds(base, CELLS), :]
        after = jnp.minimum(j + 1, count - 1)
        before = jnp.maximum(j - 1, 0)
        keep_after = jnp.where(j + 1 < count, links[0, j], 0).astype(F32)
        keep_before = jnp.where(j > 0, links[0, before], 0).astype(F32)
        over = src[pl.ds(pl.multiple_of(after * CELLS, CELLS), FACE), :]
        under = src[pl.ds(pl.multiple_of(before * CELLS + CELLS - FACE, FACE), FACE), :]
        over = (over.astype(F32) * keep_after).astype(BF16)
        under = (under.astype(F32) * keep_before).astype(BF16)
        wide = rows.astype(F32)
        planes = wide.reshape(EDGE, EDGE, EDGE, 128)
        none = jnp.zeros((EDGE, 1, EDGE, 128), F32)
        lines = wide.reshape(FACE, EDGE, 128)
        taps = [
            rows,
            jnp.concatenate([rows[FACE:], over], 0),
            jnp.concatenate([under, rows[:-FACE]], 0),
            jnp.concatenate([planes[:, 1:], none], 1).reshape(CELLS, 128).astype(BF16),
            jnp.concatenate([none, planes[:, :-1]], 1).reshape(CELLS, 128).astype(BF16),
            jnp.where(c_at == EDGE - 1, 0.0, pltpu.roll(lines, EDGE - 1, 1))
            .reshape(CELLS, 128)
            .astype(BF16),
            jnp.where(c_at == 0, 0.0, pltpu.roll(lines, 1, 1)).reshape(CELLS, 128).astype(BF16),
        ]
        total = mm(jnp.concatenate(taps, 1), weights[...])
        if residual is not None:
            total = total + residual[pl.ds(base, CELLS), :].astype(F32)
        out[pl.ds(base, CELLS), :] = total
        return carry

    lax.fori_loop(0, count, one, 0)


def first_interior_kernel(links, x, weights, out):
    interior(x, links, weights, out, None)


def second_interior_kernel(links, hidden, x, weights, out):
    interior(hidden, links, weights, out, x)


def ghost_places(count):
    faces = count * FACE
    return (0, faces, 2 * faces, 3 * faces, 4 * faces, 4 * faces + FACE)


def ghost_terms(ghosts, from_below, from_above, links, weights):
    ch = ghosts.shape[1]
    count = (from_below.shape[0] // FACE - 1) // 2
    faces = count * FACE
    b_plus, b_minus, c_plus, c_minus, a_plus, a_minus = ghost_places(count)

    def tap(k):
        return weights[k * ch : (k + 1) * ch, :]

    for start, to, axis, k in ((0, b_plus, 1, 3), (faces, c_plus, 2, 5)):
        product = mm(from_above[start : start + faces, :], tap(k))
        for j in range(count):
            rows = slice(j * FACE, (j + 1) * FACE)
            ghosts[to + j * FACE : to + (j + 1) * FACE, :] = product[rows, :] * link_of(
                links, j, axis
            )
    ghosts[b_minus : b_minus + faces, :] = mm(from_below[0:faces, :], tap(4))
    ghosts[c_minus : c_minus + faces, :] = mm(from_below[faces : 2 * faces, :], tap(6))
    product = mm(from_above[2 * faces :, :], tap(1))
    ghosts[a_plus : a_plus + FACE, :] = product * link_of(links, count - 1, 0)
    ghosts[a_minus : a_minus + FACE, :] = mm(from_below[2 * faces :, :], tap(2))


def hidden_kernel(
    links,
    partial,
    first_in,
    second_in,
    weights,
    hidden,
    first,
    second,
    total,
    up,
    down,
    from_below,
    from_above,
    ghosts,
):
    count = partial.shape[0] // CELLS
    ch = partial.shape[1]
    route(links[3, 4], first_in, second_in, from_above, from_below)
    ghost_terms(ghosts, from_below, from_above, links, weights)
    b_plus, b_minus, c_plus, c_minus, a_plus, a_minus = ghost_places(count)
    c_at = lax.broadcasted_iota(jnp.int32, (EDGE, ch), 0)
    for j in range(count):
        lines = []
        for a in range(EDGE):
            for b in range(EDGE):
                at = j * CELLS + a * FACE + b * EDGE
                line = partial[at : at + EDGE, :]
                face = j * FACE + a * EDGE
                if b == EDGE - 1:
                    line = line + ghosts[b_plus + face : b_plus + face + EDGE, :]
                if b == 0:
                    line = line + ghosts[b_minus + face : b_minus + face + EDGE, :]
                face = j * FACE + a * EDGE + b
                plus = ghosts[pl.ds(c_plus + face, EDGE, stride=0), :]
                minus = ghosts[pl.ds(c_minus + face, EDGE, stride=0), :]
                line = line + jnp.where(
                    c_at == EDGE - 1, plus, jnp.where(c_at == 0, minus, 0.0)
                )
                if j == count - 1 and a == EDGE - 1:
                    line = line + ghosts[a_plus + b * EDGE : a_plus + (b + 1) * EDGE, :]
                if j == 0 and a == 0:
                    line = line + ghosts[a_minus + b * EDGE : a_minus + (b + 1) * EDGE, :]
                lines.append(jnp.maximum(line, 0.0))
        block = jnp.concatenate(lines, 0)
        total[j * CELLS : (j + 1) * CELLS, :] = block
        hidden[j * CELLS : (j + 1) * CELLS, :] = block.astype(BF16)
    pack_faces(total, links, up, down)
    route(links[3, 4], up, down, first, second)


def lift_kernel(
    links,
    slots,
    block_levels,
    columns,
    partial,
    first_in,
    second_in,
    weights,
    height,
    *refs,
):
    *outs, ghosts, rows_in, sums, from_below, from_above = refs
    count = partial.shape[0] // CELLS
    ch = partial.shape[1]
    route(links[3, 4], first_in, second_in, from_above, from_below)
    ghost_terms(ghosts, from_below, from_above, links, weights)
    b_plus, b_minus, c_plus, c_minus, a_plus, a_minus = ghost_places(count)
    b_at = lax.rem(lax.broadcasted_iota(jnp.int32, (FACE, ch), 0), EDGE)

    def spread(to, j, c):
        rows = [to + (j * EDGE + a) * EDGE + c for a in range(EDGE)]
        return jnp.concatenate([ghosts[pl.ds(r, EDGE, stride=0), :] for r in rows], 0)

    for j in range(count):
        own = slice(j * FACE, (j + 1) * FACE)
        for c in range(EDGE):
            line = partial[pl.ds(j * CELLS + c, FACE, stride=EDGE), :]
            sides = jnp.where(b_at == 0, spread(b_minus, j, c), 0.0)
            line = line + jnp.where(b_at == EDGE - 1, spread(b_plus, j, c), sides)
            if c == EDGE - 1:
                line = line + ghosts[c_plus + j * FACE : c_plus + (j + 1) * FACE, :]
            if c == 0:
                line = line + ghosts[c_minus + j * FACE : c_minus + (j + 1) * FACE, :]
            if j == 0:
                low = line[0:EDGE] + ghosts[pl.ds(a_minus + c, EDGE, stride=EDGE), :]
                line = jnp.concatenate([low, line[EDGE:]], 0)
            if j == count - 1:
                high = line[FACE - EDGE :] + ghosts[pl.ds(a_plus + c, EDGE, stride=EDGE), :]
                line = jnp.concatenate([line[: FACE - EDGE], high], 0)
            rows_in[own, c * ch : (c + 1) * ch] = jnp.maximum(line, 0.0).astype(BF16)
    sums[...] = jnp.zeros_like(sums)

    def one(j, carry):
        rows = rows_in[pl.ds(pl.multiple_of(j * FACE, FACE), FACE), :]
        sums[slots[0, j]] += mm(rows, height[block_levels[0, j]])
        return carry

    lax.fori_loop(0, count, one, 0)
    peers = len(outs)
    per_peer = sums.shape[0] // peers
    row_at = lax.broadcasted_iota(jnp.int32, (ID_ROWS, LANES), 0)
    for k, out in enumerate(outs):
        ids = jnp.zeros(row_at.shape, F32)
        for i in range(per_peer):
            slot = (links[3, 7] ^ k) * per_peer + i
            block = sums[slot].astype(BF16)
            for h, lanes in halves(block.shape[1]):
                at = (h * per_peer + i) * FACE
                out[at : at + FACE, :] = block[:, lanes]
            ids = jnp.where(row_at == i, columns[0, slot].astype(F32), ids)
        out[out.shape[0] - ID_ROWS :, :] = ids.astype(BF16)


def gather_kernel(links, *refs):
    *arrived, bev, first, second, own, total, top, bottom = refs
    ch = bev.shape[1]
    parts = ch // LANES
    per_peer = (arrived[0].shape[0] - ID_ROWS) // (parts * FACE)
    total[...] = jnp.zeros_like(total)
    for source in arrived:
        ids = source[source.shape[0] - ID_ROWS :, :].astype(F32)
        for k in range(per_peer):
            column = jnp.max(ids[k : k + 1, :]).astype(jnp.int32)
            row_base = (column // TILE_BC) * (EDGE * COLS) + (column % TILE_BC) * EDGE
            for h in range(parts):
                start = (h * per_peer + k) * FACE
                block = source[start : start + FACE, :].astype(F32)
                for a in range(EDGE):
                    at = pl.multiple_of(row_base + a * COLS, EDGE)
                    total[h, pl.ds(at, EDGE), :] += block[a * EDGE : (a + 1) * EDGE, :]
    for h, lanes in halves(ch):
        bev[:, lanes] = total[h].astype(BF16)
        top[:, lanes] = total[h, 0 : HALO * COLS, :].astype(BF16)
        bottom[:, lanes] = total[h, (ROWS - HALO) * COLS :, :].astype(BF16)
        for x in range(HALO):
            far = COLS - HALO + x
            own[x, :, lanes] = total[h, pl.ds(x, ROWS, stride=COLS), :].astype(BF16)
            own[HALO + x, :, lanes] = total[h, pl.ds(far, ROWS, stride=COLS), :].astype(BF16)
    route(links[3, 6], bottom, top, first, second)


def halves(channels):
    return [(h, slice(h * LANES, (h + 1) * LANES)) for h in range(channels // LANES)]


WIDE_ROWS = ROWS + 2 * HALO
MID_ROWS = ROWS + HALO
RIM_ROWS = 72


def tap_columns(weights, dx):
    return jnp.concatenate([weights[dy * 3 + dx] for dy in range(3)], 0)


def three_rows(source, first_row, row_count):
    parts = []
    for dy in range(3):
        at = (first_row + dy) * COLS
        parts.append(source[at : at + row_count * COLS, :])
    return jnp.concatenate(parts, 1)


def clear(lines, side):
    at = lax.broadcasted_iota(jnp.int32, (1, EDGE, lines.shape[2]), 1)
    if side == 0:
        return jnp.concatenate([jnp.where(at == 0, 0.0, lines[:, :EDGE]), lines[:, EDGE:]], 1)
    inner = COLS - EDGE
    last = jnp.where(at == EDGE - 1, 0.0, lines[:, inner:])
    return jnp.concatenate([lines[:, :inner], last], 1)


def rows_conv(lhs, weights):
    count = lhs.shape[0]
    shape = (count // COLS, COLS, weights.shape[2])
    from_left = pltpu.roll(mm(lhs, tap_columns(weights, 0)), 1, 0)
    total = clear(from_left.reshape(shape), 0)
    total = total + mm(lhs, tap_columns(weights, 1)).reshape(shape)
    from_right = pltpu.roll(mm(lhs, tap_columns(weights, 2)), count - 1, 0)
    return total + clear(from_right.reshape(shape), 1)


def without_sides(lines):
    return clear(clear(lines, 0), 1)


EARLY_ROWS = 38
LATE_ROWS = ROWS - 2 - EARLY_ROWS


def first_early_kernel(bev, weights, early):
    block = jnp.maximum(rows_conv(three_rows(bev, 0, EARLY_ROWS), weights), 0.0)
    early[...] = without_sides(block).reshape(early.shape).astype(BF16)


def strips(upper, lower):
    parts = []
    for source in (upper, lower):
        rows = [source[dy * COLS : (dy + HALO) * COLS] for dy in range(3)]
        parts.append(jnp.concatenate(rows, 1))
    return jnp.concatenate(parts, 0)


def second_core_kernel(
    links,
    early,
    bev,
    first_row,
    second_row,
    weights_first,
    weights_second,
    out,
    flanks,
    tail,
    first,
    head,
    above,
    below,
    sem,
):
    ch = bev.shape[1]
    two = HALO * COLS
    route(links[3, 6], first_row, second_row, below, above)
    high = jnp.concatenate([above[...], bev[0:two, :]], 0)
    low = jnp.concatenate([bev[ROWS * COLS - two :, :], below[...]], 0)
    lhs = jnp.concatenate([strips(high, low), three_rows(bev, EARLY_ROWS, LATE_ROWS)], 0)
    lines = without_sides(jnp.maximum(rows_conv(lhs, weights_first), 0.0))
    ends = lines[0 : 2 * HALO]
    line = lax.broadcasted_iota(jnp.int32, ends.shape, 0)
    keep = jnp.where(line == 0, links[3, 0], jnp.where(line == 3, links[3, 1], 1)).astype(F32)
    ends = (ends * keep).reshape(2 * two, ch).astype(BF16)
    late = lines[2 * HALO :].reshape(LATE_ROWS * COLS, ch).astype(BF16)
    first[0:two, :] = ends[0:two]
    first[two : two + EARLY_ROWS * COLS, :] = early[...]
    first[two + EARLY_ROWS * COLS : ROWS * COLS, :] = late
    first[ROWS * COLS :, :] = ends[two:]

    step = ROWS // 2
    copy = pltpu.make_async_copy(head, out.at[0:step], sem)
    for row, keep in ((0, head), (step, tail)):
        lines = rows_conv(three_rows(first, row, step), weights_second)
        own = bev[row * COLS : (row + step) * COLS, :].astype(F32)
        lines = lines + own.reshape(lines.shape)
        keep[...] = lines.astype(BF16)
        for side, x in enumerate((0, COLS - EDGE)):
            flank = lines[:, x : x + EDGE, :].reshape(step * EDGE, ch)
            to = (side * ROWS + row) * EDGE
            for h, lanes in halves(ch):
                flanks[h, to : to + step * EDGE, :] = flank[:, lanes]
        if row == 0:
            copy.start()
    copy.wait()


def edges_kernel(
    links,
    unused,
    flanks,
    tail,
    own_left,
    own_right,
    first_in,
    second_in,
    weights_first,
    weights_second,
    out,
    sides,
    total,
    edge,
    sems,
):
    ch = out.shape[2]
    sides[:, WIDE_ROWS:, :] = jnp.zeros_like(sides[:, WIDE_ROWS:, :])

    def place(base, source):
        for x in range(HALO):
            sides[base + x, 0:WIDE_ROWS, :] = source[x, :, :].astype(F32)

    place(2, own_left)
    place(4, own_right)

    @pl.when(links[3, 5] == 0)
    def _():
        place(0, second_in)
        place(6, first_in)

    @pl.when(links[3, 5] != 0)
    def _():
        place(0, first_in)
        place(6, second_in)

    inner_columns = slice(EDGE, COLS - EDGE)
    row = ROWS - tail.shape[0]
    kept = tail.at[:, inner_columns, :]
    copies = [pltpu.make_async_copy(kept, out.at[row:, inner_columns, :], sems.at[2])]
    copies[0].start()
    tall = sides.shape[1]
    total[...] = flanks[...]
    narrow = [sides[k, :, :].astype(BF16) for k in range(8)]
    lhs = [jnp.concatenate(narrow[start : start + 3], 1) for start in (0, 1, 4, 5)]
    lhs = jnp.concatenate(lhs, 0)
    taps = []
    for dy in range(3):
        rows = [weights_first[dy * 3 + dx] for dx in range(3)]
        taps.append(mm(lhs, jnp.concatenate(rows, 0)))
    row_at = lax.broadcasted_iota(jnp.int32, (RIM_ROWS, ch), 0)
    keep = jnp.where(row_at == MID_ROWS - 1, links[3, 1], 1)
    keep = jnp.where(row_at == 0, links[3, 0], keep).astype(F32)
    column = []
    for k, side_keep in enumerate((links[3, 2], None, None, links[3, 3])):
        at = k * tall
        block = sum(taps[dy][at + dy : at + dy + RIM_ROWS, :] for dy in range(3))
        block = jnp.maximum(block, 0.0) * keep
        if side_keep is not None:
            block = block * side_keep.astype(F32)
        zeros = jnp.zeros((tall - RIM_ROWS, ch), F32)
        column.append(jnp.concatenate([block, zeros], 0).astype(BF16))

    parts = []
    for dx, pair in enumerate(((0, 1), (1, 2), (2, 3))):
        lhs = jnp.concatenate([column[k] for k in pair], 0)
        taps = [mm(lhs, weights_second[dy * 3 + dx]) for dy in range(3)]
        for at in (0, tall):
            parts.append(sum(taps[dy][at + dy : at + dy + ROWS, :] for dy in range(3)))
    added = (
        (0, parts[0] + parts[2]),
        (1, parts[1]),
        (ROWS * EDGE + EDGE - 2, parts[4]),
        (ROWS * EDGE + EDGE - 1, parts[3] + parts[5]),
    )
    for at, block in added:
        for h, lanes in halves(ch):
            total[h, pl.ds(at, ROWS, stride=EDGE), :] += block[:, lanes]
    for side, x in enumerate((0, COLS - EDGE)):
        group = slice(side * ROWS * EDGE, (side + 1) * ROWS * EDGE)
        for h, lanes in halves(ch):
            edge[side, :, :, lanes] = total[h, group, :].reshape(ROWS, EDGE, LANES).astype(BF16)
        copies.append(
            pltpu.make_async_copy(edge.at[side], out.at[:, x : x + EDGE, :], sems.at[side])
        )
        copies[-1].start()
    for copy in copies:
        copy.wait()


def call(kernel, out_shape, scalars, arrays, scratch=(), mib=12):
    multiple = isinstance(out_shape, (list, tuple))
    return pl.pallas_call(
        kernel,
        out_shape=out_shape,
        in_specs=[SMEM] * len(scalars) + [VMEM] * len(arrays),
        out_specs=[VMEM] * len(out_shape) if multiple else VMEM,
        scratch_shapes=list(scratch),
        compiler_params=pltpu.CompilerParams(vmem_limit_bytes=mib << 20),
    )(*scalars, *arrays)


def local(
    features,
    links,
    block_slot,
    block_level,
    slot_column,
    conv_first,
    conv_second,
    height_w,
    plane_first,
    plane_second,
):
    count, _, ch = features.shape
    rows = count * CELLS
    faces = (2 * count + 1) * FACE
    mapped = plane_first.shape[3]
    peers = lax.axis_size("gx")
    slot_total = slot_column.shape[1]
    per_peer = slot_total // peers
    x = features.reshape(rows, ch)
    w_first = conv_first.reshape(-1, ch)
    w_second = conv_second.reshape(-1, ch)
    k_first = plane_first.reshape(9, mapped, mapped)
    k_second = plane_second.reshape(9, mapped, mapped)
    slots = block_slot.reshape(1, count)
    block_levels = block_level.reshape(1, count)
    both = ("gy", "gx")

    face_shape = jax.ShapeDtypeStruct((faces, ch), BF16)
    wide = pltpu.VMEM((rows, ch), F32)
    part_shape = jax.ShapeDtypeStruct((rows, ch), F32)

    gy, gx = lax.axis_index("gy"), lax.axis_index("gx")
    last_y = lax.axis_size("gy") - 1
    places = [gy > 0, gy < last_y, gx > 0, gx < peers - 1, lax.axis_index(both) % 2, gx % 2, gy % 2, gx]
    lane = lax.broadcasted_iota(jnp.int32, (1, count), 1)
    flags = sum(jnp.where(lane == k, jnp.int32(v), 0) for k, v in enumerate(places))
    links = jnp.concatenate([links.T, flags], 0)
    face = pltpu.VMEM((faces, ch), BF16)
    ghosts = pltpu.VMEM((2 * faces, ch), F32)
    first, second = call(pack_kernel, (face_shape, face_shape), (links,), (x,), (wide, face, face))
    first, second = swap(first, second, both)
    partial = call(first_interior_kernel, part_shape, (links,), (x, w_first))
    hidden, first, second = call(
        hidden_kernel,
        (jax.ShapeDtypeStruct((rows, ch), BF16), face_shape, face_shape),
        (links,),
        (partial, first, second, w_first),
        (wide, face, face, face, face, ghosts),
    )
    first, second = swap(first, second, both)
    partial = call(second_interior_kernel, part_shape, (links,), (hidden, x, w_second))
    payload = (mapped // LANES * per_peer * FACE + ID_ROWS, LANES)
    outgoing = call(
        lift_kernel,
        [jax.ShapeDtypeStruct(payload, BF16)] * peers,
        (links, slots, block_levels, slot_column),
        (partial, first, second, w_second, height_w),
        (
            ghosts,
            pltpu.VMEM((count * FACE, EDGE * ch), BF16),
            pltpu.VMEM((slot_total, FACE, mapped), F32),
            face,
            face,
        ),
    )
    arrived = list(outgoing)
    for k in trade_order(peers):
        arrived[k] = lax.ppermute(outgoing[k], "gx", [(i, i ^ k) for i in range(peers)])

    row_shape = jax.ShapeDtypeStruct((HALO * COLS, mapped), BF16)
    row = pltpu.VMEM((HALO * COLS, mapped), BF16)
    bev, first, second, own = call(
        gather_kernel,
        (
            jax.ShapeDtypeStruct((ROWS * COLS, mapped), BF16),
            row_shape,
            row_shape,
            jax.ShapeDtypeStruct((2 * HALO, ROWS, mapped), BF16),
        ),
        (links,),
        arrived,
        (pltpu.VMEM((mapped // LANES, ROWS * COLS, LANES), F32), row, row),
    )
    first_row, second_row = swap(first, second, "gy")
    early = call(
        first_early_kernel,
        jax.ShapeDtypeStruct((EARLY_ROWS * COLS, mapped), BF16),
        (),
        (bev, k_first),
    )
    first_row, second_row, early = lax.optimization_barrier((first_row, second_row, early))
    odd_y, odd_x = gy % 2 == 1, gx % 2 == 1
    corner_above = jnp.where(odd_y, first_row, second_row).reshape(HALO, COLS, mapped)
    corner_below = jnp.where(odd_y, second_row, first_row).reshape(HALO, COLS, mapped)

    def side(own, at):
        return jnp.concatenate(
            [
                corner_above[:, at : at + HALO].transpose(1, 0, 2),
                own,
                corner_below[:, at : at + HALO].transpose(1, 0, 2),
            ],
            1,
        )

    own_left, own_right = side(own[:HALO], 0), side(own[HALO:], COLS - HALO)
    first, second = swap(
        jnp.where(odd_x, own_left, own_right), jnp.where(odd_x, own_right, own_left), "gx"
    )
    flank = (mapped // LANES, 2 * ROWS * EDGE, LANES)
    out_shape = jax.ShapeDtypeStruct((ROWS, COLS, mapped), BF16)
    limit = pltpu.CompilerParams(vmem_limit_bytes=12 << 20)
    half = (ROWS // 2, COLS, mapped)
    out, flanks, tail = pl.pallas_call(
        second_core_kernel,
        name="second_core",
        out_shape=(
            out_shape,
            jax.ShapeDtypeStruct(flank, F32),
            jax.ShapeDtypeStruct(half, BF16),
        ),
        in_specs=[SMEM] + [VMEM] * 6,
        out_specs=[ANY, VMEM, VMEM],
        scratch_shapes=[
            pltpu.VMEM((MID_ROWS * COLS, mapped), BF16),
            pltpu.VMEM(half, BF16),
            row,
            row,
            pltpu.SemaphoreType.DMA,
        ],
        compiler_params=limit,
    )(links, early, bev, first_row, second_row, k_first, k_second)
    return pl.pallas_call(
        edges_kernel,
        name="edges",
        out_shape=out_shape,
        in_specs=[SMEM, ANY] + [VMEM] * 8,
        out_specs=ANY,
        scratch_shapes=[
            pltpu.VMEM((8, RIM_ROWS + EDGE, mapped), F32),
            pltpu.VMEM(flank, F32),
            pltpu.VMEM((2, ROWS, EDGE, mapped), BF16),
            pltpu.SemaphoreType.DMA((3,)),
        ],
        input_output_aliases={1: 0},
        compiler_params=limit,
    )(links, out, flanks, tail, own_left, own_right, first, second, k_first, k_second)


def solution(mesh):
    in_specs = (
        P(("gy", "gx"), None, None),
        P(("gy", "gx"), None),
        P(("gy", "gx")),
        P(("gy", "gx")),
        P(("gy", "gx"), None),
        P(),
        P(),
        P(),
        P(),
        P(),
    )
    out_specs = P("gy", "gx", None)

    return jax.shard_map(local, mesh=mesh, in_specs=in_specs, out_specs=out_specs, check_vma=False)
```

```python
import jax
import jax.numpy as jnp
from jax import lax
from jax.experimental import pallas as pl
from jax.experimental.pallas import tpu as pltpu
from jax.sharding import PartitionSpec as P


EDGE = 8
FACE = EDGE * EDGE
CELLS = EDGE * FACE
TILE_BR = 8
TILE_BC = 4
ROWS = TILE_BR * EDGE
COLS = TILE_BC * EDGE
HALO = 2
ID_ROWS = 8
LANES = 128
F32 = jnp.float32
BF16 = jnp.bfloat16

VMEM = pl.BlockSpec(memory_space=pltpu.VMEM)
SMEM = pl.BlockSpec(memory_space=pltpu.SMEM)
ANY = pl.BlockSpec(memory_space=pl.ANY)


def swap(first, second, axis):
    count = lax.axis_size(axis)
    near = [(i, i ^ 1) for i in range(count) if i ^ 1 < count]
    far = [(i, i + 1 if i % 2 else i - 1) for i in range(1, count)]
    far = [(i, k) for i, k in far if k < count]
    first = lax.ppermute(first, axis, near)
    second = lax.ppermute(second, axis, far)
    return first, second


def trade_order(count):
    assert count & (count - 1) == 0
    far, near = range(count // 2, count), range(1, count // 2)
    return [k for half in (far, near) for odd in (1, 0) for k in half if k % 2 == odd]


def route(odd, up, down, first, second):
    @pl.when(odd == 0)
    def _():
        first[...] = up[...]
        second[...] = down[...]

    @pl.when(odd != 0)
    def _():
        first[...] = down[...]
        second[...] = up[...]


def mm(a, b):
    return jnp.dot(a, b, preferred_element_type=F32)


def link_of(links, block, axis):
    return links[axis, block].astype(F32)


def pack_faces(src, links, up, down):
    count = src.shape[0] // CELLS
    faces = count * FACE
    upper_b, lower_b = [], []
    for j in range(count):
        keep = link_of(links, j, 1)
        for a in range(EDGE):
            base = j * CELLS + a * FACE
            upper_b.append(src[base + FACE - EDGE : base + FACE, :] * keep)
            lower_b.append(src[base : base + EDGE, :])
    up[0:faces, :] = jnp.concatenate(upper_b, 0).astype(BF16)
    down[0:faces, :] = jnp.concatenate(lower_b, 0).astype(BF16)
    upper_c = []
    for j in range(count):
        upper_c.append(
            src[pl.ds(j * CELLS + EDGE - 1, FACE, stride=EDGE), :] * link_of(links, j, 2)
        )
    up[faces : 2 * faces, :] = jnp.concatenate(upper_c, 0).astype(BF16)
    down[faces : 2 * faces, :] = src[pl.ds(0, faces, stride=EDGE), :].astype(BF16)
    last = count * CELLS
    up[2 * faces :, :] = (src[last - FACE : last, :] * link_of(links, count - 1, 0)).astype(BF16)
    down[2 * faces :, :] = src[0:FACE, :].astype(BF16)


def pack_kernel(links, x, first, second, wide, up, down):
    wide[...] = x[...].astype(F32)
    pack_faces(wide, links, up, down)
    route(links[3, 4], up, down, first, second)


def interior(src, links, weights, out, residual):
    count = src.shape[0] // CELLS
    c_at = lax.broadcasted_iota(jnp.int32, (FACE, EDGE, 128), 1)

    def one(j, carry):
        base = pl.multiple_of(j * CELLS, CELLS)
        rows = src[pl.ds(base, CELLS), :]
        after = jnp.minimum(j + 1, count - 1)
        before = jnp.maximum(j - 1, 0)
        keep_after = jnp.where(j + 1 < count, links[0, j], 0).astype(F32)
        keep_before = jnp.where(j > 0, links[0, before], 0).astype(F32)
        over = src[pl.ds(pl.multiple_of(after * CELLS, CELLS), FACE), :]
        under = src[pl.ds(pl.multiple_of(before * CELLS + CELLS - FACE, FACE), FACE), :]
        over = (over.astype(F32) * keep_after).astype(BF16)
        under = (under.astype(F32) * keep_before).astype(BF16)
        wide = rows.astype(F32)
        planes = wide.reshape(EDGE, EDGE, EDGE, 128)
        none = jnp.zeros((EDGE, 1, EDGE, 128), F32)
        lines = wide.reshape(FACE, EDGE, 128)
        taps = [
            rows,
            jnp.concatenate([rows[FACE:], over], 0),
            jnp.concatenate([under, rows[:-FACE]], 0),
            jnp.concatenate([planes[:, 1:], none], 1).reshape(CELLS, 128).astype(BF16),
            jnp.concatenate([none, planes[:, :-1]], 1).reshape(CELLS, 128).astype(BF16),
            jnp.where(c_at == EDGE - 1, 0.0, pltpu.roll(lines, EDGE - 1, 1))
            .reshape(CELLS, 128)
            .astype(BF16),
            jnp.where(c_at == 0, 0.0, pltpu.roll(lines, 1, 1)).reshape(CELLS, 128).astype(BF16),
        ]
        total = mm(jnp.concatenate(taps, 1), weights[...])
        if residual is not None:
            total = total + residual[pl.ds(base, CELLS), :].astype(F32)
        out[pl.ds(base, CELLS), :] = total
        return carry

    lax.fori_loop(0, count, one, 0)


def first_interior_kernel(links, x, weights, out):
    interior(x, links, weights, out, None)


def second_interior_kernel(links, hidden, x, weights, out):
    interior(hidden, links, weights, out, x)


def ghost_places(count):
    faces = count * FACE
    return (0, faces, 2 * faces, 3 * faces, 4 * faces, 4 * faces + FACE)


def ghost_terms(ghosts, from_below, from_above, links, weights):
    ch = ghosts.shape[1]
    count = (from_below.shape[0] // FACE - 1) // 2
    faces = count * FACE
    b_plus, b_minus, c_plus, c_minus, a_plus, a_minus = ghost_places(count)

    def tap(k):
        return weights[k * ch : (k + 1) * ch, :]

    for start, to, axis, k in ((0, b_plus, 1, 3), (faces, c_plus, 2, 5)):
        product = mm(from_above[start : start + faces, :], tap(k))
        for j in range(count):
            rows = slice(j * FACE, (j + 1) * FACE)
            ghosts[to + j * FACE : to + (j + 1) * FACE, :] = product[rows, :] * link_of(
                links, j, axis
            )
    ghosts[b_minus : b_minus + faces, :] = mm(from_below[0:faces, :], tap(4))
    ghosts[c_minus : c_minus + faces, :] = mm(from_below[faces : 2 * faces, :], tap(6))
    product = mm(from_above[2 * faces :, :], tap(1))
    ghosts[a_plus : a_plus + FACE, :] = product * link_of(links, count - 1, 0)
    ghosts[a_minus : a_minus + FACE, :] = mm(from_below[2 * faces :, :], tap(2))


def hidden_kernel(
    links,
    partial,
    first_in,
    second_in,
    weights,
    hidden,
    first,
    second,
    total,
    up,
    down,
    from_below,
    from_above,
    ghosts,
):
    count = partial.shape[0] // CELLS
    ch = partial.shape[1]
    route(links[3, 4], first_in, second_in, from_above, from_below)
    ghost_terms(ghosts, from_below, from_above, links, weights)
    b_plus, b_minus, c_plus, c_minus, a_plus, a_minus = ghost_places(count)
    c_at = lax.broadcasted_iota(jnp.int32, (EDGE, ch), 0)
    for j in range(count):
        lines = []
        for a in range(EDGE):
            for b in range(EDGE):
                at = j * CELLS + a * FACE + b * EDGE
                line = partial[at : at + EDGE, :]
                face = j * FACE + a * EDGE
                if b == EDGE - 1:
                    line = line + ghosts[b_plus + face : b_plus + face + EDGE, :]
                if b == 0:
                    line = line + ghosts[b_minus + face : b_minus + face + EDGE, :]
                face = j * FACE + a * EDGE + b
                plus = ghosts[pl.ds(c_plus + face, EDGE, stride=0), :]
                minus = ghosts[pl.ds(c_minus + face, EDGE, stride=0), :]
                line = line + jnp.where(
                    c_at == EDGE - 1, plus, jnp.where(c_at == 0, minus, 0.0)
                )
                if j == count - 1 and a == EDGE - 1:
                    line = line + ghosts[a_plus + b * EDGE : a_plus + (b + 1) * EDGE, :]
                if j == 0 and a == 0:
                    line = line + ghosts[a_minus + b * EDGE : a_minus + (b + 1) * EDGE, :]
                lines.append(jnp.maximum(line, 0.0))
        block = jnp.concatenate(lines, 0)
        total[j * CELLS : (j + 1) * CELLS, :] = block
        hidden[j * CELLS : (j + 1) * CELLS, :] = block.astype(BF16)
    pack_faces(total, links, up, down)
    route(links[3, 4], up, down, first, second)


def lift_kernel(
    links,
    slots,
    block_levels,
    columns,
    partial,
    first_in,
    second_in,
    weights,
    height,
    *refs,
):
    *outs, ghosts, rows_in, sums, from_below, from_above = refs
    count = partial.shape[0] // CELLS
    ch = partial.shape[1]
    route(links[3, 4], first_in, second_in, from_above, from_below)
    ghost_terms(ghosts, from_below, from_above, links, weights)
    b_plus, b_minus, c_plus, c_minus, a_plus, a_minus = ghost_places(count)
    b_at = lax.rem(lax.broadcasted_iota(jnp.int32, (FACE, ch), 0), EDGE)

    def spread(to, j, c):
        rows = [to + (j * EDGE + a) * EDGE + c for a in range(EDGE)]
        return jnp.concatenate([ghosts[pl.ds(r, EDGE, stride=0), :] for r in rows], 0)

    for j in range(count):
        own = slice(j * FACE, (j + 1) * FACE)
        for c in range(EDGE):
            line = partial[pl.ds(j * CELLS + c, FACE, stride=EDGE), :]
            sides = jnp.where(b_at == 0, spread(b_minus, j, c), 0.0)
            line = line + jnp.where(b_at == EDGE - 1, spread(b_plus, j, c), sides)
            if c == EDGE - 1:
                line = line + ghosts[c_plus + j * FACE : c_plus + (j + 1) * FACE, :]
            if c == 0:
                line = line + ghosts[c_minus + j * FACE : c_minus + (j + 1) * FACE, :]
            if j == 0:
                low = line[0:EDGE] + ghosts[pl.ds(a_minus + c, EDGE, stride=EDGE), :]
                line = jnp.concatenate([low, line[EDGE:]], 0)
            if j == count - 1:
                high = line[FACE - EDGE :] + ghosts[pl.ds(a_plus + c, EDGE, stride=EDGE), :]
                line = jnp.concatenate([line[: FACE - EDGE], high], 0)
            rows_in[own, c * ch : (c + 1) * ch] = jnp.maximum(line, 0.0).astype(BF16)
    sums[...] = jnp.zeros_like(sums)

    for j in range(count):
        rows = rows_in[j * FACE : (j + 1) * FACE, :]
        sums[slots[0, j]] += mm(rows, height[block_levels[0, j]])
    peers = len(outs)
    per_peer = sums.shape[0] // peers
    row_at = lax.broadcasted_iota(jnp.int32, (ID_ROWS, LANES), 0)
    for k, out in enumerate(outs):
        ids = jnp.zeros(row_at.shape, F32)
        for i in range(per_peer):
            slot = (links[3, 7] ^ k) * per_peer + i
            block = sums[slot].astype(BF16)
            for h, lanes in halves(block.shape[1]):
                at = (h * per_peer + i) * FACE
                out[at : at + FACE, :] = block[:, lanes]
            ids = jnp.where(row_at == i, columns[0, slot].astype(F32), ids)
        out[out.shape[0] - ID_ROWS :, :] = ids.astype(BF16)


def gather_kernel(links, *refs):
    *arrived, bev, first, second, own, total, top, bottom = refs
    ch = bev.shape[1]
    parts = ch // LANES
    per_peer = (arrived[0].shape[0] - ID_ROWS) // (parts * FACE)
    total[...] = jnp.zeros_like(total)
    for source in arrived:
        ids = source[source.shape[0] - ID_ROWS :, :].astype(F32)
        for k in range(per_peer):
            column = jnp.max(ids[k : k + 1, :]).astype(jnp.int32)
            row_base = (column // TILE_BC) * (EDGE * COLS) + (column % TILE_BC) * EDGE
            for h in range(parts):
                start = (h * per_peer + k) * FACE
                block = source[start : start + FACE, :].astype(F32)
                for a in range(EDGE):
                    at = pl.multiple_of(row_base + a * COLS, EDGE)
                    total[h, pl.ds(at, EDGE), :] += block[a * EDGE : (a + 1) * EDGE, :]
    for h, lanes in halves(ch):
        bev[:, lanes] = total[h].astype(BF16)
        top[:, lanes] = total[h, 0 : HALO * COLS, :].astype(BF16)
        bottom[:, lanes] = total[h, (ROWS - HALO) * COLS :, :].astype(BF16)
        for x in range(HALO):
            far = COLS - HALO + x
            own[x, :, lanes] = total[h, pl.ds(x, ROWS, stride=COLS), :].astype(BF16)
            own[HALO + x, :, lanes] = total[h, pl.ds(far, ROWS, stride=COLS), :].astype(BF16)
    route(links[3, 6], bottom, top, first, second)


def halves(channels):
    return [(h, slice(h * LANES, (h + 1) * LANES)) for h in range(channels // LANES)]


WIDE_ROWS = ROWS + 2 * HALO
MID_ROWS = ROWS + HALO
RIM_ROWS = 72
INNER_ROWS = ROWS - 2
CORE_ROWS = ROWS - 4


def tap_columns(weights, dx):
    return jnp.concatenate([weights[dy * 3 + dx] for dy in range(3)], 0)


def three_rows(source, first_row, row_count):
    parts = []
    for dy in range(3):
        at = (first_row + dy) * COLS
        parts.append(source[at : at + row_count * COLS, :])
    return jnp.concatenate(parts, 1)


def clear(lines, side):
    at = lax.broadcasted_iota(jnp.int32, (1, EDGE, lines.shape[2]), 1)
    if side == 0:
        return jnp.concatenate([jnp.where(at == 0, 0.0, lines[:, :EDGE]), lines[:, EDGE:]], 1)
    inner = COLS - EDGE
    last = jnp.where(at == EDGE - 1, 0.0, lines[:, inner:])
    return jnp.concatenate([lines[:, :inner], last], 1)


def rows_conv(lhs, weights):
    count = lhs.shape[0]
    shape = (count // COLS, COLS, weights.shape[2])
    from_left = pltpu.roll(mm(lhs, tap_columns(weights, 0)), 1, 0)
    total = clear(from_left.reshape(shape), 0)
    total = total + mm(lhs, tap_columns(weights, 1)).reshape(shape)
    from_right = pltpu.roll(mm(lhs, tap_columns(weights, 2)), count - 1, 0)
    return total + clear(from_right.reshape(shape), 1)


def without_sides(lines):
    return clear(clear(lines, 0), 1)


def first_inner_kernel(bev, weights, inner):
    step = INNER_ROWS // 2
    for row in range(0, INNER_ROWS, step):
        block = jnp.maximum(rows_conv(three_rows(bev, row, step), weights), 0.0)
        block = without_sides(block).reshape(step * COLS, -1).astype(BF16)
        inner[row * COLS : (row + step) * COLS, :] = block


def strips(upper, lower):
    parts = []
    for source in (upper, lower):
        rows = [source[dy * COLS : (dy + HALO) * COLS] for dy in range(3)]
        parts.append(jnp.concatenate(rows, 1))
    return jnp.concatenate(parts, 0)


def second_core_kernel(
    links,
    inner,
    bev,
    first_row,
    second_row,
    weights_first,
    weights_second,
    out,
    flanks,
    ends,
    middle,
    above,
    below,
    sems,
):
    ch = bev.shape[1]
    two = HALO * COLS
    steps = 2
    step = CORE_ROWS // steps

    def store(lines, row, keep):
        count = lines.shape[0]
        keep[...] = lines.astype(BF16)
        for side, x in enumerate((0, COLS - EDGE)):
            flank = lines[:, x : x + EDGE, :].reshape(count * EDGE, ch)
            to = (side * ROWS + row) * EDGE
            for h, lanes in halves(ch):
                flanks[h, to : to + count * EDGE, :] = flank[:, lanes]

    copies = []
    for k in range(steps):
        row = k * step + HALO
        lines = rows_conv(three_rows(inner, k * step, step), weights_second)
        own = bev[row * COLS : (row + step) * COLS, :].astype(F32)
        kept = middle.at[k * step : (k + 1) * step]
        store(lines + own.reshape(lines.shape), row, kept)
        copies.append(pltpu.make_async_copy(kept, out.at[row : row + step], sems.at[k]))
        copies[-1].start()

    route(links[3, 6], first_row, second_row, below, above)
    top, bottom = bev[0:two, :], bev[ROWS * COLS - two :, :]
    high = jnp.concatenate([above[...], top], 0)
    low = jnp.concatenate([bottom, below[...]], 0)
    strip = without_sides(jnp.maximum(rows_conv(strips(high, low), weights_first), 0.0))
    line = lax.broadcasted_iota(jnp.int32, strip.shape, 0)
    keep = jnp.where(line == 0, links[3, 0], jnp.where(line == 3, links[3, 1], 1)).astype(F32)
    strip = (strip * keep).reshape(2 * two, ch).astype(BF16)

    high = jnp.concatenate([strip[0:two], inner[0:two, :]], 0)
    low = jnp.concatenate([inner[INNER_ROWS * COLS - two :, :], strip[two:]], 0)
    lines = rows_conv(strips(high, low), weights_second)
    own = jnp.concatenate([top, bottom], 0).astype(F32)
    lines = lines + own.reshape(lines.shape)
    store(lines[0:HALO], 0, ends.at[0:HALO])
    store(lines[HALO:], ROWS - HALO, ends.at[HALO:])
    for copy in copies:
        copy.wait()


def edges_kernel(
    links,
    unused,
    flanks,
    ends,
    own_left,
    own_right,
    first_in,
    second_in,
    weights_first,
    weights_second,
    out,
    sides,
    total,
    edge,
    sems,
):
    ch = out.shape[2]
    sides[:, WIDE_ROWS:, :] = jnp.zeros_like(sides[:, WIDE_ROWS:, :])

    def place(base, source):
        for x in range(HALO):
            sides[base + x, 0:WIDE_ROWS, :] = source[x, :, :].astype(F32)

    place(2, own_left)
    place(4, own_right)

    @pl.when(links[3, 5] == 0)
    def _():
        place(0, second_in)
        place(6, first_in)

    @pl.when(links[3, 5] != 0)
    def _():
        place(0, first_in)
        place(6, second_in)

    inner_columns = slice(EDGE, COLS - EDGE)
    copies = []
    for k, (row, source) in enumerate(((0, 0), (ROWS - HALO, HALO))):
        kept = ends.at[source : source + HALO, inner_columns, :]
        to = out.at[row : row + HALO, inner_columns, :]
        copies.append(pltpu.make_async_copy(kept, to, sems.at[k]))
        copies[-1].start()
    tall = sides.shape[1]
    total[...] = flanks[...]
    narrow = [sides[k, :, :].astype(BF16) for k in range(8)]
    lhs = [jnp.concatenate(narrow[start : start + 3], 1) for start in (0, 1, 4, 5)]
    lhs = jnp.concatenate(lhs, 0)
    taps = []
    for dy in range(3):
        rows = [weights_first[dy * 3 + dx] for dx in range(3)]
        taps.append(mm(lhs, jnp.concatenate(rows, 0)))
    row_at = lax.broadcasted_iota(jnp.int32, (RIM_ROWS, ch), 0)
    keep = jnp.where(row_at == MID_ROWS - 1, links[3, 1], 1)
    keep = jnp.where(row_at == 0, links[3, 0], keep).astype(F32)
    column = []
    for k, side_keep in enumerate((links[3, 2], None, None, links[3, 3])):
        at = k * tall
        block = sum(taps[dy][at + dy : at + dy + RIM_ROWS, :] for dy in range(3))
        block = jnp.maximum(block, 0.0) * keep
        if side_keep is not None:
            block = block * side_keep.astype(F32)
        zeros = jnp.zeros((tall - RIM_ROWS, ch), F32)
        column.append(jnp.concatenate([block, zeros], 0).astype(BF16))

    parts = []
    for dx, pair in enumerate(((0, 1), (1, 2), (2, 3))):
        lhs = jnp.concatenate([column[k] for k in pair], 0)
        taps = [mm(lhs, weights_second[dy * 3 + dx]) for dy in range(3)]
        for at in (0, tall):
            parts.append(sum(taps[dy][at + dy : at + dy + ROWS, :] for dy in range(3)))
    added = (
        (0, parts[0] + parts[2]),
        (1, parts[1]),
        (ROWS * EDGE + EDGE - 2, parts[4]),
        (ROWS * EDGE + EDGE - 1, parts[3] + parts[5]),
    )
    for at, block in added:
        for h, lanes in halves(ch):
            total[h, pl.ds(at, ROWS, stride=EDGE), :] += block[:, lanes]
    for side, x in enumerate((0, COLS - EDGE)):
        group = slice(side * ROWS * EDGE, (side + 1) * ROWS * EDGE)
        for h, lanes in halves(ch):
            edge[side, :, :, lanes] = total[h, group, :].reshape(ROWS, EDGE, LANES).astype(BF16)
        copies.append(
            pltpu.make_async_copy(edge.at[side], out.at[:, x : x + EDGE, :], sems.at[2 + side])
        )
        copies[-1].start()
    for copy in copies:
        copy.wait()


def call(kernel, out_shape, scalars, arrays, scratch=(), mib=12):
    multiple = isinstance(out_shape, (list, tuple))
    return pl.pallas_call(
        kernel,
        out_shape=out_shape,
        in_specs=[SMEM] * len(scalars) + [VMEM] * len(arrays),
        out_specs=[VMEM] * len(out_shape) if multiple else VMEM,
        scratch_shapes=list(scratch),
        compiler_params=pltpu.CompilerParams(vmem_limit_bytes=mib << 20),
    )(*scalars, *arrays)


def local(
    features,
    links,
    block_slot,
    block_level,
    slot_column,
    conv_first,
    conv_second,
    height_w,
    plane_first,
    plane_second,
):
    count, _, ch = features.shape
    rows = count * CELLS
    faces = (2 * count + 1) * FACE
    mapped = plane_first.shape[3]
    peers = lax.axis_size("gx")
    slot_total = slot_column.shape[1]
    per_peer = slot_total // peers
    x = features.reshape(rows, ch)
    w_first = conv_first.reshape(-1, ch)
    w_second = conv_second.reshape(-1, ch)
    k_first = plane_first.reshape(9, mapped, mapped)
    k_second = plane_second.reshape(9, mapped, mapped)
    slots = block_slot.reshape(1, count)
    block_levels = block_level.reshape(1, count)
    both = ("gy", "gx")

    face_shape = jax.ShapeDtypeStruct((faces, ch), BF16)
    wide = pltpu.VMEM((rows, ch), F32)
    part_shape = jax.ShapeDtypeStruct((rows, ch), F32)

    gy, gx = lax.axis_index("gy"), lax.axis_index("gx")
    last_y = lax.axis_size("gy") - 1
    places = [gy > 0, gy < last_y, gx > 0, gx < peers - 1, lax.axis_index(both) % 2, gx % 2, gy % 2, gx]
    lane = lax.broadcasted_iota(jnp.int32, (1, count), 1)
    flags = sum(jnp.where(lane == k, jnp.int32(v), 0) for k, v in enumerate(places))
    links = jnp.concatenate([links.T, flags], 0)
    face = pltpu.VMEM((faces, ch), BF16)
    ghosts = pltpu.VMEM((2 * faces, ch), F32)
    first, second = call(pack_kernel, (face_shape, face_shape), (links,), (x,), (wide, face, face))
    first, second = swap(first, second, both)
    partial = call(first_interior_kernel, part_shape, (links,), (x, w_first))
    hidden, first, second = call(
        hidden_kernel,
        (jax.ShapeDtypeStruct((rows, ch), BF16), face_shape, face_shape),
        (links,),
        (partial, first, second, w_first),
        (wide, face, face, face, face, ghosts),
    )
    first, second = swap(first, second, both)
    partial = call(second_interior_kernel, part_shape, (links,), (hidden, x, w_second))
    payload = (mapped // LANES * per_peer * FACE + ID_ROWS, LANES)
    outgoing = call(
        lift_kernel,
        [jax.ShapeDtypeStruct(payload, BF16)] * peers,
        (links, slots, block_levels, slot_column),
        (partial, first, second, w_second, height_w),
        (
            ghosts,
            pltpu.VMEM((count * FACE, EDGE * ch), BF16),
            pltpu.VMEM((slot_total, FACE, mapped), F32),
            face,
            face,
        ),
    )
    arrived = list(outgoing)
    for k in trade_order(peers):
        arrived[k] = lax.ppermute(outgoing[k], "gx", [(i, i ^ k) for i in range(peers)])

    row_shape = jax.ShapeDtypeStruct((HALO * COLS, mapped), BF16)
    row = pltpu.VMEM((HALO * COLS, mapped), BF16)
    bev, first, second, own = call(
        gather_kernel,
        (
            jax.ShapeDtypeStruct((ROWS * COLS, mapped), BF16),
            row_shape,
            row_shape,
            jax.ShapeDtypeStruct((2 * HALO, ROWS, mapped), BF16),
        ),
        (links,),
        arrived,
        (pltpu.VMEM((mapped // LANES, ROWS * COLS, LANES), F32), row, row),
    )
    first_row, second_row = swap(first, second, "gy")
    inner = call(
        first_inner_kernel,
        jax.ShapeDtypeStruct((INNER_ROWS * COLS, mapped), BF16),
        (),
        (bev, k_first),
    )
    first_row, second_row, inner = lax.optimization_barrier((first_row, second_row, inner))
    odd_y, odd_x = gy % 2 == 1, gx % 2 == 1
    corner_above = jnp.where(odd_y, first_row, second_row).reshape(HALO, COLS, mapped)
    corner_below = jnp.where(odd_y, second_row, first_row).reshape(HALO, COLS, mapped)

    def side(own, at):
        return jnp.concatenate(
            [
                corner_above[:, at : at + HALO].transpose(1, 0, 2),
                own,
                corner_below[:, at : at + HALO].transpose(1, 0, 2),
            ],
            1,
        )

    own_left, own_right = side(own[:HALO], 0), side(own[HALO:], COLS - HALO)
    first, second = swap(
        jnp.where(odd_x, own_left, own_right), jnp.where(odd_x, own_right, own_left), "gx"
    )
    flank = (mapped // LANES, 2 * ROWS * EDGE, LANES)
    out_shape = jax.ShapeDtypeStruct((ROWS, COLS, mapped), BF16)
    limit = pltpu.CompilerParams(vmem_limit_bytes=12 << 20)
    out, flanks, ends = pl.pallas_call(
        second_core_kernel,
        name="second_core",
        out_shape=(
            out_shape,
            jax.ShapeDtypeStruct(flank, F32),
            jax.ShapeDtypeStruct((2 * HALO, COLS, mapped), BF16),
        ),
        in_specs=[SMEM] + [VMEM] * 6,
        out_specs=[ANY, VMEM, VMEM],
        scratch_shapes=[
            pltpu.VMEM((CORE_ROWS, COLS, mapped), BF16),
            row,
            row,
            pltpu.SemaphoreType.DMA((2,)),
        ],
        compiler_params=limit,
    )(links, inner, bev, first_row, second_row, k_first, k_second)
    return pl.pallas_call(
        edges_kernel,
        name="edges",
        out_shape=out_shape,
        in_specs=[SMEM, ANY] + [VMEM] * 8,
        out_specs=ANY,
        scratch_shapes=[
            pltpu.VMEM((8, RIM_ROWS + EDGE, mapped), F32),
            pltpu.VMEM(flank, F32),
            pltpu.VMEM((2, ROWS, EDGE, mapped), BF16),
            pltpu.SemaphoreType.DMA((4,)),
        ],
        input_output_aliases={1: 0},
        compiler_params=limit,
    )(links, out, flanks, ends, own_left, own_right, first, second, k_first, k_second)


def solution(mesh):
    in_specs = (
        P(("gy", "gx"), None, None),
        P(("gy", "gx"), None),
        P(("gy", "gx")),
        P(("gy", "gx")),
        P(("gy", "gx"), None),
        P(),
        P(),
        P(),
        P(),
        P(),
    )
    out_specs = P("gy", "gx", None)

    return jax.shard_map(local, mesh=mesh, in_specs=in_specs, out_specs=out_specs, check_vma=False)
```
